512 devices in a mesh: dp: 16 (over y, core), lat: 32 (over z, x).
Axes of the slice: x: 4, y: 8, z: 8, core: 2. Of those that a mesh axis runs over, the one named last changes fastest.
Arguments:
- fields: bfloat16 [16, 96, 180, 768], P('dp', 'lat'), may hold values from -6 to 6
- cotangent: bfloat16 [16, 96, 180, 768], P('dp', 'lat'), may hold values from -6 to 6
- w_first: bfloat16 [2, 8, 96, 96], replicated, may hold values from -0.4375 to 0.4375
- b_first: float32 [2, 768], replicated, may hold values from -3 to 3
- w_second: bfloat16 [2, 8, 96, 96], replicated, may hold values from -0.4375 to 0.4375
- b_second: float32 [2, 768], replicated, may hold values from -3 to 3
Outputs:
- output: bfloat16 [16, 96, 180, 768], P('dp', 'lat')
- grad_fields: bfloat16 [16, 96, 180, 768], P('dp', 'lat')
- grad_w_first: float32 [2, 8, 96, 96], replicated
- grad_b_first: float32 [2, 768], replicated
- grad_w_second: float32 [2, 8, 96, 96], replicated
- grad_b_second: float32 [2, 768], replicated
The draws below stay inside these ranges and needn't reach their ends.
All inputs are finite; a program needn't handle non-finite values.
Results may differ from the reference program's by a relative error of at most 0.015.
Values may be sent and summed in bfloat16 or wider, within the bound.
No kernel may reach another device: no remote copies, remote signals or barrier semaphores. Data moves between devices by JAX's collectives and lax.ppermute only.
A program may use at most 64 MiB of HBM per device.

```python
import math
from functools import partial
import jax
import jax.numpy as jnp
from jax import lax

C = 768
NB = 8
BS = 96
H = 96
W = 180
KX = 64
SAMPLES = 16


def level_of(stream_key, dims, split, low, high):
    gain, own = 1.0, jax.random.fold_in(stream_key, 6)
    for dim, shards_of in split:
        draws = jnp.exp(jax.random.uniform(jax.random.fold_in(own, dim), (shards_of,), jnp.float32, low / len(split), high / len(split)))
        gain = gain * jnp.repeat(draws, dims[dim] // shards_of).reshape([-1 if axis == dim else 1 for axis in range(len(dims))])
    return gain


def normal_values(stream_key, shape, deviation, bound, split=(), kind=jnp.bfloat16):
    drawn = deviation * jax.random.normal(stream_key, shape, jnp.float32)
    if split:
        drawn = drawn * level_of(stream_key, shape, split, -0.22, 0.18)
    return jnp.clip(drawn, -bound, bound).astype(kind)


def setup_inputs(seed: int = 0) -> dict:
    key_list = jax.random.split(jax.random.key(seed), 7)
    return {
        "fields": normal_values(key_list[0], (SAMPLES, H, W, C), 1.0, 6.0, ((0, 16), (1, 32))),
        "cotangent": normal_values(key_list[1], (SAMPLES, H, W, C), 1.0, 6.0, ((0, 16), (1, 32))),
        "w_first": normal_values(key_list[2], (2, NB, BS, BS), (2 * BS) ** -0.5, 0.4375),
        "b_first": normal_values(key_list[3], (2, C), 0.5, 3.0, (), jnp.float32),
        "w_second": normal_values(key_list[4], (2, NB, BS, BS), (2 * BS) ** -0.5, 0.4375),
        "b_second": normal_values(key_list[5], (2, C), 0.5, 3.0, (), jnp.float32),
    }


EPSILON = 1e-06

def layer_norm(values):
    centered = values - lax.optimization_barrier(jnp.mean(values, axis=-1, keepdims=True))
    spread = lax.optimization_barrier(jnp.mean(centered * centered, axis=-1, keepdims=True))
    return centered / jnp.sqrt(spread + EPSILON)

def angles(count_left, count_right, period):
    left_index = jnp.arange(count_left, dtype=jnp.int32)[:, None]
    right_index = jnp.arange(count_right, dtype=jnp.int32)[None, :]
    return 2.0 * math.pi / period * (left_index * right_index % period).astype(jnp.float32)

def longitude_tables(mode_count):
    angle_grid = angles(W, mode_count, W)
    mode_index = jnp.arange(mode_count, dtype=jnp.int32)[None, :]
    live_modes = jnp.where(mode_index <= W // 2, 1.0, 0.0).astype(jnp.float32) / math.sqrt(W)
    weight = jnp.where(mode_index == 0, 1.0, 2.0).astype(jnp.float32) * live_modes
    forward = jnp.stack([jnp.cos(angle_grid) * live_modes, -jnp.sin(angle_grid) * live_modes], axis=2)
    inverse = jnp.stack([jnp.cos(angle_grid) * weight, -jnp.sin(angle_grid) * weight], axis=2)
    return (forward.astype(jnp.bfloat16), inverse.astype(jnp.bfloat16))

def latitude_table():
    angle_grid = angles(H, H, H)
    cosine = jnp.cos(angle_grid) / math.sqrt(H)
    sine_part = jnp.sin(angle_grid) / math.sqrt(H)
    real_row = jnp.stack([cosine, sine_part], axis=2)
    imag_row = jnp.stack([-sine_part, cosine], axis=2)
    return jnp.stack([real_row, imag_row], axis=1).astype(jnp.bfloat16)

def real_form(weight):
    real_part = weight[0]
    imag_part = weight[1]
    upper_rows = jnp.stack([real_part, imag_part], axis=2)
    lower_rows = jnp.stack([-imag_part, real_part], axis=2)
    return jnp.stack([upper_rows, lower_rows], axis=1)

def fold_grads(gathered):
    real_grad = gathered[:, 0, :, 0, :] + gathered[:, 1, :, 1, :]
    imag_grad = gathered[:, 0, :, 1, :] - gathered[:, 1, :, 0, :]
    return jnp.stack([real_grad, imag_grad], axis=0)

def product(pattern, left_side, right_side):
    return jnp.einsum(pattern, left_side.astype(jnp.float32), right_side.astype(jnp.float32))

def spectral_forward(spectra_modes, first_form, bias_one, second_form, bias_two):
    leading = spectra_modes.shape[:3]
    blocked = spectra_modes.reshape(leading + (2, NB, BS))
    pre_one = product('bmkqni,nqipo->bmkpno', blocked, first_form).reshape(leading + (2, C)) + bias_one.astype(jnp.float32)
    hidden = jax.nn.gelu(pre_one, approximate=False).astype(jnp.bfloat16)
    pre_two = product('bmkqni,nqipo->bmkpno', hidden.reshape(leading + (2, NB, BS)), second_form).reshape(leading + (2, C)) + bias_two.astype(jnp.float32)
    return (pre_one, hidden, pre_two)

def spectral_backward(spectra_modes, pre_one, hidden, first_form, second_form, back_filtered):
    leading = spectra_modes.shape[:3]
    back_blocked = back_filtered.reshape(leading + (2, NB, BS))
    grad_second = product('bmkqni,bmkpno->nqipo', hidden.reshape(leading + (2, NB, BS)), back_blocked)
    bias_two_grad = lax.optimization_barrier(jnp.sum(back_filtered.astype(jnp.float32), axis=(0, 1, 2)))
    back_hidden = product('bmkpno,nqipo->bmkqni', back_blocked, second_form).reshape(leading + (2, C))
    unused, gelu_back = jax.vjp(partial(jax.nn.gelu, approximate=False), pre_one)
    back_pre = gelu_back(back_hidden)[0].astype(jnp.bfloat16)
    pre_blocked = back_pre.reshape(leading + (2, NB, BS))
    grad_first = product('bmkqni,bmkpno->nqipo', spectra_modes.reshape(leading + (2, NB, BS)), pre_blocked)
    bias_one_grad = lax.optimization_barrier(jnp.sum(back_pre.astype(jnp.float32), axis=(0, 1, 2)))
    back_modes = product('bmkpno,nqipo->bmkqni', pre_blocked, first_form).reshape(leading + (2, C)).astype(jnp.bfloat16)
    return (fold_grads(grad_first), bias_one_grad, fold_grads(grad_second), bias_two_grad, back_modes)

def reference(fields, cotangent, w_first, b_first, w_second, b_second):
    forward_lon, inverse_lon = longitude_tables(KX)
    latitude = latitude_table()
    first_form = real_form(w_first)
    second_form = real_form(w_second)

    def one_sample(sample_pair):
        sample, tangent = sample_pair
        values = sample[None].astype(jnp.float32)
        normed, norm_back = jax.vjp(layer_norm, values)
        spectra = product('bhwc,wkp->bhkpc', normed.astype(jnp.bfloat16), forward_lon).astype(jnp.bfloat16)
        spectra_modes = product('mqhp,bhkpc->bmkqc', latitude, spectra).astype(jnp.bfloat16)
        pre_one, hidden, pre_two = spectral_forward(spectra_modes, first_form, b_first, second_form, b_second)
        filtered = pre_two.astype(jnp.bfloat16)
        row_spectra = product('mphq,bmkpc->bhkqc', latitude, filtered).astype(jnp.bfloat16)
        mixed = product('bhkpc,wkp->bhwc', row_spectra, inverse_lon)
        result = (values + normed + mixed).astype(jnp.bfloat16)
        upstream = tangent[None].astype(jnp.float32)
        back_rows = product('bhwc,wkp->bhkpc', tangent[None], inverse_lon).astype(jnp.bfloat16)
        back_filtered = product('mphq,bhkqc->bmkpc', latitude, back_rows).astype(jnp.bfloat16)
        grad_one, bias_one, grad_two, bias_two, back_modes = spectral_backward(spectra_modes, pre_one, hidden, first_form, second_form, back_filtered)
        back_spectra = product('mqhp,bmkqc->bhkpc', latitude, back_modes).astype(jnp.bfloat16)
        back_normed = upstream + product('bhkpc,wkp->bhwc', back_spectra, forward_lon)
        back_fields = (upstream + norm_back(back_normed)[0]).astype(jnp.bfloat16)
        return (result[0], back_fields[0], grad_one, bias_one, grad_two, bias_two)
    result, back_fields, grad_one, bias_one, grad_two, bias_two = lax.map(one_sample, (fields, cotangent))
    grad_scale = 1.0 / (SAMPLES * H)
    return (result, back_fields, lax.optimization_barrier(jnp.sum(grad_one, axis=0)) * grad_scale, lax.optimization_barrier(jnp.sum(bias_one, axis=0)) * grad_scale, lax.optimization_barrier(jnp.sum(grad_two, axis=0)) * grad_scale, lax.optimization_barrier(jnp.sum(bias_two, axis=0)) * grad_scale)
```

```python
import math

import jax
import jax.numpy as jnp
import numpy as np
from jax import lax
from jax.experimental import pallas as pl
from jax.experimental.pallas import tpu as pltpu
from jax.sharding import PartitionSpec as P

C = 768
NB = 8
BS = 96
H = 96
W = 180
KX = 64
SAMPLES = 16
EPSILON = 1e-06

BANDS = 32
GROUPS = 4
MODES = KX // GROUPS
ROWS = H // BANDS
WPAD = 192
PACK = 72
CHUNKS = 16
CHUNK_ROWS = 24
BF = jnp.bfloat16
F32 = jnp.float32
VMEM_LIMIT = 48 * 1024 * 1024


def tables():
    w_index = np.arange(W)[:, None]
    k_index = np.arange(KX)[None, :]
    lon = (2.0 * math.pi / W * (w_index * k_index % W)).astype(np.float64)
    fwd = np.stack([np.cos(lon), -np.sin(lon)], axis=1) / math.sqrt(W)
    weight = np.where(k_index == 0, 1.0, 2.0)[:, None, :]
    inv = fwd * weight
    def order(table):
        grouped = table.reshape(W, 2, GROUPS, MODES).transpose(0, 2, 1, 3).reshape(W, 2 * KX)
        padded = np.zeros((WPAD, 2 * KX))
        padded[:W] = grouped
        return padded

    h_index = np.arange(H)
    lat = 2.0 * math.pi / H * (h_index[:, None] * h_index[None, :] % H)
    cosine = np.cos(lat) / math.sqrt(H)
    sine = np.sin(lat) / math.sqrt(H)
    full = np.stack(
        [np.stack([cosine, sine], axis=2), np.stack([-sine, cosine], axis=2)], axis=0
    ).reshape(2 * H, 2 * H)
    return order(fwd), order(inv), full


LON_FWD, LON_INV, LAT = tables()


def lanes(shape):
    return lax.broadcasted_iota(jnp.int32, shape, 1)


def roll(value, shift):
    return pltpu.roll(value, shift % 128, 1)


def pack_tile(tile):
    lane = lanes((24, 128))
    tail = tile[72:96]
    return [
        jnp.where(lane < 96, tile[24 * i : 24 * i + 24], roll(tail, 96 - 32 * i))
        for i in range(3)
    ]


def unpack_tail(pieces):
    lane = lanes((24, 128))
    return jnp.where(
        lane < 32,
        roll(pieces[0], 32),
        jnp.where(lane < 64, roll(pieces[1], 64), roll(pieces[2], 96)),
    )


def block_lanes(value, block):
    start = BS * block
    first, shift = start // 128, start % 128
    head = value[:, 128 * first : 128 * first + 128]
    if shift == 0:
        return head
    head = roll(head, 128 - shift)
    if shift + BS <= 128:
        return head
    after = roll(value[:, 128 * first + 128 : 128 * first + 256], 128 - shift)
    return jnp.where(lanes(head.shape) < 128 - shift, head, after)


def join_lanes(parts):
    lane = lanes(parts[0].shape)
    return [
        jnp.where(lane < 96, parts[0], roll(parts[1], 96)),
        jnp.where(lane < 64, roll(parts[1], 96), roll(parts[2], 64)),
        jnp.where(lane < 32, roll(parts[2], 64), roll(parts[3], 32)),
    ]


ROW_CHUNKS = [(start, min(32, W - start)) for start in range(0, W, 32)]


def normalize(values):
    mean = jnp.sum(values, axis=-1, keepdims=True) * (1.0 / C)
    centered = values - mean
    spread = jnp.sum(centered * centered, axis=-1, keepdims=True) * (1.0 / C)
    scale = 1.0 / jnp.sqrt(spread + EPSILON)
    return centered * scale, scale


def send_packed(acc_ref, out_ref):
    for block in range(NB):
        rows = [block_lanes(acc_ref[r], block) for r in range(ROWS)]
        for group in range(GROUPS):
            tile = jnp.concatenate(
                [row[32 * group : 32 * group + 32] for row in rows], axis=0
            )
            pieces = pack_tile(tile)
            out_ref[block * GROUPS + group] = jnp.concatenate(pieces, axis=0).astype(BF)


def fields_kernel(x_ref, table_ref, out_ref, normed_ref, acc_ref):
    r = pl.program_id(0)

    @pl.when(r == 0)
    def _():
        normed_ref[...] = jnp.zeros_like(normed_ref)

    for start, size in ROW_CHUNKS:
        values = x_ref[0, 0, start : start + size].astype(F32)
        normed_ref[start : start + size] = normalize(values)[0].astype(BF)
    acc_ref[r] = jnp.dot(table_ref[...], normed_ref[...], preferred_element_type=F32)

    @pl.when(r == ROWS - 1)
    def _():
        send_packed(acc_ref, out_ref)


def cotangent_kernel(x_ref, table_ref, out_ref, padded_ref, acc_ref):
    r = pl.program_id(0)

    @pl.when(r == 0)
    def _():
        padded_ref[...] = jnp.zeros_like(padded_ref)

    padded_ref[0:W] = x_ref[0, 0]
    acc_ref[r] = jnp.dot(table_ref[...], padded_ref[...], preferred_element_type=F32)

    @pl.when(r == ROWS - 1)
    def _():
        send_packed(acc_ref, out_ref)


def to_spectra(kernel, name, array, table):
    return pl.pallas_call(
        kernel,
        name=name,
        grid=(ROWS,),
        in_specs=[
            pl.BlockSpec((1, 1, W, C), lambda r: (0, r, 0, 0)),
            pl.BlockSpec((2 * KX, WPAD), lambda r: (0, 0)),
        ],
        out_specs=pl.BlockSpec((BANDS, PACK, 128), lambda r: (0, 0, 0)),
        out_shape=jax.ShapeDtypeStruct((BANDS, PACK, 128), BF),
        scratch_shapes=[
            pltpu.VMEM((WPAD, C), BF),
            pltpu.VMEM((ROWS, 2 * KX, C), F32),
        ],
        compiler_params=pltpu.CompilerParams(vmem_limit_bytes=VMEM_LIMIT),
        cost_estimate=pl.CostEstimate(
            flops=2 * ROWS * W * 2 * KX * C, bytes_accessed=1500000, transcendentals=0
        ),
    )(array, table)


TILE_ROWS = 2 * ROWS * MODES


def unpack_bands(recv_ref, rows_ref):
    def one(s, carry):
        pieces = [
            recv_ref[s, 24 * i : 24 * i + 24, :].astype(F32) for i in range(3)
        ]
        base = pl.multiple_of(s * TILE_ROWS, TILE_ROWS)
        for i in range(3):
            rows_ref[pl.ds(base + 24 * i, 24), :] = pieces[i]
        rows_ref[pl.ds(base + 72, 24), :] = unpack_tail(pieces)
        return carry

    lax.fori_loop(0, BANDS, one, 0, unroll=4)


def pack_bands(rows_ref, out_ref):
    def one(s, carry):
        base = pl.multiple_of(s * TILE_ROWS, TILE_ROWS)
        pieces = pack_tile(rows_ref[pl.ds(base, TILE_ROWS), :])
        out_ref[s] = jnp.concatenate(pieces, axis=0).astype(BF)
        return carry

    lax.fori_loop(0, BANDS, one, 0, unroll=4)


def mode_rows(rows_ref, lat, pair):
    columns = jnp.concatenate(
        [
            rows_ref[pl.ds(2 * pair + j, 2 * H, stride=MODES), :].astype(BF)
            for j in range(2)
        ],
        axis=1,
    )
    done = jnp.dot(lat, columns, preferred_element_type=F32).astype(BF)
    return jnp.concatenate(
        [
            jnp.concatenate(
                [done[0:H, 128 * j : 128 * j + 128], done[H : 2 * H, 128 * j : 128 * j + 128]],
                axis=1,
            )
            for j in range(2)
        ],
        axis=0,
    )


def store_rows(rows_ref, lat, pair, modes):
    columns = jnp.concatenate(
        [
            jnp.concatenate(
                [modes[H * j : H * j + H, 0:128], modes[H * j : H * j + H, 128:256]], axis=0
            )
            for j in range(2)
        ],
        axis=1,
    )
    done = lax.dot_general(
        lat, columns, (((0,), (0,)), ((), ())), preferred_element_type=F32
    )
    for j in range(2):
        rows_ref[pl.ds(2 * pair + j, 2 * H, stride=MODES), :] = done[:, 128 * j : 128 * j + 128]


PAIR_ROWS = 2 * H
PAIRS = MODES // 2


def forward_kernel(
    recv_ref, lat_ref, w1_ref, b1_ref, w2_ref, b2_ref,
    out_ref, modes_ref, hidden_ref, slope_ref, rows_ref,
):
    unpack_bands(recv_ref, rows_ref)
    lat = lat_ref[...]
    w1 = w1_ref[...]
    w2 = w2_ref[...]
    for pair in range(PAIRS):
        span = slice(PAIR_ROWS * pair, PAIR_ROWS * pair + PAIR_ROWS)
        modes = mode_rows(rows_ref, lat, pair)
        modes_ref[span] = modes
        pre = jnp.dot(modes, w1, preferred_element_type=F32) + b1_ref[...]
        cdf = 0.5 + 0.5 * lax.erf(pre * math.sqrt(0.5))
        hidden = (pre * cdf).astype(BF)
        slope_ref[span] = cdf + pre * (
            jnp.exp(-0.5 * pre * pre) * (1.0 / math.sqrt(2.0 * math.pi))
        )
        hidden_ref[span] = hidden
        filtered = (jnp.dot(hidden, w2, preferred_element_type=F32) + b2_ref[...]).astype(BF)
        store_rows(rows_ref, lat, pair, filtered)
    pack_bands(rows_ref, out_ref)


NT = (((1,), (1,)), ((), ()))
TN = (((0,), (0,)), ((), ()))


def backward_kernel(
    recv_ref, lat_ref, w1_ref, w2_ref, modes_ref, hidden_ref, slope_ref,
    out_ref, grad_ref, rows_ref, filtered_ref, pre_ref,
):
    unpack_bands(recv_ref, rows_ref)
    lat = lat_ref[...]
    w1 = w1_ref[...]
    w2 = w2_ref[...]
    for pair in range(PAIRS):
        span = slice(PAIR_ROWS * pair, PAIR_ROWS * pair + PAIR_ROWS)
        back_filtered = mode_rows(rows_ref, lat, pair)
        filtered_ref[span] = back_filtered
        back_hidden = lax.dot_general(back_filtered, w2, NT, preferred_element_type=F32)
        back_pre = (back_hidden * slope_ref[span]).astype(BF)
        pre_ref[span] = back_pre
        back_modes = lax.dot_general(back_pre, w1, NT, preferred_element_type=F32).astype(BF)
        store_rows(rows_ref, lat, pair, back_modes)
    ones = jnp.ones((8, MODES * H), BF)
    row = 0
    bias_rows = []
    for left_ref, right_ref in ((modes_ref, pre_ref), (hidden_ref, filtered_ref)):
        right = right_ref[...]
        gathered = lax.dot_general(left_ref[...], right, TN, preferred_element_type=F32)
        real = gathered[0:BS, 0:128] + gathered[128 : 128 + BS, 128:256]
        imag = gathered[0:BS, 128:256] - gathered[128 : 128 + BS, 0:128]
        for part in (real, imag):
            for piece in pack_tile(part):
                grad_ref[row : row + 24] = piece
                row += 24
        bias = jnp.dot(ones, right, preferred_element_type=F32)
        bias_rows += [bias[:, 0:128], bias[:, 128:256]]
    for value in bias_rows:
        grad_ref[row : row + 8] = value
        row += 8
    grad_ref[row:] = jnp.zeros((CHUNKS * CHUNK_ROWS - row, 128), F32)
    pack_bands(rows_ref, out_ref)


def receive(recv_ref, rows_ref):
    for group in range(GROUPS):
        for quad in range(2):
            tiles = []
            for block in range(4):
                band = (4 * quad + block) * GROUPS + group
                pieces = [
                    recv_ref[band, 24 * i : 24 * i + 24, :].astype(F32) for i in range(3)
                ]
                tiles.append(jnp.concatenate(pieces + [unpack_tail(pieces)], axis=0))
            for t, joined in enumerate(join_lanes(tiles)):
                for r in range(ROWS):
                    rows_ref[
                        r,
                        32 * group : 32 * group + 32,
                        384 * quad + 128 * t : 384 * quad + 128 * t + 128,
                    ] = joined[32 * r : 32 * r + 32].astype(BF)


def output_kernel(recv_ref, x_ref, table_ref, out_ref, rows_ref, mixed_ref):
    r = pl.program_id(0)

    @pl.when(r == 0)
    def _():
        receive(recv_ref, rows_ref)

    mixed_ref[...] = jnp.dot(table_ref[...], rows_ref[r], preferred_element_type=F32)
    for start, size in ROW_CHUNKS:
        values = x_ref[0, 0, start : start + size].astype(F32)
        normed = normalize(values)[0]
        out_ref[0, 0, start : start + size] = (
            values + normed + mixed_ref[start : start + size]
        ).astype(BF)


def input_grad_kernel(recv_ref, x_ref, g_ref, table_ref, out_ref, rows_ref, mixed_ref):
    r = pl.program_id(0)

    @pl.when(r == 0)
    def _():
        receive(recv_ref, rows_ref)

    mixed_ref[...] = jnp.dot(table_ref[...], rows_ref[r], preferred_element_type=F32)
    for start, size in ROW_CHUNKS:
        values = x_ref[0, 0, start : start + size].astype(F32)
        upstream = g_ref[0, 0, start : start + size].astype(F32)
        normed, scale = normalize(values)
        back = upstream + mixed_ref[start : start + size]
        mean = jnp.sum(back, axis=-1, keepdims=True) * (1.0 / C)
        along = jnp.sum(back * normed, axis=-1, keepdims=True) * (1.0 / C)
        out_ref[0, 0, start : start + size] = (
            upstream + scale * (back - mean - normed * along)
        ).astype(BF)


def from_spectra(kernel, name, recv, arrays, table):
    token_spec = pl.BlockSpec((1, 1, W, C), lambda r: (0, r, 0, 0))
    return pl.pallas_call(
        kernel,
        name=name,
        grid=(ROWS,),
        in_specs=[pl.BlockSpec((BANDS, PACK, 128), lambda r: (0, 0, 0))]
        + [token_spec] * len(arrays)
        + [pl.BlockSpec((WPAD, 2 * KX), lambda r: (0, 0))],
        out_specs=token_spec,
        out_shape=jax.ShapeDtypeStruct((1, ROWS, W, C), BF),
        scratch_shapes=[
            pltpu.VMEM((ROWS, 2 * KX, C), BF),
            pltpu.VMEM((WPAD, C), F32),
        ],
        compiler_params=pltpu.CompilerParams(vmem_limit_bytes=VMEM_LIMIT),
        cost_estimate=pl.CostEstimate(
            flops=2 * ROWS * W * 2 * KX * C, bytes_accessed=3000000, transcendentals=0
        ),
    )(recv, *arrays, table)


def whole(shape):
    return pl.BlockSpec(shape, lambda: (0,) * len(shape))


def spectral_call(kernel, name, operands, outs, scratch):
    return pl.pallas_call(
        kernel,
        name=name,
        in_specs=[whole(operand.shape) for operand in operands],
        out_specs=[whole(out.shape) for out in outs],
        out_shape=outs,
        scratch_shapes=scratch,
        compiler_params=pltpu.CompilerParams(vmem_limit_bytes=VMEM_LIMIT),
        cost_estimate=pl.CostEstimate(
            flops=1000000000, bytes_accessed=6000000, transcendentals=800000
        ),
    )(*operands)


SPECTRA = jax.ShapeDtypeStruct((BANDS, PACK, 128), BF)


def sum_kernel(recv_ref, out_ref):
    total = recv_ref[0].astype(F32)
    for i in range(1, recv_ref.shape[0]):
        total = total + recv_ref[i].astype(F32)
    out_ref[...] = total.astype(BF)


def group_sum_kernel(recv_ref, out_ref):
    for block in range(NB):
        total = recv_ref[block * GROUPS].astype(F32)
        for group in range(1, GROUPS):
            total = total + recv_ref[block * GROUPS + group].astype(F32)
        out_ref[block] = total.astype(BF)


GRAD_SCALE = 1.0 / (SAMPLES * H)


def grads_kernel(recv_ref, w1_ref, b1_ref, w2_ref, b2_ref):
    for block in range(NB):
        chunk = 0
        for out_ref in (w1_ref, w2_ref):
            for part in range(2):
                pieces = [
                    recv_ref[chunk + i, block].astype(F32) * GRAD_SCALE for i in range(3)
                ]
                chunk += 3
                for i in range(3):
                    out_ref[part, block, 24 * i : 24 * i + 24, :] = pieces[i][:, :BS]
                out_ref[part, block, 72:96, :] = unpack_tail(pieces)[:, :BS]
    rows = [
        jnp.concatenate([recv_ref[12, block], recv_ref[13, block]], axis=0).astype(F32)
        * GRAD_SCALE
        for block in range(NB)
    ]
    for out_ref, first in ((b1_ref, 0), (b2_ref, 16)):
        for part in range(2):
            at = first + 8 * part
            for quad in range(2):
                parts = [rows[4 * quad + j][at : at + 8] for j in range(4)]
                for t, joined in enumerate(join_lanes(parts)):
                    lane = 384 * quad + 128 * t
                    out_ref[part : part + 1, lane : lane + 128] = joined[0:1]


def padded_form(weight, block):
    chosen = lax.dynamic_index_in_dim(weight, block, axis=1, keepdims=False)
    padded = jnp.pad(chosen, ((0, 0), (0, 128 - BS), (0, 128 - BS)))
    upper = jnp.concatenate([padded[0], padded[1]], axis=1)
    lower = jnp.concatenate([-padded[1], padded[0]], axis=1)
    return jnp.concatenate([upper, lower], axis=0)


def padded_bias(bias, block):
    chosen = lax.dynamic_index_in_dim(bias.reshape(2, NB, BS), block, axis=1, keepdims=False)
    return jnp.pad(chosen, ((0, 0), (0, 128 - BS))).reshape(1, 256)


def exchange(value):
    return lax.all_to_all(value, "lat", split_axis=0, concat_axis=0, tiled=True)


def on_device(fields, cotangent, w_first, b_first, w_second, b_second):
    block = lax.axis_index("lat") // GROUPS
    lon_fwd = jnp.asarray(LON_FWD, BF)
    lon_inv = jnp.asarray(LON_INV, BF)
    lon_fwd_t = jnp.asarray(LON_FWD.T, BF)
    lon_inv_t = jnp.asarray(LON_INV.T, BF)
    lat = jnp.asarray(LAT, BF)
    w1 = padded_form(w_first, block)
    w2 = padded_form(w_second, block)
    b1 = padded_bias(b_first, block)
    b2 = padded_bias(b_second, block)

    spectra = exchange(to_spectra(fields_kernel, "fields_dft", fields, lon_fwd_t))
    back_rows = exchange(to_spectra(cotangent_kernel, "cot_dft", cotangent, lon_inv_t))

    wide = (MODES * H, 256)
    rows_scratch = pltpu.VMEM((BANDS * TILE_ROWS, 128), F32)
    row_spectra, modes, hidden, slope = spectral_call(
        forward_kernel,
        "spectral_fwd",
        (spectra, lat, w1, b1, w2, b2),
        [
            SPECTRA,
            jax.ShapeDtypeStruct(wide, BF),
            jax.ShapeDtypeStruct(wide, BF),
            jax.ShapeDtypeStruct(wide, F32),
        ],
        [rows_scratch],
    )
    back_spectra, grads = spectral_call(
        backward_kernel,
        "spectral_bwd",
        (back_rows, lat, w1, w2, modes, hidden, slope),
        [SPECTRA, jax.ShapeDtypeStruct((CHUNKS * CHUNK_ROWS, 128), F32)],
        [rows_scratch, pltpu.VMEM(wide, BF), pltpu.VMEM(wide, BF)],
    )
    dp_size = lax.axis_size("dp")
    rows = CHUNKS * CHUNK_ROWS // dp_size
    shares = lax.all_to_all(
        grads.astype(BF).reshape(dp_size, rows, 128), "dp", 0, 0, tiled=True
    )
    share = spectral_call(
        sum_kernel, "grad_sum", (shares,), [jax.ShapeDtypeStruct((rows, 128), BF)], []
    )[0]
    banded = lax.all_gather(share, "lat", axis=0, tiled=False)
    blocks = spectral_call(
        group_sum_kernel, "grad_groups", (banded,), [jax.ShapeDtypeStruct((NB, rows, 128), BF)], []
    )[0]
    every = lax.all_gather(blocks, "dp", axis=0, tiled=False)
    if dp_size != CHUNKS:
        every = (
            every.transpose(1, 0, 2, 3)
            .reshape(NB, CHUNKS, CHUNK_ROWS, 128)
            .transpose(1, 0, 2, 3)
        )
    grad_w = jax.ShapeDtypeStruct((2, NB, BS, BS), F32)
    grad_b = jax.ShapeDtypeStruct((2, C), F32)
    g_w1, g_b1, g_w2, g_b2 = spectral_call(
        grads_kernel, "grad_out", (every,), [grad_w, grad_b, grad_w, grad_b], []
    )

    row_spectra = exchange(row_spectra)
    back_spectra = exchange(back_spectra)
    result = from_spectra(output_kernel, "output", row_spectra, (fields,), lon_inv)
    back_fields = from_spectra(
        input_grad_kernel, "fields_grad", back_spectra, (fields, cotangent), lon_fwd
    )
    return (result, back_fields, g_w1, g_b1, g_w2, g_b2)


def solution(mesh):
    placed = (P("dp", "lat", None, None), P("dp", "lat", None, None), P(), P(), P(), P())
    return jax.shard_map(
        on_device,
        mesh=mesh,
        in_specs=placed,
        out_specs=(P("dp", "lat", None, None), P("dp", "lat", None, None), P(), P(), P(), P()),
        check_vma=False,
    )
```

```python
import math

import jax
import jax.numpy as jnp
import numpy as np
from jax import lax
from jax.experimental import pallas as pl
from jax.experimental.pallas import tpu as pltpu
from jax.sharding import PartitionSpec as P

C = 768
NB = 8
BS = 96
H = 96
W = 180
KX = 64
SAMPLES = 16
EPSILON = 1e-06

BANDS = 32
GROUPS = 4
MODES = KX // GROUPS
ROWS = H // BANDS
WPAD = 192
PACK = 72
CHUNKS = 16
CHUNK_ROWS = 24
BF = jnp.bfloat16
F32 = jnp.float32
VMEM_LIMIT = 16 * 1024 * 1024


def tables():
    w_index = np.arange(W)[:, None]
    k_index = np.arange(KX)[None, :]
    lon = (2.0 * math.pi / W * (w_index * k_index % W)).astype(np.float64)
    fwd = np.stack([np.cos(lon), -np.sin(lon)], axis=1) / math.sqrt(W)
    weight = np.where(k_index == 0, 1.0, 2.0)[:, None, :]
    inv = fwd * weight
    def order(table):
        grouped = table.reshape(W, 2, GROUPS, MODES).transpose(0, 2, 1, 3).reshape(W, 2 * KX)
        padded = np.zeros((WPAD, 2 * KX))
        padded[:W] = grouped
        return padded

    h_index = np.arange(H)
    lat = 2.0 * math.pi / H * (h_index[:, None] * h_index[None, :] % H)
    cosine = np.cos(lat) / math.sqrt(H)
    sine = np.sin(lat) / math.sqrt(H)
    full = np.stack(
        [np.stack([cosine, sine], axis=2), np.stack([-sine, cosine], axis=2)], axis=0
    ).reshape(2 * H, 2 * H)
    return order(fwd), order(inv), full


LON_FWD, LON_INV, LAT = tables()


def lanes(shape):
    return lax.broadcasted_iota(jnp.int32, shape, 1)


def roll(value, shift):
    return pltpu.roll(value, shift % 128, 1)


def pack_tile(tile):
    lane = lanes((24, 128))
    tail = tile[72:96]
    return [
        jnp.where(lane < 96, tile[24 * i : 24 * i + 24], roll(tail, 96 - 32 * i))
        for i in range(3)
    ]


def unpack_tail(pieces):
    lane = lanes((24, 128))
    return jnp.where(
        lane < 32,
        roll(pieces[0], 32),
        jnp.where(lane < 64, roll(pieces[1], 64), roll(pieces[2], 96)),
    )


def block_lanes(value, block):
    start = BS * block
    first, shift = start // 128, start % 128
    head = value[:, 128 * first : 128 * first + 128]
    if shift == 0:
        return head
    head = roll(head, 128 - shift)
    if shift + BS <= 128:
        return head
    after = roll(value[:, 128 * first + 128 : 128 * first + 256], 128 - shift)
    return jnp.where(lanes(head.shape) < 128 - shift, head, after)


def join_lanes(parts):
    lane = lanes(parts[0].shape)
    return [
        jnp.where(lane < 96, parts[0], roll(parts[1], 96)),
        jnp.where(lane < 64, roll(parts[1], 96), roll(parts[2], 64)),
        jnp.where(lane < 32, roll(parts[2], 64), roll(parts[3], 32)),
    ]


ROW_CHUNKS = [(start, min(32, W - start)) for start in range(0, W, 32)]


def normalize(values):
    mean = jnp.sum(values, axis=-1, keepdims=True) * (1.0 / C)
    centered = values - mean
    spread = jnp.sum(centered * centered, axis=-1, keepdims=True) * (1.0 / C)
    scale = 1.0 / jnp.sqrt(spread + EPSILON)
    return centered * scale, scale


def send_packed(acc_ref, out_ref, first):
    for block in range(NB):
        rows = [block_lanes(acc_ref[r], block) for r in range(ROWS)]
        for group in range(GROUPS):
            tile = jnp.concatenate(
                [row[32 * group : 32 * group + 32] for row in rows], axis=0
            )
            pieces = pack_tile(tile)
            out_ref[block * GROUPS + group, first : first + PACK] = jnp.concatenate(
                pieces, axis=0
            ).astype(BF)


def spectra_kernel(x_ref, g_ref, fwd_ref, inv_ref, out_ref, padded_ref, acc_ref):
    step = pl.program_id(0)

    @pl.when(step == 0)
    def _():
        padded_ref[...] = jnp.zeros_like(padded_ref)

    @pl.when(step < ROWS)
    def _():
        for start, size in ROW_CHUNKS:
            values = x_ref[0, 0, start : start + size].astype(F32)
            padded_ref[start : start + size] = normalize(values)[0].astype(BF)
        acc_ref[step] = jnp.dot(fwd_ref[...], padded_ref[...], preferred_element_type=F32)

    @pl.when(step == ROWS - 1)
    def _():
        send_packed(acc_ref, out_ref, 0)

    @pl.when(step >= ROWS)
    def _():
        padded_ref[0:W] = g_ref[0, 0]
        acc_ref[step - ROWS] = jnp.dot(
            inv_ref[...], padded_ref[...], preferred_element_type=F32
        )

    @pl.when(step == 2 * ROWS - 1)
    def _():
        send_packed(acc_ref, out_ref, PACK)


def to_spectra(fields, cotangent, forward, inverse):
    table_spec = pl.BlockSpec((2 * KX, WPAD), lambda r: (0, 0))
    return pl.pallas_call(
        spectra_kernel,
        name="to_spectra",
        grid=(2 * ROWS,),
        in_specs=[
            pl.BlockSpec((1, 1, W, C), lambda r: (0, jnp.minimum(r, ROWS - 1), 0, 0)),
            pl.BlockSpec((1, 1, W, C), lambda r: (0, jnp.maximum(r - ROWS, 0), 0, 0)),
            table_spec,
            table_spec,
        ],
        out_specs=pl.BlockSpec((BANDS, 2 * PACK, 128), lambda r: (0, 0, 0)),
        out_shape=jax.ShapeDtypeStruct((BANDS, 2 * PACK, 128), BF),
        scratch_shapes=[
            pltpu.VMEM((WPAD, C), BF),
            pltpu.VMEM((ROWS, 2 * KX, C), F32),
        ],
        compiler_params=pltpu.CompilerParams(vmem_limit_bytes=VMEM_LIMIT),
        cost_estimate=pl.CostEstimate(
            flops=4 * ROWS * W * 2 * KX * C, bytes_accessed=3000000, transcendentals=0
        ),
    )(fields, cotangent, forward, inverse)


TILE_ROWS = 2 * ROWS * MODES


def unpack_bands(recv_ref, first, rows_ref):
    def one(s, carry):
        pieces = [
            recv_ref[s, first + 24 * i : first + 24 * i + 24, :].astype(F32)
            for i in range(3)
        ]
        base = pl.multiple_of(s * TILE_ROWS, TILE_ROWS)
        for i in range(3):
            rows_ref[pl.ds(base + 24 * i, 24), :] = pieces[i]
        rows_ref[pl.ds(base + 72, 24), :] = unpack_tail(pieces)
        return carry

    lax.fori_loop(0, BANDS, one, 0, unroll=4)


def pack_bands(rows_ref, out_ref):
    def one(s, carry):
        base = pl.multiple_of(s * TILE_ROWS, TILE_ROWS)
        pieces = pack_tile(rows_ref[pl.ds(base, TILE_ROWS), :])
        out_ref[s, 0:PACK] = jnp.concatenate(pieces, axis=0).astype(BF)
        return carry

    lax.fori_loop(0, BANDS, one, 0, unroll=4)


def mode_rows(rows_ref, lat, pair):
    columns = jnp.concatenate(
        [
            rows_ref[pl.ds(2 * pair + j, 2 * H, stride=MODES), :].astype(BF)
            for j in range(2)
        ],
        axis=1,
    )
    done = jnp.dot(lat, columns, preferred_element_type=F32).astype(BF)
    return jnp.concatenate(
        [
            jnp.concatenate(
                [done[0:H, 128 * j : 128 * j + 128], done[H : 2 * H, 128 * j : 128 * j + 128]],
                axis=1,
            )
            for j in range(2)
        ],
        axis=0,
    )


def store_rows(rows_ref, lat, pair, modes):
    columns = jnp.concatenate(
        [
            jnp.concatenate(
                [modes[H * j : H * j + H, 0:128], modes[H * j : H * j + H, 128:256]], axis=0
            )
            for j in range(2)
        ],
        axis=1,
    )
    done = lax.dot_general(
        lat, columns, (((0,), (0,)), ((), ())), preferred_element_type=F32
    )
    for j in range(2):
        rows_ref[pl.ds(2 * pair + j, 2 * H, stride=MODES), :] = done[:, 128 * j : 128 * j + 128]


PAIR_ROWS = 2 * H
PAIRS = MODES // 2


def fill_weight(weight_ref, form_ref):
    form_ref[...] = jnp.zeros_like(form_ref)
    real = weight_ref[0, 0]
    imag = weight_ref[1, 0]
    form_ref[0:BS, 0:BS] = real
    form_ref[0:BS, 128 : 128 + BS] = imag
    form_ref[128 : 128 + BS, 0:BS] = -imag
    form_ref[128 : 128 + BS, 128 : 128 + BS] = real


def choose_bias(block, bias_ref):
    bias = bias_ref[...]
    chosen = block_lanes(bias, 0)
    for other in range(1, NB):
        chosen = jnp.where(block == other, block_lanes(bias, other), chosen)
    chosen = jnp.where(lanes(chosen.shape) < BS, chosen, 0.0)
    return jnp.concatenate([chosen[0:1], chosen[1:2]], axis=1)


NT = (((1,), (1,)), ((), ()))
TN = (((0,), (0,)), ((), ()))


def gradient_kernel(
    block_ref, recv_ref, lat_ref, first_ref, bias_ref, second_ref,
    hidden_ref, pre_ref, grad_ref,
    w1_ref, w2_ref, rows_ref, back_rows_ref, modes_ref, filtered_ref, sums_ref,
):
    fill_weight(first_ref, w1_ref)
    fill_weight(second_ref, w2_ref)
    bias = choose_bias(block_ref[0], bias_ref)
    unpack_bands(recv_ref, 0, rows_ref)
    unpack_bands(recv_ref, PACK, back_rows_ref)
    lat = lat_ref[...]
    w1 = w1_ref[...]
    w2 = w2_ref[...]
    for pair in range(PAIRS):
        span = slice(PAIR_ROWS * pair, PAIR_ROWS * pair + PAIR_ROWS)
        modes = mode_rows(rows_ref, lat, pair)
        modes_ref[span] = modes
        pre = jnp.dot(modes, w1, preferred_element_type=F32) + bias
        cdf = 0.5 + 0.5 * lax.erf(pre * math.sqrt(0.5))
        hidden_ref[span] = (pre * cdf).astype(BF)
        slope = cdf + pre * (jnp.exp(-0.5 * pre * pre) * (1.0 / math.sqrt(2.0 * math.pi)))
        back_filtered = mode_rows(back_rows_ref, lat, pair)
        filtered_ref[span] = back_filtered
        back_hidden = lax.dot_general(back_filtered, w2, NT, preferred_element_type=F32)
        pre_ref[span] = (back_hidden * slope).astype(BF)
    ones = jnp.ones((8, MODES * H), BF)
    row = 0
    bias_rows = []
    for left_ref, right_ref in ((modes_ref, pre_ref), (hidden_ref, filtered_ref)):
        right = right_ref[...]
        gathered = lax.dot_general(left_ref[...], right, TN, preferred_element_type=F32)
        real = gathered[0:BS, 0:128] + gathered[128 : 128 + BS, 128:256]
        imag = gathered[0:BS, 128:256] - gathered[128 : 128 + BS, 0:128]
        for part in (real, imag):
            for piece in pack_tile(part):
                sums_ref[row : row + 24] = piece
                row += 24
        bias = jnp.dot(ones, right, preferred_element_type=F32)
        bias_rows += [bias[:, 0:128], bias[:, 128:256]]
    for value in bias_rows:
        sums_ref[row : row + 8] = value
        row += 8
    sums_ref[row:] = jnp.zeros((CHUNKS * CHUNK_ROWS - row, 128), F32)
    for chunk in range(CHUNKS):
        grad_ref[chunk] = sums_ref[CHUNK_ROWS * chunk : CHUNK_ROWS * chunk + CHUNK_ROWS].astype(
            BF
        )


def return_kernel(
    block_ref, hidden_ref, pre_ref, lat_ref, first_ref, second_ref, bias_ref,
    row_ref, back_ref,
    w1_ref, w2_ref, rows_ref, back_rows_ref,
):
    fill_weight(first_ref, w1_ref)
    fill_weight(second_ref, w2_ref)
    bias = choose_bias(block_ref[0], bias_ref)
    lat = lat_ref[...]
    w1 = w1_ref[...]
    w2 = w2_ref[...]
    for pair in range(PAIRS):
        span = slice(PAIR_ROWS * pair, PAIR_ROWS * pair + PAIR_ROWS)
        filtered = jnp.dot(hidden_ref[span], w2, preferred_element_type=F32) + bias
        store_rows(rows_ref, lat, pair, filtered.astype(BF))
        back_modes = lax.dot_general(pre_ref[span], w1, NT, preferred_element_type=F32)
        store_rows(back_rows_ref, lat, pair, back_modes.astype(BF))
    pack_bands(rows_ref, row_ref)
    pack_bands(back_rows_ref, back_ref)


PAIR_ROWS = 2 * H
PAIRS = MODES // 2
WIDE = (MODES * H, 256)
FORM = pltpu.VMEM((256, 256), BF)
BAND_ROWS = pltpu.VMEM((2 * H * MODES, 128), F32)


def block_call(kernel, name, block, operands, specs, outs, scratch):
    return pl.pallas_call(
        kernel,
        name=name,
        grid_spec=pltpu.PrefetchScalarGridSpec(
            num_scalar_prefetch=1,
            grid=(1,),
            in_specs=[
                pl.BlockSpec((2, 1, BS, BS), lambda i, n: (0, n[0], 0, 0))
                if spec == "weight"
                else pl.BlockSpec(operand.shape, lambda i, n, d=operand.ndim: (0,) * d)
                for operand, spec in zip(operands, specs)
            ],
            out_specs=[
                pl.BlockSpec(out.shape, lambda i, n, d=len(out.shape): (0,) * d)
                for out in outs
            ],
            scratch_shapes=scratch,
        ),
        out_shape=outs,
        compiler_params=pltpu.CompilerParams(vmem_limit_bytes=24 * 1024 * 1024),
        cost_estimate=pl.CostEstimate(
            flops=1000000000, bytes_accessed=6000000, transcendentals=800000
        ),
    )(block, *operands)


def receive(recv_ref, rows_ref):
    for group in range(GROUPS):
        for quad in range(2):
            tiles = []
            for block in range(4):
                band = (4 * quad + block) * GROUPS + group
                pieces = [
                    recv_ref[band, 24 * i : 24 * i + 24, :].astype(F32) for i in range(3)
                ]
                tiles.append(jnp.concatenate(pieces + [unpack_tail(pieces)], axis=0))
            for t, joined in enumerate(join_lanes(tiles)):
                for r in range(ROWS):
                    rows_ref[
                        r,
                        32 * group : 32 * group + 32,
                        384 * quad + 128 * t : 384 * quad + 128 * t + 128,
                    ] = joined[32 * r : 32 * r + 32].astype(BF)


def output_kernel(recv_ref, x_ref, table_ref, out_ref, rows_ref, mixed_ref):
    r = pl.program_id(0)

    @pl.when(r == 0)
    def _():
        receive(recv_ref, rows_ref)

    mixed_ref[...] = jnp.dot(table_ref[...], rows_ref[r], preferred_element_type=F32)
    for start, size in ROW_CHUNKS:
        values = x_ref[0, 0, start : start + size].astype(F32)
        normed = normalize(values)[0]
        out_ref[0, 0, start : start + size] = (
            values + normed + mixed_ref[start : start + size]
        ).astype(BF)


def input_grad_kernel(recv_ref, x_ref, g_ref, table_ref, out_ref, rows_ref, mixed_ref):
    r = pl.program_id(0)

    @pl.when(r == 0)
    def _():
        receive(recv_ref, rows_ref)

    mixed_ref[...] = jnp.dot(table_ref[...], rows_ref[r], preferred_element_type=F32)
    for start, size in ROW_CHUNKS:
        values = x_ref[0, 0, start : start + size].astype(F32)
        upstream = g_ref[0, 0, start : start + size].astype(F32)
        normed, scale = normalize(values)
        back = upstream + mixed_ref[start : start + size]
        mean = jnp.sum(back, axis=-1, keepdims=True) * (1.0 / C)
        along = jnp.sum(back * normed, axis=-1, keepdims=True) * (1.0 / C)
        out_ref[0, 0, start : start + size] = (
            upstream + scale * (back - mean - normed * along)
        ).astype(BF)


def from_spectra(kernel, name, recv, arrays, table):
    token_spec = pl.BlockSpec((1, 1, W, C), lambda r: (0, r, 0, 0))
    return pl.pallas_call(
        kernel,
        name=name,
        grid=(ROWS,),
        in_specs=[pl.BlockSpec((BANDS, PACK, 128), lambda r: (0, 0, 0))]
        + [token_spec] * len(arrays)
        + [pl.BlockSpec((WPAD, 2 * KX), lambda r: (0, 0))],
        out_specs=token_spec,
        out_shape=jax.ShapeDtypeStruct((1, ROWS, W, C), BF),
        scratch_shapes=[
            pltpu.VMEM((ROWS, 2 * KX, C), BF),
            pltpu.VMEM((WPAD, C), F32),
        ],
        compiler_params=pltpu.CompilerParams(vmem_limit_bytes=VMEM_LIMIT),
        cost_estimate=pl.CostEstimate(
            flops=2 * ROWS * W * 2 * KX * C, bytes_accessed=3000000, transcendentals=0
        ),
    )(recv, *arrays, table)


def whole(shape):
    return pl.BlockSpec(shape, lambda: (0,) * len(shape))


def spectral_call(kernel, name, operands, outs, scratch):
    return pl.pallas_call(
        kernel,
        name=name,
        in_specs=[whole(operand.shape) for operand in operands],
        out_specs=[whole(out.shape) for out in outs],
        out_shape=outs,
        scratch_shapes=scratch,
        compiler_params=pltpu.CompilerParams(vmem_limit_bytes=VMEM_LIMIT),
        cost_estimate=pl.CostEstimate(
            flops=1000000000, bytes_accessed=6000000, transcendentals=800000
        ),
    )(*operands)


def share_kernel(recv_ref, held_ref, out_ref):
    total = recv_ref[0].astype(F32)
    for i in range(1, recv_ref.shape[0]):
        total = total + recv_ref[i].astype(F32)
    share = total.astype(BF)
    for band in range(BANDS):
        out_ref[band] = share


def add_share(shares, held):
    return pl.pallas_call(
        share_kernel,
        name="grad_share",
        grid=(1,),
        in_specs=[
            pl.BlockSpec(shares.shape, lambda i: (0, 0, 0)),
            pl.BlockSpec(memory_space=pl.ANY),
        ],
        out_specs=pl.BlockSpec((BANDS, CHUNK_ROWS, 128), lambda i: (0, 3, 0)),
        out_shape=jax.ShapeDtypeStruct(held.shape, BF),
        input_output_aliases={1: 0},
        compiler_params=pltpu.CompilerParams(vmem_limit_bytes=VMEM_LIMIT),
    )(shares, held)


def group_sum_kernel(recv_ref, out_ref):
    for block in range(NB):
        total = recv_ref[block * GROUPS].astype(F32)
        for group in range(1, GROUPS):
            total = total + recv_ref[block * GROUPS + group].astype(F32)
        out_ref[block] = total.astype(BF)


def group_sums(message):
    return pl.pallas_call(
        group_sum_kernel,
        name="grad_groups",
        grid=(1,),
        in_specs=[pl.BlockSpec((BANDS, CHUNK_ROWS, 128), lambda i: (0, 3, 0))],
        out_specs=pl.BlockSpec((NB, CHUNK_ROWS, 128), lambda i: (0, 0, 0)),
        out_shape=jax.ShapeDtypeStruct((NB, CHUNK_ROWS, 128), BF),
        compiler_params=pltpu.CompilerParams(vmem_limit_bytes=VMEM_LIMIT),
    )(message)


GRAD_SCALE = 1.0 / (SAMPLES * H)


def grads_kernel(recv_ref, w1_ref, b1_ref, w2_ref, b2_ref):
    for block in range(NB):
        chunk = 0
        for out_ref in (w1_ref, w2_ref):
            for part in range(2):
                pieces = [
                    recv_ref[chunk + i, block].astype(F32) * GRAD_SCALE for i in range(3)
                ]
                chunk += 3
                for i in range(3):
                    out_ref[part, block, 24 * i : 24 * i + 24, :] = pieces[i][:, :BS]
                out_ref[part, block, 72:96, :] = unpack_tail(pieces)[:, :BS]
    rows = [
        jnp.concatenate([recv_ref[12, block], recv_ref[13, block]], axis=0).astype(F32)
        * GRAD_SCALE
        for block in range(NB)
    ]
    for out_ref, first in ((b1_ref, 0), (b2_ref, 16)):
        for part in range(2):
            at = first + 8 * part
            for quad in range(2):
                parts = [rows[4 * quad + j][at : at + 8] for j in range(4)]
                for t, joined in enumerate(join_lanes(parts)):
                    lane = 384 * quad + 128 * t
                    out_ref[part : part + 1, lane : lane + 128] = joined[0:1]


def exchange(value):
    return lax.all_to_all(value, "lat", split_axis=0, concat_axis=0, tiled=True)


def on_device(fields, cotangent, w_first, b_first, w_second, b_second):
    block = (lax.axis_index("lat") // GROUPS).astype(jnp.int32).reshape(1)
    lon_fwd = jnp.asarray(LON_FWD, BF)
    lon_inv = jnp.asarray(LON_INV, BF)
    lon_fwd_t = jnp.asarray(LON_FWD.T, BF)
    lon_inv_t = jnp.asarray(LON_INV.T, BF)
    lat = jnp.asarray(LAT, BF)

    spectra = exchange(to_spectra(fields, cotangent, lon_fwd_t, lon_inv_t))
    wide = jax.ShapeDtypeStruct(WIDE, BF)
    hidden, pre, grads = block_call(
        gradient_kernel,
        "spectral_grads",
        block,
        (spectra, lat, w_first, b_first, w_second),
        ("", "", "weight", "", "weight"),
        [wide, wide, jax.ShapeDtypeStruct((CHUNKS, CHUNK_ROWS, 128), BF)],
        [FORM, FORM, BAND_ROWS, BAND_ROWS, pltpu.VMEM(WIDE, BF), pltpu.VMEM(WIDE, BF)]
        + [pltpu.VMEM((CHUNKS * CHUNK_ROWS, 128), F32)],
    )
    dp_size = lax.axis_size("dp")
    if dp_size == CHUNKS:
        shares = lax.all_to_all(grads, "dp", 0, 0, tiled=True)
    else:
        shares = grads
    row_send, back_send = block_call(
        return_kernel,
        "spectral_return",
        block,
        (hidden, pre, lat, w_first, w_second, b_second),
        ("", "", "", "weight", "weight", ""),
        [
            jax.ShapeDtypeStruct((BANDS, PACK + CHUNK_ROWS, 128), BF),
            jax.ShapeDtypeStruct((BANDS, PACK, 128), BF),
        ],
        [FORM, FORM, BAND_ROWS, BAND_ROWS],
    )
    message = exchange(add_share(shares, row_send))
    back_send, message = lax.optimization_barrier((back_send, message))
    back_spectra = exchange(back_send)
    blocks = group_sums(message)
    every = lax.all_gather(blocks, "dp", axis=0, tiled=False)
    grad_w = jax.ShapeDtypeStruct((2, NB, BS, BS), F32)
    grad_b = jax.ShapeDtypeStruct((2, C), F32)
    g_w1, g_b1, g_w2, g_b2 = spectral_call(
        grads_kernel, "grad_out", (every,), [grad_w, grad_b, grad_w, grad_b], []
    )
    result = from_spectra(output_kernel, "output", message, (fields,), lon_inv)
    back_fields = from_spectra(
        input_grad_kernel, "fields_grad", back_spectra, (fields, cotangent), lon_fwd
    )
    return (result, back_fields, g_w1, g_b1, g_w2, g_b2)


def solution(mesh):
    placed = (P("dp", "lat", None, None), P("dp", "lat", None, None), P(), P(), P(), P())
    return jax.shard_map(
        on_device,
        mesh=mesh,
        in_specs=placed,
        out_specs=(P("dp", "lat", None, None), P("dp", "lat", None, None), P(), P(), P(), P()),
        check_vma=False,
    )
```

```python
import math

import jax
import jax.numpy as jnp
import numpy as np
from jax import lax
from jax.experimental import pallas as pl
from jax.experimental.pallas import tpu as pltpu
from jax.sharding import PartitionSpec as P

C = 768
NB = 8
BS = 96
H = 96
W = 180
KX = 64
SAMPLES = 16
EPSILON = 1e-06

BANDS = 32
GROUPS = 4
MODES = KX // GROUPS
ROWS = H // BANDS
WPAD = 192
PACK = 72
CHUNKS = 16
CHUNK_ROWS = 24
BF = jnp.bfloat16
F32 = jnp.float32
VMEM_LIMIT = 10 * 1024 * 1024


def tables():
    w_index = np.arange(W)[:, None]
    k_index = np.arange(KX)[None, :]
    lon = (2.0 * math.pi / W * (w_index * k_index % W)).astype(np.float64)
    fwd = np.stack([np.cos(lon), -np.sin(lon)], axis=1) / math.sqrt(W)
    weight = np.where(k_index == 0, 1.0, 2.0)[:, None, :]
    inv = fwd * weight
    def order(table):
        grouped = table.reshape(W, 2, GROUPS, MODES).transpose(0, 2, 1, 3).reshape(W, 2 * KX)
        padded = np.zeros((WPAD, 2 * KX))
        padded[:W] = grouped
        return padded

    h_index = np.arange(H)
    lat = 2.0 * math.pi / H * (h_index[:, None] * h_index[None, :] % H)
    cosine = np.cos(lat) / math.sqrt(H)
    sine = np.sin(lat) / math.sqrt(H)
    full = np.stack(
        [np.stack([cosine, sine], axis=2), np.stack([-sine, cosine], axis=2)], axis=0
    ).reshape(2 * H, 2 * H)
    return order(fwd), order(inv), full


LON_FWD, LON_INV, LAT = tables()


def lanes(shape):
    return lax.broadcasted_iota(jnp.int32, shape, 1)


def roll(value, shift):
    return pltpu.roll(value, shift % 128, 1)


def pack_tile(tile):
    lane = lanes((24, 128))
    tail = tile[72:96]
    return [
        jnp.where(lane < 96, tile[24 * i : 24 * i + 24], roll(tail, 96 - 32 * i))
        for i in range(3)
    ]


def unpack_tail(pieces):
    lane = lanes((24, 128))
    return jnp.where(
        lane < 32,
        roll(pieces[0], 32),
        jnp.where(lane < 64, roll(pieces[1], 64), roll(pieces[2], 96)),
    )


def block_lanes(value, block):
    start = BS * block
    first, shift = start // 128, start % 128
    head = value[:, 128 * first : 128 * first + 128]
    if shift == 0:
        return head
    head = roll(head, 128 - shift)
    if shift + BS <= 128:
        return head
    after = roll(value[:, 128 * first + 128 : 128 * first + 256], 128 - shift)
    return jnp.where(lanes(head.shape) < 128 - shift, head, after)


def join_lanes(parts):
    lane = lanes(parts[0].shape)
    return [
        jnp.where(lane < 96, parts[0], roll(parts[1], 96)),
        jnp.where(lane < 64, roll(parts[1], 96), roll(parts[2], 64)),
        jnp.where(lane < 32, roll(parts[2], 64), roll(parts[3], 32)),
    ]


ROW_CHUNKS = [(start, min(32, W - start)) for start in range(0, W, 32)]


def normalize(values):
    mean = jnp.sum(values, axis=-1, keepdims=True) * (1.0 / C)
    centered = values - mean
    spread = jnp.sum(centered * centered, axis=-1, keepdims=True) * (1.0 / C)
    scale = 1.0 / jnp.sqrt(spread + EPSILON)
    return centered * scale, scale


def send_packed(acc_ref, out_ref, first):
    for block in range(NB):
        rows = [block_lanes(acc_ref[r], block) for r in range(ROWS)]
        for group in range(GROUPS):
            tile = jnp.concatenate(
                [row[32 * group : 32 * group + 32] for row in rows], axis=0
            )
            pieces = pack_tile(tile)
            out_ref[block * GROUPS + group, first : first + PACK] = jnp.concatenate(
                pieces, axis=0
            ).astype(BF)


def spectra_kernel(
    x_ref, g_ref, fwd_ref, inv_ref, out_ref,
    x_rows, g_rows, fwd_table, inv_table, padded_ref, acc_ref, sems,
):
    copies = [pltpu.make_async_copy(x_ref.at[0, 0], x_rows.at[0], sems.at[0])]
    copies += [pltpu.make_async_copy(fwd_ref, fwd_table, sems.at[1])]
    copies += [
        pltpu.make_async_copy(x_ref.at[0, r], x_rows.at[r], sems.at[1 + r])
        for r in range(1, ROWS)
    ]
    copies += [pltpu.make_async_copy(inv_ref, inv_table, sems.at[1 + ROWS])]
    copies += [
        pltpu.make_async_copy(g_ref.at[0, r], g_rows.at[r], sems.at[2 + ROWS + r])
        for r in range(ROWS)
    ]
    for copy in copies:
        copy.start()
    padded_ref[W - 20 :] = jnp.zeros((WPAD - W + 20, C), BF)
    for r in range(ROWS):
        copies[0 if r == 0 else 1 + r].wait()
        for start, size in ROW_CHUNKS:
            values = x_rows[r, start : start + size].astype(F32)
            padded_ref[start : start + size] = normalize(values)[0].astype(BF)
        if r == 0:
            copies[1].wait()
        acc_ref[r] = jnp.dot(fwd_table[...], padded_ref[...], preferred_element_type=F32)
    send_packed(acc_ref, out_ref, 0)
    copies[1 + ROWS].wait()
    for r in range(ROWS):
        copies[2 + ROWS + r].wait()
        padded_ref[0:W] = g_rows[r]
        acc_ref[r] = jnp.dot(inv_table[...], padded_ref[...], preferred_element_type=F32)
    send_packed(acc_ref, out_ref, PACK)


def to_spectra(fields, cotangent, forward, inverse):
    held = pl.BlockSpec(memory_space=pltpu.HBM)
    return pl.pallas_call(
        spectra_kernel,
        name="to_spectra",
        in_specs=[held, held, held, held],
        out_specs=pl.BlockSpec(memory_space=pltpu.VMEM),
        out_shape=jax.ShapeDtypeStruct((BANDS, 2 * PACK, 128), BF),
        scratch_shapes=[
            pltpu.VMEM((ROWS, W, C), BF),
            pltpu.VMEM((ROWS, W, C), BF),
            pltpu.VMEM((2 * KX, WPAD), BF),
            pltpu.VMEM((2 * KX, WPAD), BF),
            pltpu.VMEM((WPAD, C), BF),
            pltpu.VMEM((ROWS, 2 * KX, C), F32),
            pltpu.SemaphoreType.DMA((2 + 2 * ROWS,)),
        ],
        compiler_params=pltpu.CompilerParams(vmem_limit_bytes=VMEM_LIMIT),
        cost_estimate=pl.CostEstimate(
            flops=4 * ROWS * W * 2 * KX * C, bytes_accessed=3000000, transcendentals=0
        ),
    )(*[pltpu.with_memory_space_constraint(a, pltpu.HBM) for a in (fields, cotangent, forward, inverse)])


TILE_ROWS = 2 * ROWS * MODES


def unpack_bands(recv_ref, first, rows_ref):
    def one(s, carry):
        pieces = [
            recv_ref[s, first + 24 * i : first + 24 * i + 24, :].astype(F32)
            for i in range(3)
        ]
        base = pl.multiple_of(s * TILE_ROWS, TILE_ROWS)
        for i in range(3):
            rows_ref[pl.ds(base + 24 * i, 24), :] = pieces[i]
        rows_ref[pl.ds(base + 72, 24), :] = unpack_tail(pieces)
        return carry

    lax.fori_loop(0, BANDS, one, 0, unroll=4)


def pack_bands(rows_ref, first, out_ref):
    def one(s, carry):
        base = pl.multiple_of(s * TILE_ROWS, TILE_ROWS)
        pieces = pack_tile(rows_ref[pl.ds(base, TILE_ROWS), :])
        out_ref[s, first : first + PACK] = jnp.concatenate(pieces, axis=0).astype(BF)
        return carry

    lax.fori_loop(0, BANDS, one, 0, unroll=4)


def mode_rows(rows_ref, lat, pair):
    columns = jnp.concatenate(
        [
            rows_ref[pl.ds(2 * pair + j, 2 * H, stride=MODES), :].astype(BF)
            for j in range(2)
        ],
        axis=1,
    )
    done = jnp.dot(lat, columns, preferred_element_type=F32).astype(BF)
    return jnp.concatenate(
        [
            jnp.concatenate(
                [done[0:H, 128 * j : 128 * j + 128], done[H : 2 * H, 128 * j : 128 * j + 128]],
                axis=1,
            )
            for j in range(2)
        ],
        axis=0,
    )


def store_rows(rows_ref, lat, pair, modes):
    columns = jnp.concatenate(
        [
            jnp.concatenate(
                [modes[H * j : H * j + H, 0:128], modes[H * j : H * j + H, 128:256]], axis=0
            )
            for j in range(2)
        ],
        axis=1,
    )
    done = lax.dot_general(
        lat, columns, (((0,), (0,)), ((), ())), preferred_element_type=F32
    )
    for j in range(2):
        rows_ref[pl.ds(2 * pair + j, 2 * H, stride=MODES), :] = done[:, 128 * j : 128 * j + 128]


PAIR_ROWS = 2 * H
PAIRS = MODES // 2


def fill_weight(weight_ref, form_ref):
    form_ref[...] = jnp.zeros_like(form_ref)
    real = weight_ref[0, 0]
    imag = weight_ref[1, 0]
    form_ref[0:BS, 0:BS] = real
    form_ref[0:BS, 128 : 128 + BS] = imag
    form_ref[128 : 128 + BS, 0:BS] = -imag
    form_ref[128 : 128 + BS, 128 : 128 + BS] = real


def choose_bias(block, bias_ref):
    bias = bias_ref[...]
    chosen = block_lanes(bias, 0)
    for other in range(1, NB):
        chosen = jnp.where(block == other, block_lanes(bias, other), chosen)
    chosen = jnp.where(lanes(chosen.shape) < BS, chosen, 0.0)
    return jnp.concatenate([chosen[0:1], chosen[1:2]], axis=1)


NT = (((1,), (1,)), ((), ()))
TN = (((0,), (0,)), ((), ()))


def gradient_kernel(
    block_ref, recv_ref, lat_ref, first_ref, bias_ref, second_ref,
    kept_ref, grad_ref,
    w1_ref, w2_ref, rows_ref, back_rows_ref, modes_ref, filtered_ref, sums_ref,
):
    fill_weight(first_ref, w1_ref)
    fill_weight(second_ref, w2_ref)
    bias = choose_bias(block_ref[0], bias_ref)
    unpack_bands(recv_ref, 0, rows_ref)
    unpack_bands(recv_ref, PACK, back_rows_ref)
    lat = lat_ref[...]
    w1 = w1_ref[...]
    w2 = w2_ref[...]
    for pair in range(PAIRS):
        span = slice(PAIR_ROWS * pair, PAIR_ROWS * pair + PAIR_ROWS)
        modes = mode_rows(rows_ref, lat, pair)
        modes_ref[span] = modes
        pre = jnp.dot(modes, w1, preferred_element_type=F32) + bias
        cdf = 0.5 + 0.5 * lax.erf(pre * math.sqrt(0.5))
        kept_ref[0, span] = (pre * cdf).astype(BF)
        slope = cdf + pre * (jnp.exp(-0.5 * pre * pre) * (1.0 / math.sqrt(2.0 * math.pi)))
        back_filtered = mode_rows(back_rows_ref, lat, pair)
        filtered_ref[span] = back_filtered
        back_hidden = lax.dot_general(back_filtered, w2, NT, preferred_element_type=F32)
        kept_ref[1, span] = (back_hidden * slope).astype(BF)
    ones = jnp.ones((8, MODES * H), BF)
    row = 0
    bias_rows = []
    for left_ref, right_ref in ((modes_ref, kept_ref.at[1]), (kept_ref.at[0], filtered_ref)):
        right = right_ref[...]
        gathered = lax.dot_general(left_ref[...], right, TN, preferred_element_type=F32)
        real = gathered[0:BS, 0:128] + gathered[128 : 128 + BS, 128:256]
        imag = gathered[0:BS, 128:256] - gathered[128 : 128 + BS, 0:128]
        for part in (real, imag):
            for piece in pack_tile(part):
                sums_ref[row : row + 24] = piece
                row += 24
        bias = jnp.dot(ones, right, preferred_element_type=F32)
        bias_rows += [bias[:, 0:128], bias[:, 128:256]]
    for value in bias_rows:
        sums_ref[row : row + 8] = value
        row += 8
    sums_ref[row:] = jnp.zeros((CHUNKS * CHUNK_ROWS - row, 128), F32)
    for chunk in range(CHUNKS):
        grad_ref[chunk] = sums_ref[CHUNK_ROWS * chunk : CHUNK_ROWS * chunk + CHUNK_ROWS].astype(
            BF
        )


def return_kernel(
    block_ref, kept_ref, lat_ref, first_ref, second_ref, bias_ref,
    out_ref,
    w1_ref, w2_ref, rows_ref, back_rows_ref,
):
    fill_weight(first_ref, w1_ref)
    fill_weight(second_ref, w2_ref)
    bias = choose_bias(block_ref[0], bias_ref)
    lat = lat_ref[...]
    w1 = w1_ref[...]
    w2 = w2_ref[...]
    for pair in range(PAIRS):
        span = slice(PAIR_ROWS * pair, PAIR_ROWS * pair + PAIR_ROWS)
        filtered = jnp.dot(kept_ref[0, span], w2, preferred_element_type=F32) + bias
        store_rows(rows_ref, lat, pair, filtered.astype(BF))
        back_modes = lax.dot_general(kept_ref[1, span], w1, NT, preferred_element_type=F32)
        store_rows(back_rows_ref, lat, pair, back_modes.astype(BF))
    pack_bands(rows_ref, 0, out_ref)
    pack_bands(back_rows_ref, PACK, out_ref)


PAIR_ROWS = 2 * H
PAIRS = MODES // 2
WIDE = (MODES * H, 256)
FORM = pltpu.VMEM((256, 256), BF)
BAND_ROWS = pltpu.VMEM((2 * H * MODES, 128), F32)


def block_call(kernel, name, block, operands, specs, outs, scratch):
    return pl.pallas_call(
        kernel,
        name=name,
        grid_spec=pltpu.PrefetchScalarGridSpec(
            num_scalar_prefetch=1,
            grid=(1,),
            in_specs=[
                pl.BlockSpec((2, 1, BS, BS), lambda i, n: (0, n[0], 0, 0))
                if spec == "weight"
                else pl.BlockSpec(operand.shape, lambda i, n, d=operand.ndim: (0,) * d)
                for operand, spec in zip(operands, specs)
            ],
            out_specs=[
                pl.BlockSpec(out.shape, lambda i, n, d=len(out.shape): (0,) * d)
                for out in outs
            ],
            scratch_shapes=scratch,
        ),
        out_shape=outs,
        compiler_params=pltpu.CompilerParams(vmem_limit_bytes=14 * 1024 * 1024),
        cost_estimate=pl.CostEstimate(
            flops=1000000000, bytes_accessed=6000000, transcendentals=800000
        ),
    )(block, *operands)


def receive(recv_ref, first, rows_ref):
    for group in range(GROUPS):
        for quad in range(2):
            tiles = []
            for block in range(4):
                band = (4 * quad + block) * GROUPS + group
                pieces = [
                    recv_ref[band, first + 24 * i : first + 24 * i + 24, :].astype(F32)
                    for i in range(3)
                ]
                tiles.append(jnp.concatenate(pieces + [unpack_tail(pieces)], axis=0))
            for t, joined in enumerate(join_lanes(tiles)):
                for r in range(ROWS):
                    rows_ref[
                        r,
                        32 * group : 32 * group + 32,
                        384 * quad + 128 * t : 384 * quad + 128 * t + 128,
                    ] = joined[32 * r : 32 * r + 32].astype(BF)


def output_kernel(
    recv_ref, x_ref, g_ref, fwd_ref, inv_ref, out_ref, grad_ref,
    rows_ref, back_rows_ref, mixed_ref, back_ref,
):
    r = pl.program_id(0)

    @pl.when(r == 0)
    def _():
        receive(recv_ref, 0, rows_ref)
        receive(recv_ref, PACK, back_rows_ref)

    mixed_ref[...] = jnp.dot(inv_ref[...], rows_ref[r], preferred_element_type=F32)
    back_ref[...] = jnp.dot(fwd_ref[...], back_rows_ref[r], preferred_element_type=F32)
    for start, size in ROW_CHUNKS:
        span = slice(start, start + size)
        values = x_ref[0, 0, span].astype(F32)
        normed, scale = normalize(values)
        out_ref[0, 0, span] = (values + normed + mixed_ref[span]).astype(BF)
        upstream = g_ref[0, 0, span].astype(F32)
        back = upstream + back_ref[span]
        mean = jnp.sum(back, axis=-1, keepdims=True) * (1.0 / C)
        along = jnp.sum(back * normed, axis=-1, keepdims=True) * (1.0 / C)
        grad_ref[0, 0, span] = (upstream + scale * (back - mean - normed * along)).astype(BF)


def from_spectra(recv, fields, cotangent, forward, inverse):
    token_spec = pl.BlockSpec((1, 1, W, C), lambda r: (0, r, 0, 0))
    table_spec = pl.BlockSpec((WPAD, 2 * KX), lambda r: (0, 0))
    token = jax.ShapeDtypeStruct((1, ROWS, W, C), BF)
    return pl.pallas_call(
        output_kernel,
        name="from_spectra",
        grid=(ROWS,),
        in_specs=[
            pl.BlockSpec((BANDS, 2 * PACK, 128), lambda r: (0, 0, 0)),
            token_spec,
            token_spec,
            table_spec,
            table_spec,
        ],
        out_specs=[token_spec, token_spec],
        out_shape=[token, token],
        scratch_shapes=[
            pltpu.VMEM((ROWS, 2 * KX, C), BF),
            pltpu.VMEM((ROWS, 2 * KX, C), BF),
            pltpu.VMEM((WPAD, C), F32),
            pltpu.VMEM((WPAD, C), F32),
        ],
        compiler_params=pltpu.CompilerParams(vmem_limit_bytes=VMEM_LIMIT),
        cost_estimate=pl.CostEstimate(
            flops=4 * ROWS * W * 2 * KX * C, bytes_accessed=5000000, transcendentals=0
        ),
    )(recv, fields, cotangent, forward, inverse)


def whole(shape):
    return pl.BlockSpec(shape, lambda: (0,) * len(shape))


def spectral_call(kernel, name, operands, outs, scratch):
    return pl.pallas_call(
        kernel,
        name=name,
        in_specs=[whole(operand.shape) for operand in operands],
        out_specs=[whole(out.shape) for out in outs],
        out_shape=outs,
        scratch_shapes=scratch,
        compiler_params=pltpu.CompilerParams(vmem_limit_bytes=VMEM_LIMIT),
        cost_estimate=pl.CostEstimate(
            flops=1000000, bytes_accessed=1000000, transcendentals=0
        ),
    )(*operands)


def share_kernel(recv_ref, out_ref):
    total = recv_ref[0].astype(F32)
    for i in range(1, recv_ref.shape[0]):
        total = total + recv_ref[i].astype(F32)
    share = total.astype(BF)
    for band in range(BANDS):
        out_ref[band] = share


def group_sum_kernel(recv_ref, out_ref):
    for block in range(NB):
        total = recv_ref[block * GROUPS].astype(F32)
        for group in range(1, GROUPS):
            total = total + recv_ref[block * GROUPS + group].astype(F32)
        out_ref[block] = total.astype(BF)


GRAD_SCALE = 1.0 / (SAMPLES * H)


def grads_kernel(recv_ref, w1_ref, b1_ref, w2_ref, b2_ref):
    for block in range(NB):
        chunk = 0
        for out_ref in (w1_ref, w2_ref):
            for part in range(2):
                pieces = [
                    recv_ref[chunk + i, block].astype(F32) * GRAD_SCALE for i in range(3)
                ]
                chunk += 3
                for i in range(3):
                    out_ref[part, block, 24 * i : 24 * i + 24, :] = pieces[i][:, :BS]
                out_ref[part, block, 72:96, :] = unpack_tail(pieces)[:, :BS]
    rows = [
        jnp.concatenate([recv_ref[12, block], recv_ref[13, block]], axis=0).astype(F32)
        * GRAD_SCALE
        for block in range(NB)
    ]
    for out_ref, first in ((b1_ref, 0), (b2_ref, 16)):
        for part in range(2):
            at = first + 8 * part
            for quad in range(2):
                parts = [rows[4 * quad + j][at : at + 8] for j in range(4)]
                for t, joined in enumerate(join_lanes(parts)):
                    lane = 384 * quad + 128 * t
                    out_ref[part : part + 1, lane : lane + 128] = joined[0:1]


def exchange(value):
    return lax.all_to_all(value, "lat", split_axis=0, concat_axis=0, tiled=True)


def on_device(fields, cotangent, w_first, b_first, w_second, b_second):
    block = (lax.axis_index("lat") // GROUPS).astype(jnp.int32).reshape(1)
    lon_fwd = jnp.asarray(LON_FWD, BF)
    lon_inv = jnp.asarray(LON_INV, BF)
    lon_fwd_t = jnp.asarray(LON_FWD.T, BF)
    lon_inv_t = jnp.asarray(LON_INV.T, BF)
    lat = jnp.asarray(LAT, BF)

    spectra = exchange(to_spectra(fields, cotangent, lon_fwd_t, lon_inv_t))
    kept, grads = block_call(
        gradient_kernel,
        "spectral_grads",
        block,
        (spectra, lat, w_first, b_first, w_second),
        ("", "", "weight", "", "weight"),
        [jax.ShapeDtypeStruct((2,) + WIDE, BF), jax.ShapeDtypeStruct((CHUNKS, CHUNK_ROWS, 128), BF)],
        [FORM, FORM, BAND_ROWS, BAND_ROWS, pltpu.VMEM(WIDE, BF), pltpu.VMEM(WIDE, BF)]
        + [pltpu.VMEM((CHUNKS * CHUNK_ROWS, 128), F32)],
    )
    dp_size = lax.axis_size("dp")
    if dp_size == CHUNKS:
        shares = lax.all_to_all(grads, "dp", 0, 0, tiled=True)
    else:
        shares = grads
    send = block_call(
        return_kernel,
        "spectral_return",
        block,
        (kept, lat, w_first, w_second, b_second),
        ("", "", "weight", "weight", ""),
        [jax.ShapeDtypeStruct((BANDS, 2 * PACK, 128), BF)],
        [FORM, FORM, BAND_ROWS, BAND_ROWS],
    )[0]
    share = spectral_call(
        share_kernel,
        "grad_share",
        (shares,),
        [jax.ShapeDtypeStruct((BANDS, CHUNK_ROWS, 128), BF)],
        [],
    )[0]
    banded = exchange(share)
    send, banded = lax.optimization_barrier((send, banded))
    returned = exchange(send)
    blocks = spectral_call(
        group_sum_kernel,
        "grad_groups",
        (banded,),
        [jax.ShapeDtypeStruct((NB, CHUNK_ROWS, 128), BF)],
        [],
    )[0]
    every = lax.all_gather(blocks, "dp", axis=0, tiled=False)
    if dp_size != CHUNKS:
        every = jnp.broadcast_to(every, (CHUNKS, NB, CHUNK_ROWS, 128))
    grad_w = jax.ShapeDtypeStruct((2, NB, BS, BS), F32)
    grad_b = jax.ShapeDtypeStruct((2, C), F32)
    g_w1, g_b1, g_w2, g_b2 = spectral_call(
        grads_kernel, "grad_out", (every,), [grad_w, grad_b, grad_w, grad_b], []
    )
    result, back_fields = from_spectra(returned, fields, cotangent, lon_fwd, lon_inv)
    return (result, back_fields, g_w1, g_b1, g_w2, g_b2)


def solution(mesh):
    placed = (P("dp", "lat", None, None), P("dp", "lat", None, None), P(), P(), P(), P())
    return jax.shard_map(
        on_device,
        mesh=mesh,
        in_specs=placed,
        out_specs=(P("dp", "lat", None, None), P("dp", "lat", None, None), P(), P(), P(), P()),
        check_vma=False,
    )
```

```python
import math

import jax
import jax.numpy as jnp
import numpy as np
from jax import lax
from jax.experimental import pallas as pl
from jax.experimental.pallas import tpu as pltpu
from jax.sharding import PartitionSpec as P

C = 768
NB = 8
BS = 96
H = 96
W = 180
KX = 64
SAMPLES = 16
EPSILON = 1e-06

BANDS = 32
GROUPS = 4
MODES = KX // GROUPS
ROWS = H // BANDS
WPAD = 192
PACK = 72
CHUNKS = 16
CHUNK_ROWS = 24
BF = jnp.bfloat16
F32 = jnp.float32
VMEM_LIMIT = 10 * 1024 * 1024


def tables():
    w_index = np.arange(W)[:, None]
    k_index = np.arange(KX)[None, :]
    lon = (2.0 * math.pi / W * (w_index * k_index % W)).astype(np.float64)
    fwd = np.stack([np.cos(lon), -np.sin(lon)], axis=1) / math.sqrt(W)
    weight = np.where(k_index == 0, 1.0, 2.0)[:, None, :]
    inv = fwd * weight
    def order(table):
        grouped = table.reshape(W, 2, GROUPS, MODES).transpose(0, 2, 1, 3).reshape(W, 2 * KX)
        padded = np.zeros((WPAD, 2 * KX))
        padded[:W] = grouped
        return padded

    h_index = np.arange(H)
    lat = 2.0 * math.pi / H * (h_index[:, None] * h_index[None, :] % H)
    cosine = np.cos(lat) / math.sqrt(H)
    sine = np.sin(lat) / math.sqrt(H)
    full = np.stack(
        [np.stack([cosine, sine], axis=2), np.stack([-sine, cosine], axis=2)], axis=0
    ).reshape(2 * H, 2 * H)
    return order(fwd), order(inv), full


LON_FWD, LON_INV, LAT = tables()


def lanes(shape):
    return lax.broadcasted_iota(jnp.int32, shape, 1)


def roll(value, shift):
    return pltpu.roll(value, shift % 128, 1)


def pack_tile(tile):
    lane = lanes((24, 128))
    tail = tile[72:96]
    return [
        jnp.where(lane < 96, tile[24 * i : 24 * i + 24], roll(tail, 96 - 32 * i))
        for i in range(3)
    ]


def unpack_tail(pieces):
    lane = lanes((24, 128))
    return jnp.where(
        lane < 32,
        roll(pieces[0], 32),
        jnp.where(lane < 64, roll(pieces[1], 64), roll(pieces[2], 96)),
    )


def block_lanes(value, block):
    start = BS * block
    first, shift = start // 128, start % 128
    head = value[:, 128 * first : 128 * first + 128]
    if shift == 0:
        return head
    head = roll(head, 128 - shift)
    if shift + BS <= 128:
        return head
    after = roll(value[:, 128 * first + 128 : 128 * first + 256], 128 - shift)
    return jnp.where(lanes(head.shape) < 128 - shift, head, after)


def join_lanes(parts):
    lane = lanes(parts[0].shape)
    return [
        jnp.where(lane < 96, parts[0], roll(parts[1], 96)),
        jnp.where(lane < 64, roll(parts[1], 96), roll(parts[2], 64)),
        jnp.where(lane < 32, roll(parts[2], 64), roll(parts[3], 32)),
    ]


ROW_CHUNKS = [(start, min(32, W - start)) for start in range(0, W, 32)]


def normalize(values):
    mean = jnp.sum(values, axis=-1, keepdims=True) * (1.0 / C)
    centered = values - mean
    spread = jnp.sum(centered * centered, axis=-1, keepdims=True) * (1.0 / C)
    scale = 1.0 / jnp.sqrt(spread + EPSILON)
    return centered * scale, scale


def send_packed(acc_ref, out_ref, first):
    for block in range(NB):
        rows = [block_lanes(acc_ref[r], block) for r in range(ROWS)]
        for group in range(GROUPS):
            tile = jnp.concatenate(
                [row[32 * group : 32 * group + 32] for row in rows], axis=0
            )
            pieces = pack_tile(tile)
            out_ref[block * GROUPS + group, first : first + PACK] = jnp.concatenate(
                pieces, axis=0
            ).astype(BF)


def spectra_kernel(
    x_ref, g_ref, fwd_ref, inv_ref, out_ref,
    x_rows, g_rows, fwd_table, inv_table, padded_ref, acc_ref, sems,
):
    copies = [pltpu.make_async_copy(x_ref.at[0, 0], x_rows.at[0], sems.at[0])]
    copies += [pltpu.make_async_copy(fwd_ref, fwd_table, sems.at[1])]
    copies += [
        pltpu.make_async_copy(x_ref.at[0, r], x_rows.at[r], sems.at[1 + r])
        for r in range(1, ROWS)
    ]
    copies += [pltpu.make_async_copy(inv_ref, inv_table, sems.at[1 + ROWS])]
    copies += [
        pltpu.make_async_copy(g_ref.at[0, r], g_rows.at[r], sems.at[2 + ROWS + r])
        for r in range(ROWS)
    ]
    for copy in copies:
        copy.start()
    padded_ref[W - 20 :] = jnp.zeros((WPAD - W + 20, C), BF)
    for r in range(ROWS):
        copies[0 if r == 0 else 1 + r].wait()
        for start, size in ROW_CHUNKS:
            values = x_rows[r, start : start + size].astype(F32)
            padded_ref[start : start + size] = normalize(values)[0].astype(BF)
        if r == 0:
            copies[1].wait()
        acc_ref[r] = jnp.dot(fwd_table[...], padded_ref[...], preferred_element_type=F32)
    send_packed(acc_ref, out_ref, 0)
    copies[1 + ROWS].wait()
    for r in range(ROWS):
        copies[2 + ROWS + r].wait()
        padded_ref[0:W] = g_rows[r]
        acc_ref[r] = jnp.dot(inv_table[...], padded_ref[...], preferred_element_type=F32)
    send_packed(acc_ref, out_ref, PACK)


def to_spectra(fields, cotangent, forward, inverse):
    held = pl.BlockSpec(memory_space=pltpu.HBM)
    return pl.pallas_call(
        spectra_kernel,
        name="to_spectra",
        in_specs=[held, held, held, held],
        out_specs=pl.BlockSpec(memory_space=pltpu.VMEM),
        out_shape=jax.ShapeDtypeStruct((BANDS, 2 * PACK, 128), BF),
        scratch_shapes=[
            pltpu.VMEM((ROWS, W, C), BF),
            pltpu.VMEM((ROWS, W, C), BF),
            pltpu.VMEM((2 * KX, WPAD), BF),
            pltpu.VMEM((2 * KX, WPAD), BF),
            pltpu.VMEM((WPAD, C), BF),
            pltpu.VMEM((ROWS, 2 * KX, C), F32),
            pltpu.SemaphoreType.DMA((2 + 2 * ROWS,)),
        ],
        compiler_params=pltpu.CompilerParams(vmem_limit_bytes=VMEM_LIMIT),
        cost_estimate=pl.CostEstimate(
            flops=4 * ROWS * W * 2 * KX * C, bytes_accessed=3000000, transcendentals=0
        ),
    )(*[pltpu.with_memory_space_constraint(a, pltpu.HBM) for a in (fields, cotangent, forward, inverse)])


TILE_ROWS = 2 * ROWS * MODES


def unpack_bands(recv_ref, first, rows_ref):
    def one(s, carry):
        pieces = [
            recv_ref[s, first + 24 * i : first + 24 * i + 24, :].astype(F32)
            for i in range(3)
        ]
        base = pl.multiple_of(s * TILE_ROWS, TILE_ROWS)
        for i in range(3):
            rows_ref[pl.ds(base + 24 * i, 24), :] = pieces[i]
        rows_ref[pl.ds(base + 72, 24), :] = unpack_tail(pieces)
        return carry

    lax.fori_loop(0, BANDS, one, 0, unroll=4)


def pack_bands(rows_ref, back_rows_ref, early_ref, late_ref):
    def one(s, carry):
        base = pl.multiple_of(s * TILE_ROWS, TILE_ROWS)
        pieces = pack_tile(rows_ref[pl.ds(base, TILE_ROWS), :])
        early_ref[s, 0:48] = jnp.concatenate(pieces[:2], axis=0).astype(BF)
        back = pack_tile(back_rows_ref[pl.ds(base, TILE_ROWS), :])
        late_ref[s] = jnp.concatenate(pieces[2:] + back, axis=0).astype(BF)
        return carry

    lax.fori_loop(0, BANDS, one, 0, unroll=4)


def mode_rows(rows_ref, lat, pair):
    columns = jnp.concatenate(
        [
            rows_ref[pl.ds(2 * pair + j, 2 * H, stride=MODES), :].astype(BF)
            for j in range(2)
        ],
        axis=1,
    )
    done = jnp.dot(lat, columns, preferred_element_type=F32).astype(BF)
    return jnp.concatenate(
        [
            jnp.concatenate(
                [done[0:H, 128 * j : 128 * j + 128], done[H : 2 * H, 128 * j : 128 * j + 128]],
                axis=1,
            )
            for j in range(2)
        ],
        axis=0,
    )


def store_rows(rows_ref, lat, pair, modes):
    columns = jnp.concatenate(
        [
            jnp.concatenate(
                [modes[H * j : H * j + H, 0:128], modes[H * j : H * j + H, 128:256]], axis=0
            )
            for j in range(2)
        ],
        axis=1,
    )
    done = lax.dot_general(
        lat, columns, (((0,), (0,)), ((), ())), preferred_element_type=F32
    )
    for j in range(2):
        rows_ref[pl.ds(2 * pair + j, 2 * H, stride=MODES), :] = done[:, 128 * j : 128 * j + 128]


PAIR_ROWS = 2 * H
PAIRS = MODES // 2


def fill_weight(weight_ref, form_ref):
    form_ref[...] = jnp.zeros_like(form_ref)
    real = weight_ref[0, 0]
    imag = weight_ref[1, 0]
    form_ref[0:BS, 0:BS] = real
    form_ref[0:BS, 128 : 128 + BS] = imag
    form_ref[128 : 128 + BS, 0:BS] = -imag
    form_ref[128 : 128 + BS, 128 : 128 + BS] = real


def choose_bias(block, bias_ref):
    bias = bias_ref[...]
    chosen = block_lanes(bias, 0)
    for other in range(1, NB):
        chosen = jnp.where(block == other, block_lanes(bias, other), chosen)
    chosen = jnp.where(lanes(chosen.shape) < BS, chosen, 0.0)
    return jnp.concatenate([chosen[0:1], chosen[1:2]], axis=1)


NT = (((1,), (1,)), ((), ()))
TN = (((0,), (0,)), ((), ()))


def gradient_kernel(
    block_ref, recv_ref, lat_ref, first_ref, bias_ref, second_ref,
    saved_ref, grad_ref,
    w1_ref, w2_ref, rows_ref, back_rows_ref, modes_ref, filtered_ref, sums_ref, kept_ref, sem,
):
    fill_weight(first_ref, w1_ref)
    fill_weight(second_ref, w2_ref)
    bias = choose_bias(block_ref[0], bias_ref)
    unpack_bands(recv_ref, 0, rows_ref)
    unpack_bands(recv_ref, PACK, back_rows_ref)
    lat = lat_ref[...]
    w1 = w1_ref[...]
    w2 = w2_ref[...]
    for pair in range(PAIRS):
        span = slice(PAIR_ROWS * pair, PAIR_ROWS * pair + PAIR_ROWS)
        modes = mode_rows(rows_ref, lat, pair)
        modes_ref[span] = modes
        pre = jnp.dot(modes, w1, preferred_element_type=F32) + bias
        cdf = 0.5 + 0.5 * lax.erf(pre * math.sqrt(0.5))
        kept_ref[0, span] = (pre * cdf).astype(BF)
        slope = cdf + pre * (jnp.exp(-0.5 * pre * pre) * (1.0 / math.sqrt(2.0 * math.pi)))
        back_filtered = mode_rows(back_rows_ref, lat, pair)
        filtered_ref[span] = back_filtered
        back_hidden = lax.dot_general(back_filtered, w2, NT, preferred_element_type=F32)
        kept_ref[1, span] = (back_hidden * slope).astype(BF)
    save = pltpu.make_async_copy(kept_ref, saved_ref, sem)
    save.start()
    ones = jnp.ones((8, MODES * H), BF)
    row = 0
    bias_rows = []
    for left_ref, right_ref in ((modes_ref, kept_ref.at[1]), (kept_ref.at[0], filtered_ref)):
        right = right_ref[...]
        gathered = lax.dot_general(left_ref[...], right, TN, preferred_element_type=F32)
        real = gathered[0:BS, 0:128] + gathered[128 : 128 + BS, 128:256]
        imag = gathered[0:BS, 128:256] - gathered[128 : 128 + BS, 0:128]
        for part in (real, imag):
            for piece in pack_tile(part):
                sums_ref[row : row + 24] = piece
                row += 24
        bias = jnp.dot(ones, right, preferred_element_type=F32)
        bias_rows += [bias[:, 0:128], bias[:, 128:256]]
    for value in bias_rows:
        sums_ref[row : row + 8] = value
        row += 8
    sums_ref[row:] = jnp.zeros((CHUNKS * CHUNK_ROWS - row, 128), F32)
    for chunk in range(CHUNKS):
        grad_ref[chunk] = sums_ref[CHUNK_ROWS * chunk : CHUNK_ROWS * chunk + CHUNK_ROWS].astype(
            BF
        )
    save.wait()


def return_kernel(
    block_ref, kept_ref, lat_ref, first_ref, second_ref, bias_ref,
    early_ref, late_ref,
    w1_ref, w2_ref, rows_ref, back_rows_ref,
):
    fill_weight(first_ref, w1_ref)
    fill_weight(second_ref, w2_ref)
    bias = choose_bias(block_ref[0], bias_ref)
    lat = lat_ref[...]
    w1 = w1_ref[...]
    w2 = w2_ref[...]
    for pair in range(PAIRS):
        span = slice(PAIR_ROWS * pair, PAIR_ROWS * pair + PAIR_ROWS)
        filtered = jnp.dot(kept_ref[0, span], w2, preferred_element_type=F32) + bias
        store_rows(rows_ref, lat, pair, filtered.astype(BF))
        back_modes = lax.dot_general(kept_ref[1, span], w1, NT, preferred_element_type=F32)
        store_rows(back_rows_ref, lat, pair, back_modes.astype(BF))
    pack_bands(rows_ref, back_rows_ref, early_ref, late_ref)


PAIR_ROWS = 2 * H
PAIRS = MODES // 2
WIDE = (MODES * H, 256)
FORM = pltpu.VMEM((256, 256), BF)
BAND_ROWS = pltpu.VMEM((2 * H * MODES, 128), F32)


def block_call(kernel, name, block, operands, specs, outs, scratch):
    return pl.pallas_call(
        kernel,
        name=name,
        grid_spec=pltpu.PrefetchScalarGridSpec(
            num_scalar_prefetch=1,
            grid=(1,),
            in_specs=[
                pl.BlockSpec((2, 1, BS, BS), lambda i, n: (0, n[0], 0, 0))
                if spec == "weight"
                else pl.BlockSpec(operand.shape, lambda i, n, d=operand.ndim: (0,) * d)
                for operand, spec in zip(operands, specs)
            ],
            out_specs=[
                pl.BlockSpec(memory_space=pltpu.HBM)
                if out.shape == (2,) + WIDE
                else pl.BlockSpec(out.shape, lambda i, n, d=len(out.shape): (0,) * d)
                for out in outs
            ],
            scratch_shapes=scratch,
        ),
        out_shape=[
            pltpu.HBM(out.shape, out.dtype) if out.shape == (2,) + WIDE else out for out in outs
        ],
        compiler_params=pltpu.CompilerParams(vmem_limit_bytes=14 * 1024 * 1024),
        cost_estimate=pl.CostEstimate(
            flops=1000000000, bytes_accessed=6000000, transcendentals=800000
        ),
    )(block, *operands)


def receive(parts, rows_ref):
    for group in range(GROUPS):
        for quad in range(2):
            tiles = []
            for block in range(4):
                band = (4 * quad + block) * GROUPS + group
                pieces = [ref[band, at : at + 24, :].astype(F32) for ref, at in parts]
                tiles.append(jnp.concatenate(pieces + [unpack_tail(pieces)], axis=0))
            for t, joined in enumerate(join_lanes(tiles)):
                for r in range(ROWS):
                    rows_ref[
                        r,
                        32 * group : 32 * group + 32,
                        384 * quad + 128 * t : 384 * quad + 128 * t + 128,
                    ] = joined[32 * r : 32 * r + 32].astype(BF)


def output_kernel(
    early_ref, late_ref, x_ref, g_ref, fwd_ref, inv_ref, out_ref, grad_ref,
    rows_ref, back_rows_ref, mixed_ref, back_ref,
):
    r = pl.program_id(0)

    @pl.when(r == 0)
    def _():
        receive(((early_ref, 0), (early_ref, 24), (late_ref, 0)), rows_ref)
        receive(((late_ref, 24), (late_ref, 48), (late_ref, 72)), back_rows_ref)

    mixed_ref[...] = jnp.dot(inv_ref[...], rows_ref[r], preferred_element_type=F32)
    back_ref[...] = jnp.dot(fwd_ref[...], back_rows_ref[r], preferred_element_type=F32)
    for start, size in ROW_CHUNKS:
        span = slice(start, start + size)
        values = x_ref[0, 0, span].astype(F32)
        normed, scale = normalize(values)
        out_ref[0, 0, span] = (values + normed + mixed_ref[span]).astype(BF)
        upstream = g_ref[0, 0, span].astype(F32)
        back = upstream + back_ref[span]
        mean = jnp.sum(back, axis=-1, keepdims=True) * (1.0 / C)
        along = jnp.sum(back * normed, axis=-1, keepdims=True) * (1.0 / C)
        grad_ref[0, 0, span] = (upstream + scale * (back - mean - normed * along)).astype(BF)


def from_spectra(early, late, fields, cotangent, forward, inverse):
    token_spec = pl.BlockSpec((1, 1, W, C), lambda r: (0, r, 0, 0))
    table_spec = pl.BlockSpec((WPAD, 2 * KX), lambda r: (0, 0))
    token = jax.ShapeDtypeStruct((1, ROWS, W, C), BF)
    return pl.pallas_call(
        output_kernel,
        name="from_spectra",
        grid=(ROWS,),
        in_specs=[
            pl.BlockSpec((BANDS, PACK, 128), lambda r: (0, 0, 0)),
            pl.BlockSpec((BANDS, 96, 128), lambda r: (0, 0, 0)),
            token_spec,
            token_spec,
            table_spec,
            table_spec,
        ],
        out_specs=[token_spec, token_spec],
        out_shape=[token, token],
        scratch_shapes=[
            pltpu.VMEM((ROWS, 2 * KX, C), BF),
            pltpu.VMEM((ROWS, 2 * KX, C), BF),
            pltpu.VMEM((WPAD, C), F32),
            pltpu.VMEM((WPAD, C), F32),
        ],
        compiler_params=pltpu.CompilerParams(vmem_limit_bytes=VMEM_LIMIT),
        cost_estimate=pl.CostEstimate(
            flops=4 * ROWS * W * 2 * KX * C, bytes_accessed=5000000, transcendentals=0
        ),
    )(early, late, fields, cotangent, forward, inverse)


def whole(shape):
    return pl.BlockSpec(shape, lambda: (0,) * len(shape))


def spectral_call(kernel, name, operands, outs, scratch):
    return pl.pallas_call(
        kernel,
        name=name,
        in_specs=[whole(operand.shape) for operand in operands],
        out_specs=[whole(out.shape) for out in outs],
        out_shape=outs,
        scratch_shapes=scratch,
        compiler_params=pltpu.CompilerParams(vmem_limit_bytes=VMEM_LIMIT),
        cost_estimate=pl.CostEstimate(
            flops=1000000, bytes_accessed=1000000, transcendentals=0
        ),
    )(*operands)


def share_kernel(recv_ref, held_ref, out_ref):
    total = recv_ref[0].astype(F32)
    for i in range(1, recv_ref.shape[0]):
        total = total + recv_ref[i].astype(F32)
    share = total.astype(BF)
    for band in range(BANDS):
        out_ref[band] = share


def add_share(shares, held):
    return pl.pallas_call(
        share_kernel,
        name="grad_share",
        grid=(1,),
        in_specs=[
            pl.BlockSpec(shares.shape, lambda i: (0, 0, 0)),
            pl.BlockSpec(memory_space=pl.ANY),
        ],
        out_specs=pl.BlockSpec((BANDS, CHUNK_ROWS, 128), lambda i: (0, 2, 0)),
        out_shape=jax.ShapeDtypeStruct(held.shape, BF),
        input_output_aliases={1: 0},
        compiler_params=pltpu.CompilerParams(vmem_limit_bytes=VMEM_LIMIT),
    )(shares, held)


def group_sum_kernel(recv_ref, out_ref):
    for block in range(NB):
        total = recv_ref[block * GROUPS].astype(F32)
        for group in range(1, GROUPS):
            total = total + recv_ref[block * GROUPS + group].astype(F32)
        out_ref[block] = total.astype(BF)


def group_sums(message):
    return pl.pallas_call(
        group_sum_kernel,
        name="grad_groups",
        grid=(1,),
        in_specs=[pl.BlockSpec((BANDS, CHUNK_ROWS, 128), lambda i: (0, 2, 0))],
        out_specs=pl.BlockSpec((NB, CHUNK_ROWS, 128), lambda i: (0, 0, 0)),
        out_shape=jax.ShapeDtypeStruct((NB, CHUNK_ROWS, 128), BF),
        compiler_params=pltpu.CompilerParams(vmem_limit_bytes=VMEM_LIMIT),
    )(message)


GRAD_SCALE = 1.0 / (SAMPLES * H)


def grads_kernel(recv_ref, w1_ref, b1_ref, w2_ref, b2_ref):
    for block in range(NB):
        chunk = 0
        for out_ref in (w1_ref, w2_ref):
            for part in range(2):
                pieces = [
                    recv_ref[chunk + i, block].astype(F32) * GRAD_SCALE for i in range(3)
                ]
                chunk += 3
                for i in range(3):
                    out_ref[part, block, 24 * i : 24 * i + 24, :] = pieces[i][:, :BS]
                out_ref[part, block, 72:96, :] = unpack_tail(pieces)[:, :BS]
    rows = [
        jnp.concatenate([recv_ref[12, block], recv_ref[13, block]], axis=0).astype(F32)
        * GRAD_SCALE
        for block in range(NB)
    ]
    for out_ref, first in ((b1_ref, 0), (b2_ref, 16)):
        for part in range(2):
            at = first + 8 * part
            for quad in range(2):
                parts = [rows[4 * quad + j][at : at + 8] for j in range(4)]
                for t, joined in enumerate(join_lanes(parts)):
                    lane = 384 * quad + 128 * t
                    out_ref[part : part + 1, lane : lane + 128] = joined[0:1]


def exchange(value):
    return lax.all_to_all(value, "lat", split_axis=0, concat_axis=0, tiled=True)


def on_device(fields, cotangent, w_first, b_first, w_second, b_second):
    block = (lax.axis_index("lat") // GROUPS).astype(jnp.int32).reshape(1)
    lon_fwd = jnp.asarray(LON_FWD, BF)
    lon_inv = jnp.asarray(LON_INV, BF)
    lon_fwd_t = jnp.asarray(LON_FWD.T, BF)
    lon_inv_t = jnp.asarray(LON_INV.T, BF)
    lat = jnp.asarray(LAT, BF)

    spectra = exchange(to_spectra(fields, cotangent, lon_fwd_t, lon_inv_t))
    kept, grads = block_call(
        gradient_kernel,
        "spectral_grads",
        block,
        (spectra, lat, w_first, b_first, w_second),
        ("", "", "weight", "", "weight"),
        [jax.ShapeDtypeStruct((2,) + WIDE, BF), jax.ShapeDtypeStruct((CHUNKS, CHUNK_ROWS, 128), BF)],
        [FORM, FORM, BAND_ROWS, BAND_ROWS, pltpu.VMEM(WIDE, BF), pltpu.VMEM(WIDE, BF)]
        + [pltpu.VMEM((CHUNKS * CHUNK_ROWS, 128), F32), pltpu.VMEM((2,) + WIDE, BF)]
        + [pltpu.SemaphoreType.DMA],
    )
    kept = pltpu.with_memory_space_constraint(kept, pltpu.HBM)
    dp_size = lax.axis_size("dp")
    if dp_size == CHUNKS:
        shares = lax.all_to_all(grads, "dp", 0, 0, tiled=True)
    else:
        shares = grads
    early, late = block_call(
        return_kernel,
        "spectral_return",
        block,
        (kept, lat, w_first, w_second, b_second),
        ("", "", "weight", "weight", ""),
        [
            jax.ShapeDtypeStruct((BANDS, PACK, 128), BF),
            jax.ShapeDtypeStruct((BANDS, 96, 128), BF),
        ],
        [FORM, FORM, BAND_ROWS, BAND_ROWS],
    )
    early = exchange(add_share(shares, early))
    late, early = lax.optimization_barrier((late, early))
    late = exchange(late)
    blocks = group_sums(early)
    every = lax.all_gather(blocks, "dp", axis=0, tiled=False)
    if dp_size != CHUNKS:
        every = jnp.broadcast_to(every, (CHUNKS, NB, CHUNK_ROWS, 128))
    grad_w = jax.ShapeDtypeStruct((2, NB, BS, BS), F32)
    grad_b = jax.ShapeDtypeStruct((2, C), F32)
    g_w1, g_b1, g_w2, g_b2 = spectral_call(
        grads_kernel, "grad_out", (every,), [grad_w, grad_b, grad_w, grad_b], []
    )
    result, back_fields = from_spectra(early, late, fields, cotangent, lon_fwd, lon_inv)
    return (result, back_fields, g_w1, g_b1, g_w2, g_b2)


def solution(mesh):
    placed = (P("dp", "lat", None, None), P("dp", "lat", None, None), P(), P(), P(), P())
    return jax.shard_map(
        on_device,
        mesh=mesh,
        in_specs=placed,
        out_specs=(P("dp", "lat", None, None), P("dp", "lat", None, None), P(), P(), P(), P()),
        check_vma=False,
    )
```

```python
import math

import jax
import jax.numpy as jnp
import numpy as np
from jax import lax
from jax.experimental import pallas as pl
from jax.experimental.pallas import tpu as pltpu
from jax.sharding import PartitionSpec as P

C = 768
NB = 8
BS = 96
H = 96
W = 180
KX = 64
SAMPLES = 16
EPSILON = 1e-06

BANDS = 32
GROUPS = 4
MODES = KX // GROUPS
ROWS = H // BANDS
WPAD = 192
PACK = 72
CHUNKS = 16
CHUNK_ROWS = 24
BF = jnp.bfloat16
F32 = jnp.float32
VMEM_LIMIT = 10 * 1024 * 1024


def tables():
    w_index = np.arange(W)[:, None]
    k_index = np.arange(KX)[None, :]
    lon = (2.0 * math.pi / W * (w_index * k_index % W)).astype(np.float64)
    fwd = np.stack([np.cos(lon), -np.sin(lon)], axis=1) / math.sqrt(W)
    weight = np.where(k_index == 0, 1.0, 2.0)[:, None, :]
    inv = fwd * weight
    def order(table):
        grouped = table.reshape(W, 2, GROUPS, MODES).transpose(0, 2, 1, 3).reshape(W, 2 * KX)
        padded = np.zeros((WPAD, 2 * KX))
        padded[:W] = grouped
        return padded

    h_index = np.arange(H)
    lat = 2.0 * math.pi / H * (h_index[:, None] * h_index[None, :] % H)
    cosine = np.cos(lat) / math.sqrt(H)
    sine = np.sin(lat) / math.sqrt(H)
    full = np.stack(
        [np.stack([cosine, sine], axis=2), np.stack([-sine, cosine], axis=2)], axis=0
    ).reshape(2 * H, 2 * H)
    return order(fwd), order(inv), full


LON_FWD, LON_INV, LAT = tables()


def lanes(shape):
    return lax.broadcasted_iota(jnp.int32, shape, 1)


def roll(value, shift):
    return pltpu.roll(value, shift % 128, 1)


def pack_tile(tile):
    lane = lanes((24, 128))
    tail = tile[72:96]
    return [
        jnp.where(lane < 96, tile[24 * i : 24 * i + 24], roll(tail, 96 - 32 * i))
        for i in range(3)
    ]


def unpack_tail(pieces):
    lane = lanes((24, 128))
    return jnp.where(
        lane < 32,
        roll(pieces[0], 32),
        jnp.where(lane < 64, roll(pieces[1], 64), roll(pieces[2], 96)),
    )


def block_lanes(value, block):
    start = BS * block
    first, shift = start // 128, start % 128
    head = value[:, 128 * first : 128 * first + 128]
    if shift == 0:
        return head
    head = roll(head, 128 - shift)
    if shift + BS <= 128:
        return head
    after = roll(value[:, 128 * first + 128 : 128 * first + 256], 128 - shift)
    return jnp.where(lanes(head.shape) < 128 - shift, head, after)


def join_lanes(parts):
    lane = lanes(parts[0].shape)
    return [
        jnp.where(lane < 96, parts[0], roll(parts[1], 96)),
        jnp.where(lane < 64, roll(parts[1], 96), roll(parts[2], 64)),
        jnp.where(lane < 32, roll(parts[2], 64), roll(parts[3], 32)),
    ]


ROW_CHUNKS = [(start, min(32, W - start)) for start in range(0, W, 32)]


def normalize(values):
    mean = jnp.sum(values, axis=-1, keepdims=True) * (1.0 / C)
    centered = values - mean
    spread = jnp.sum(centered * centered, axis=-1, keepdims=True) * (1.0 / C)
    scale = 1.0 / jnp.sqrt(spread + EPSILON)
    return centered * scale, mean, scale


def send_packed(acc_ref, out_ref):
    for block in range(NB):
        rows = [block_lanes(acc_ref[r], block) for r in range(ROWS)]
        for group in range(GROUPS):
            tile = jnp.concatenate(
                [row[32 * group : 32 * group + 32] for row in rows], axis=0
            )
            pieces = pack_tile(tile)
            out_ref[block * GROUPS + group] = jnp.concatenate(pieces, axis=0).astype(BF)


def spectra_kernel(
    x_ref, g_ref, fwd_ref, inv_ref, out_ref, moments_ref,
    x_rows, g_rows, fwd_table, inv_table, padded_ref, acc_ref, send_ref, kept_ref, sems, out_sems,
):
    copies = [pltpu.make_async_copy(x_ref.at[0, 0], x_rows.at[0], sems.at[0])]
    copies += [pltpu.make_async_copy(fwd_ref, fwd_table, sems.at[1])]
    copies += [
        pltpu.make_async_copy(x_ref.at[0, r], x_rows.at[r], sems.at[1 + r])
        for r in range(1, ROWS)
    ]
    copies += [pltpu.make_async_copy(inv_ref, inv_table, sems.at[1 + ROWS])]
    copies += [
        pltpu.make_async_copy(g_ref.at[0, r], g_rows.at[r], sems.at[2 + ROWS + r])
        for r in range(ROWS)
    ]
    for copy in copies:
        copy.start()
    padded_ref[W - 20 :] = jnp.zeros((WPAD - W + 20, C), BF)
    for r in range(ROWS):
        copies[0 if r == 0 else 1 + r].wait()
        for start, size in ROW_CHUNKS:
            values = x_rows[r, start : start + size].astype(F32)
            normed, mean, scale = normalize(values)
            padded_ref[start : start + size] = normed.astype(BF)
            kept_ref[r, start : start + size, 0:128] = jnp.broadcast_to(mean, (size, 128))
            kept_ref[r, start : start + size, 128:256] = jnp.broadcast_to(scale, (size, 128))
        if r == 0:
            copies[1].wait()
        acc_ref[r] = jnp.dot(fwd_table[...], padded_ref[...], preferred_element_type=F32)
    moments_out = pltpu.make_async_copy(kept_ref, moments_ref, out_sems.at[2])
    moments_out.start()
    send_packed(acc_ref, send_ref.at[0])
    fields_out = pltpu.make_async_copy(
        send_ref.at[0], out_ref.at[:, pl.ds(0, PACK), :], out_sems.at[0]
    )
    fields_out.start()
    copies[1 + ROWS].wait()
    for r in range(ROWS):
        copies[2 + ROWS + r].wait()
        padded_ref[0:W] = g_rows[r]
        acc_ref[r] = jnp.dot(inv_table[...], padded_ref[...], preferred_element_type=F32)
    send_packed(acc_ref, send_ref.at[1])
    back_out = pltpu.make_async_copy(
        send_ref.at[1], out_ref.at[:, pl.ds(PACK, PACK), :], out_sems.at[1]
    )
    back_out.start()
    moments_out.wait()
    fields_out.wait()
    back_out.wait()


def to_spectra(fields, cotangent, forward, inverse):
    held = pl.BlockSpec(memory_space=pltpu.HBM)
    return pl.pallas_call(
        spectra_kernel,
        name="to_spectra",
        in_specs=[held, held, held, held],
        out_specs=[held, held],
        out_shape=[
            pltpu.HBM((BANDS, 2 * PACK, 128), BF),
            pltpu.HBM((ROWS, W, 256), F32),
        ],
        scratch_shapes=[
            pltpu.VMEM((ROWS, W, C), BF),
            pltpu.VMEM((ROWS, W, C), BF),
            pltpu.VMEM((2 * KX, WPAD), BF),
            pltpu.VMEM((2 * KX, WPAD), BF),
            pltpu.VMEM((WPAD, C), BF),
            pltpu.VMEM((ROWS, 2 * KX, C), F32),
            pltpu.VMEM((2, BANDS, PACK, 128), BF),
            pltpu.VMEM((ROWS, W, 256), F32),
            pltpu.SemaphoreType.DMA((2 + 2 * ROWS,)),
            pltpu.SemaphoreType.DMA((3,)),
        ],
        compiler_params=pltpu.CompilerParams(vmem_limit_bytes=VMEM_LIMIT),
        cost_estimate=pl.CostEstimate(
            flops=4 * ROWS * W * 2 * KX * C, bytes_accessed=3000000, transcendentals=0
        ),
    )(*[pltpu.with_memory_space_constraint(a, pltpu.HBM) for a in (fields, cotangent, forward, inverse)])


TILE_ROWS = 2 * ROWS * MODES


def unpack_bands(recv_ref, first, rows_ref):
    def one(s, carry):
        pieces = [
            recv_ref[s, first + 24 * i : first + 24 * i + 24, :].astype(F32)
            for i in range(3)
        ]
        base = pl.multiple_of(s * TILE_ROWS, TILE_ROWS)
        for i in range(3):
            rows_ref[pl.ds(base + 24 * i, 24), :] = pieces[i]
        rows_ref[pl.ds(base + 72, 24), :] = unpack_tail(pieces)
        return carry

    lax.fori_loop(0, BANDS, one, 0, unroll=4)


def pack_bands(rows_ref, back_rows_ref, early_ref, late_ref, first):
    def one(s, carry):
        base = pl.multiple_of(s * TILE_ROWS, TILE_ROWS)
        pieces = pack_tile(rows_ref[pl.ds(base, TILE_ROWS), :])
        early_ref[s, 0:48] = jnp.concatenate(pieces[:2], axis=0).astype(BF)
        back = pack_tile(back_rows_ref[pl.ds(base, TILE_ROWS), :])
        late_ref[s] = jnp.concatenate(pieces[2:] + back, axis=0).astype(BF)
        return carry

    lax.fori_loop(first, first + BANDS // 4, one, 0, unroll=4)


def mode_rows(rows_ref, lat, pair):
    columns = jnp.concatenate(
        [
            rows_ref[pl.ds(2 * pair + j, 2 * H, stride=MODES), :].astype(BF)
            for j in range(2)
        ],
        axis=1,
    )
    done = jnp.dot(lat, columns, preferred_element_type=F32).astype(BF)
    return jnp.concatenate(
        [
            jnp.concatenate(
                [done[0:H, 128 * j : 128 * j + 128], done[H : 2 * H, 128 * j : 128 * j + 128]],
                axis=1,
            )
            for j in range(2)
        ],
        axis=0,
    )


def store_rows(rows_ref, lat, pair, modes):
    columns = jnp.concatenate(
        [
            jnp.concatenate(
                [modes[H * j : H * j + H, 0:128], modes[H * j : H * j + H, 128:256]], axis=0
            )
            for j in range(2)
        ],
        axis=1,
    )
    done = lax.dot_general(
        lat, columns, (((0,), (0,)), ((), ())), preferred_element_type=F32
    )
    for j in range(2):
        rows_ref[pl.ds(2 * pair + j, 2 * H, stride=MODES), :] = done[:, 128 * j : 128 * j + 128]


PAIR_ROWS = 2 * H
PAIRS = MODES // 2


def fill_weight(weight_ref, form_ref):
    form_ref[...] = jnp.zeros_like(form_ref)
    real = weight_ref[0, 0]
    imag = weight_ref[1, 0]
    form_ref[0:BS, 0:BS] = real
    form_ref[0:BS, 128 : 128 + BS] = imag
    form_ref[128 : 128 + BS, 0:BS] = -imag
    form_ref[128 : 128 + BS, 128 : 128 + BS] = real


def choose_bias(block, bias_ref):
    bias = bias_ref[...]
    chosen = block_lanes(bias, 0)
    for other in range(1, NB):
        chosen = jnp.where(block == other, block_lanes(bias, other), chosen)
    chosen = jnp.where(lanes(chosen.shape) < BS, chosen, 0.0)
    return jnp.concatenate([chosen[0:1], chosen[1:2]], axis=1)


NT = (((1,), (1,)), ((), ()))
TN = (((0,), (0,)), ((), ()))


def gradient_kernel(
    block_ref, recv_ref, lat_ref, first_ref, bias_ref, second_ref,
    saved_ref, grad_ref,
    w1_ref, w2_ref, rows_ref, back_rows_ref, modes_ref, filtered_ref, sums_ref, kept_ref, sems,
):
    fill_weight(first_ref, w1_ref)
    fill_weight(second_ref, w2_ref)
    bias = choose_bias(block_ref[0], bias_ref)
    unpack_bands(recv_ref, 0, rows_ref)
    unpack_bands(recv_ref, PACK, back_rows_ref)
    lat = lat_ref[...]
    w1 = w1_ref[...]
    w2 = w2_ref[...]
    saves = []
    for pair in range(PAIRS):
        span = slice(PAIR_ROWS * pair, PAIR_ROWS * pair + PAIR_ROWS)
        modes = mode_rows(rows_ref, lat, pair)
        modes_ref[span] = modes
        pre = jnp.dot(modes, w1, preferred_element_type=F32) + bias
        cdf = 0.5 + 0.5 * lax.erf(pre * math.sqrt(0.5))
        kept_ref[0, span] = (pre * cdf).astype(BF)
        slope = cdf + pre * (jnp.exp(-0.5 * pre * pre) * (1.0 / math.sqrt(2.0 * math.pi)))
        back_filtered = mode_rows(back_rows_ref, lat, pair)
        filtered_ref[span] = back_filtered
        back_hidden = lax.dot_general(back_filtered, w2, NT, preferred_element_type=F32)
        kept_ref[1, span] = (back_hidden * slope).astype(BF)
        pair_rows = pl.ds(PAIR_ROWS * pair, PAIR_ROWS)
        save = pltpu.make_async_copy(
            kept_ref.at[:, pair_rows, :], saved_ref.at[:, pair_rows, :], sems.at[pair]
        )
        save.start()
        saves.append(save)
    ones = jnp.ones((8, MODES * H), BF)
    row = 0
    bias_rows = []
    for left_ref, right_ref in ((modes_ref, kept_ref.at[1]), (kept_ref.at[0], filtered_ref)):
        right = right_ref[...]
        gathered = lax.dot_general(left_ref[...], right, TN, preferred_element_type=F32)
        real = gathered[0:BS, 0:128] + gathered[128 : 128 + BS, 128:256]
        imag = gathered[0:BS, 128:256] - gathered[128 : 128 + BS, 0:128]
        for part in (real, imag):
            for piece in pack_tile(part):
                sums_ref[row : row + 24] = piece
                row += 24
        bias = jnp.dot(ones, right, preferred_element_type=F32)
        bias_rows += [bias[:, 0:128], bias[:, 128:256]]
    for value in bias_rows:
        sums_ref[row : row + 8] = value
        row += 8
    sums_ref[row:] = jnp.zeros((CHUNKS * CHUNK_ROWS - row, 128), F32)
    for chunk in range(CHUNKS):
        grad_ref[chunk] = sums_ref[CHUNK_ROWS * chunk : CHUNK_ROWS * chunk + CHUNK_ROWS].astype(
            BF
        )
    for save in saves:
        save.wait()


def return_kernel(
    block_ref, saved_ref, lat_ref, first_ref, second_ref, bias_ref,
    early_ref, sent_ref,
    w1_ref, w2_ref, rows_ref, back_rows_ref, kept_ref, late_ref, sems, out_sems,
):
    fetches = []
    for pair in range(PAIRS):
        pair_rows = pl.ds(PAIR_ROWS * pair, PAIR_ROWS)
        fetch = pltpu.make_async_copy(
            saved_ref.at[:, pair_rows, :], kept_ref.at[:, pair_rows, :], sems.at[pair]
        )
        fetch.start()
        fetches.append(fetch)
    fill_weight(first_ref, w1_ref)
    fill_weight(second_ref, w2_ref)
    bias = choose_bias(block_ref[0], bias_ref)
    lat = lat_ref[...]
    w1 = w1_ref[...]
    w2 = w2_ref[...]
    for pair in range(PAIRS):
        span = slice(PAIR_ROWS * pair, PAIR_ROWS * pair + PAIR_ROWS)
        fetches[pair].wait()
        filtered = jnp.dot(kept_ref[0, span], w2, preferred_element_type=F32) + bias
        store_rows(rows_ref, lat, pair, filtered.astype(BF))
        back_modes = lax.dot_general(kept_ref[1, span], w1, NT, preferred_element_type=F32)
        store_rows(back_rows_ref, lat, pair, back_modes.astype(BF))
    leaving = []
    for part in range(4):
        pack_bands(rows_ref, back_rows_ref, early_ref, late_ref, part * (BANDS // 4))
        bands = pl.ds(part * (BANDS // 4), BANDS // 4)
        copy = pltpu.make_async_copy(
            late_ref.at[bands], sent_ref.at[bands], out_sems.at[part]
        )
        copy.start()
        leaving.append(copy)
    for copy in leaving:
        copy.wait()


PAIR_ROWS = 2 * H
PAIRS = MODES // 2
WIDE = (MODES * H, 256)
FORM = pltpu.VMEM((256, 256), BF)
BAND_ROWS = pltpu.VMEM((2 * H * MODES, 128), F32)


def block_call(kernel, name, block, operands, specs, outs, places, scratch):
    return pl.pallas_call(
        kernel,
        name=name,
        grid_spec=pltpu.PrefetchScalarGridSpec(
            num_scalar_prefetch=1,
            grid=(1,),
            in_specs=[
                pl.BlockSpec((2, 1, BS, BS), lambda i, n: (0, n[0], 0, 0))
                if spec == "weight"
                else pl.BlockSpec(memory_space=pltpu.HBM)
                if spec == "far"
                else pl.BlockSpec(memory_space=pltpu.VMEM)
                for operand, spec in zip(operands, specs)
            ],
            out_specs=[
                pl.BlockSpec(memory_space=pltpu.HBM if place == "far" else pltpu.VMEM)
                for place in places
            ],
            scratch_shapes=scratch,
        ),
        out_shape=[
            pltpu.HBM(out.shape, out.dtype) if place == "far" else out
            for out, place in zip(outs, places)
        ],
        compiler_params=pltpu.CompilerParams(vmem_limit_bytes=14 * 1024 * 1024),
        cost_estimate=pl.CostEstimate(
            flops=1000000000, bytes_accessed=6000000, transcendentals=800000
        ),
    )(block, *operands)


def receive(parts, rows_ref):
    for group in range(GROUPS):
        for quad in range(2):
            tiles = []
            for block in range(4):
                band = (4 * quad + block) * GROUPS + group
                pieces = [ref[band, at : at + 24, :].astype(F32) for ref, at in parts]
                tiles.append(
                    jnp.concatenate(pieces + [unpack_tail(pieces)], axis=0).astype(BF)
                )
            for t, joined in enumerate(join_lanes(tiles)):
                for r in range(ROWS):
                    rows_ref[
                        r,
                        32 * group : 32 * group + 32,
                        384 * quad + 128 * t : 384 * quad + 128 * t + 128,
                    ] = joined[32 * r : 32 * r + 32]


def output_kernel(
    early_ref, late_ref, x_ref, moments_ref, g_ref, fwd_ref, inv_ref,
    out_ref, grad_ref,
    rows_ref, back_rows_ref, mixed_ref, back_ref, held_ref, sem,
):
    r = pl.program_id(0)

    @pl.when(r == 0)
    def _():
        fetch = pltpu.make_async_copy(moments_ref, held_ref, sem)
        fetch.start()
        receive(((early_ref, 0), (early_ref, 24), (late_ref, 0)), rows_ref)
        receive(((late_ref, 24), (late_ref, 48), (late_ref, 72)), back_rows_ref)
        fetch.wait()

    mixed_ref[...] = jnp.dot(inv_ref[...], rows_ref[r], preferred_element_type=F32)
    back_ref[...] = jnp.dot(fwd_ref[...], back_rows_ref[r], preferred_element_type=F32)
    for start, size in ROW_CHUNKS:
        span = slice(start, start + size)
        values = x_ref[0, r, span].astype(F32)
        scale = held_ref[r, span, 128:256][:, 0:1]
        normed = (values - held_ref[r, span, 0:128][:, 0:1]) * scale
        out_ref[0, 0, span] = (values + normed + mixed_ref[span]).astype(BF)
        upstream = g_ref[0, r, span].astype(F32)
        back = upstream + back_ref[span]
        mean = jnp.sum(back, axis=-1, keepdims=True) * (1.0 / C)
        along = jnp.sum(back * normed, axis=-1, keepdims=True) * (1.0 / C)
        grad_ref[0, 0, span] = (upstream + scale * (back - mean - normed * along)).astype(BF)


def from_spectra(early, late, fields, moments, cotangent, forward, inverse):
    token_spec = pl.BlockSpec((1, 1, W, C), lambda r: (0, r, 0, 0))
    near = pl.BlockSpec(memory_space=pltpu.VMEM)
    token = jax.ShapeDtypeStruct((1, ROWS, W, C), BF)
    return pl.pallas_call(
        output_kernel,
        name="from_spectra",
        grid=(ROWS,),
        in_specs=[near] * 3 + [pl.BlockSpec(memory_space=pltpu.HBM)] + [near] * 3,
        out_specs=[token_spec, token_spec],
        out_shape=[token, token],
        scratch_shapes=[
            pltpu.VMEM((ROWS, 2 * KX, C), BF),
            pltpu.VMEM((ROWS, 2 * KX, C), BF),
            pltpu.VMEM((WPAD, C), F32),
            pltpu.VMEM((WPAD, C), F32),
            pltpu.VMEM((ROWS, W, 256), F32),
            pltpu.SemaphoreType.DMA,
        ],
        compiler_params=pltpu.CompilerParams(vmem_limit_bytes=VMEM_LIMIT),
        cost_estimate=pl.CostEstimate(
            flops=4 * ROWS * W * 2 * KX * C, bytes_accessed=5000000, transcendentals=0
        ),
    )(early, late, fields, moments, cotangent, forward, inverse)


def whole(shape):
    return pl.BlockSpec(shape, lambda: (0,) * len(shape))


def spectral_call(kernel, name, operands, outs, scratch):
    return pl.pallas_call(
        kernel,
        name=name,
        in_specs=[whole(operand.shape) for operand in operands],
        out_specs=[whole(out.shape) for out in outs],
        out_shape=outs,
        scratch_shapes=scratch,
        compiler_params=pltpu.CompilerParams(vmem_limit_bytes=VMEM_LIMIT),
        cost_estimate=pl.CostEstimate(
            flops=1000000, bytes_accessed=1000000, transcendentals=0
        ),
    )(*operands)


def share_kernel(recv_ref, held_ref, out_ref):
    total = recv_ref[0].astype(F32)
    for i in range(1, recv_ref.shape[0]):
        total = total + recv_ref[i].astype(F32)
    share = total.astype(BF)
    for band in range(BANDS):
        out_ref[band] = share


def add_share(shares, held):
    return pl.pallas_call(
        share_kernel,
        name="grad_share",
        grid=(1,),
        in_specs=[
            pl.BlockSpec(shares.shape, lambda i: (0, 0, 0)),
            pl.BlockSpec(memory_space=pl.ANY),
        ],
        out_specs=pl.BlockSpec((BANDS, CHUNK_ROWS, 128), lambda i: (0, 2, 0)),
        out_shape=jax.ShapeDtypeStruct(held.shape, BF),
        input_output_aliases={1: 0},
        compiler_params=pltpu.CompilerParams(vmem_limit_bytes=VMEM_LIMIT),
    )(shares, held)


def group_sum_kernel(recv_ref, out_ref):
    for block in range(NB):
        total = recv_ref[block * GROUPS].astype(F32)
        for group in range(1, GROUPS):
            total = total + recv_ref[block * GROUPS + group].astype(F32)
        out_ref[block] = total.astype(BF)


def group_sums(message):
    return pl.pallas_call(
        group_sum_kernel,
        name="grad_groups",
        grid=(1,),
        in_specs=[pl.BlockSpec((BANDS, CHUNK_ROWS, 128), lambda i: (0, 2, 0))],
        out_specs=pl.BlockSpec((NB, CHUNK_ROWS, 128), lambda i: (0, 0, 0)),
        out_shape=jax.ShapeDtypeStruct((NB, CHUNK_ROWS, 128), BF),
        compiler_params=pltpu.CompilerParams(vmem_limit_bytes=VMEM_LIMIT),
    )(message)


GRAD_SCALE = 1.0 / (SAMPLES * H)


def grads_kernel(recv_ref, w1_ref, b1_ref, w2_ref, b2_ref):
    for block in range(NB):
        chunk = 0
        for out_ref in (w1_ref, w2_ref):
            for part in range(2):
                pieces = [
                    recv_ref[chunk + i, block].astype(F32) * GRAD_SCALE for i in range(3)
                ]
                chunk += 3
                for i in range(3):
                    out_ref[part, block, 24 * i : 24 * i + 24, :] = pieces[i][:, :BS]
                out_ref[part, block, 72:96, :] = unpack_tail(pieces)[:, :BS]
    rows = [
        jnp.concatenate([recv_ref[12, block], recv_ref[13, block]], axis=0).astype(F32)
        * GRAD_SCALE
        for block in range(NB)
    ]
    for out_ref, first in ((b1_ref, 0), (b2_ref, 16)):
        for part in range(2):
            at = first + 8 * part
            for quad in range(2):
                parts = [rows[4 * quad + j][at : at + 8] for j in range(4)]
                for t, joined in enumerate(join_lanes(parts)):
                    lane = 384 * quad + 128 * t
                    out_ref[part : part + 1, lane : lane + 128] = joined[0:1]


def exchange(value):
    return lax.all_to_all(value, "lat", split_axis=0, concat_axis=0, tiled=True)


def on_device(fields, cotangent, w_first, b_first, w_second, b_second):
    block = (lax.axis_index("lat") // GROUPS).astype(jnp.int32).reshape(1)
    lon_fwd = jnp.asarray(LON_FWD, BF)
    lon_inv = jnp.asarray(LON_INV, BF)
    lon_fwd_t = jnp.asarray(LON_FWD.T, BF)
    lon_inv_t = jnp.asarray(LON_INV.T, BF)
    lat = jnp.asarray(LAT, BF)

    spectra, moments = to_spectra(fields, cotangent, lon_fwd_t, lon_inv_t)
    moments = pltpu.with_memory_space_constraint(moments, pltpu.HBM)
    spectra = exchange(spectra)
    kept, grads = block_call(
        gradient_kernel,
        "spectral_grads",
        block,
        (spectra, lat, w_first, b_first, w_second),
        ("", "", "weight", "", "weight"),
        [jax.ShapeDtypeStruct((2,) + WIDE, BF), jax.ShapeDtypeStruct((CHUNKS, CHUNK_ROWS, 128), BF)],
        ("far", "near"),
        [FORM, FORM, BAND_ROWS, BAND_ROWS, pltpu.VMEM(WIDE, BF), pltpu.VMEM(WIDE, BF)]
        + [pltpu.VMEM((CHUNKS * CHUNK_ROWS, 128), F32), pltpu.VMEM((2,) + WIDE, BF)]
        + [pltpu.SemaphoreType.DMA((PAIRS,))],
    )
    kept = pltpu.with_memory_space_constraint(kept, pltpu.HBM)
    dp_size = lax.axis_size("dp")
    if dp_size == CHUNKS:
        shares = lax.all_to_all(grads, "dp", 0, 0, tiled=True)
    else:
        shares = grads
    early, late = block_call(
        return_kernel,
        "spectral_return",
        block,
        (kept, lat, w_first, w_second, b_second),
        ("far", "", "weight", "weight", ""),
        [
            jax.ShapeDtypeStruct((BANDS, PACK, 128), BF),
            jax.ShapeDtypeStruct((BANDS, 96, 128), BF),
        ],
        ("near", "far"),
        [FORM, FORM, BAND_ROWS, BAND_ROWS, pltpu.VMEM((2,) + WIDE, BF)]
        + [pltpu.VMEM((BANDS, 96, 128), BF)]
        + [pltpu.SemaphoreType.DMA((PAIRS,)), pltpu.SemaphoreType.DMA((4,))],
    )
    early = exchange(add_share(shares, early))
    late, early = lax.optimization_barrier((late, early))
    late = exchange(late)
    blocks = group_sums(early)
    every = lax.all_gather(blocks, "dp", axis=0, tiled=False)
    if dp_size != CHUNKS:
        every = jnp.broadcast_to(every, (CHUNKS, NB, CHUNK_ROWS, 128))
    grad_w = jax.ShapeDtypeStruct((2, NB, BS, BS), F32)
    grad_b = jax.ShapeDtypeStruct((2, C), F32)
    g_w1, g_b1, g_w2, g_b2 = spectral_call(
        grads_kernel, "grad_out", (every,), [grad_w, grad_b, grad_w, grad_b], []
    )
    result, back_fields = from_spectra(
        early, late, fields, moments, cotangent, lon_fwd, lon_inv
    )
    return (result, back_fields, g_w1, g_b1, g_w2, g_b2)


def solution(mesh):
    placed = (P("dp", "lat", None, None), P("dp", "lat", None, None), P(), P(), P(), P())
    return jax.shard_map(
        on_device,
        mesh=mesh,
        in_specs=placed,
        out_specs=(P("dp", "lat", None, None), P("dp", "lat", None, None), P(), P(), P(), P()),
        check_vma=False,
    )
```

```python
import math

import jax
import jax.numpy as jnp
import numpy as np
from jax import lax
from jax.experimental import pallas as pl
from jax.experimental.pallas import tpu as pltpu
from jax.sharding import PartitionSpec as P

C = 768
NB = 8
BS = 96
H = 96
W = 180
KX = 64
SAMPLES = 16
EPSILON = 1e-06

BANDS = 32
GROUPS = 4
MODES = KX // GROUPS
ROWS = H // BANDS
WPAD = 192
PACK = 72
CHUNKS = 16
CHUNK_ROWS = 24
BF = jnp.bfloat16
F32 = jnp.float32
VMEM_LIMIT = 10 * 1024 * 1024


def tables():
    w_index = np.arange(W)[:, None]
    k_index = np.arange(KX)[None, :]
    lon = (2.0 * math.pi / W * (w_index * k_index % W)).astype(np.float64)
    fwd = np.stack([np.cos(lon), -np.sin(lon)], axis=1) / math.sqrt(W)
    weight = np.where(k_index == 0, 1.0, 2.0)[:, None, :]
    inv = fwd * weight
    def order(table):
        grouped = table.reshape(W, 2, GROUPS, MODES).transpose(0, 2, 1, 3).reshape(W, 2 * KX)
        padded = np.zeros((WPAD, 2 * KX))
        padded[:W] = grouped
        return padded

    h_index = np.arange(H)
    lat = 2.0 * math.pi / H * (h_index[:, None] * h_index[None, :] % H)
    cosine = np.cos(lat) / math.sqrt(H)
    sine = np.sin(lat) / math.sqrt(H)
    full = np.stack(
        [np.stack([cosine, sine], axis=2), np.stack([-sine, cosine], axis=2)], axis=0
    ).reshape(2 * H, 2 * H)
    return order(fwd), order(inv), full


LON_FWD, LON_INV, LAT = tables()


def lanes(shape):
    return lax.broadcasted_iota(jnp.int32, shape, 1)


def roll(value, shift):
    return pltpu.roll(value, shift % 128, 1)


def pack_tile(tile):
    lane = lanes((24, 128))
    tail = tile[72:96]
    return [
        jnp.where(lane < 96, tile[24 * i : 24 * i + 24], roll(tail, 96 - 32 * i))
        for i in range(3)
    ]


def unpack_tail(pieces):
    lane = lanes((24, 128))
    return jnp.where(
        lane < 32,
        roll(pieces[0], 32),
        jnp.where(lane < 64, roll(pieces[1], 64), roll(pieces[2], 96)),
    )


def block_lanes(value, block):
    start = BS * block
    first, shift = start // 128, start % 128
    head = value[:, 128 * first : 128 * first + 128]
    if shift == 0:
        return head
    head = roll(head, 128 - shift)
    if shift + BS <= 128:
        return head
    after = roll(value[:, 128 * first + 128 : 128 * first + 256], 128 - shift)
    return jnp.where(lanes(head.shape) < 128 - shift, head, after)


def join_lanes(parts):
    lane = lanes(parts[0].shape)
    return [
        jnp.where(lane < 96, parts[0], roll(parts[1], 96)),
        jnp.where(lane < 64, roll(parts[1], 96), roll(parts[2], 64)),
        jnp.where(lane < 32, roll(parts[2], 64), roll(parts[3], 32)),
    ]


ROW_CHUNKS = [(start, min(32, W - start)) for start in range(0, W, 32)]


def normalize(values):
    mean = jnp.sum(values, axis=-1, keepdims=True) * (1.0 / C)
    centered = values - mean
    spread = jnp.sum(centered * centered, axis=-1, keepdims=True) * (1.0 / C)
    scale = 1.0 / jnp.sqrt(spread + EPSILON)
    return centered * scale, scale


def send_packed(acc_ref, out_ref):
    for block in range(NB):
        rows = [block_lanes(acc_ref[r], block) for r in range(ROWS)]
        for group in range(GROUPS):
            tile = jnp.concatenate(
                [row[32 * group : 32 * group + 32] for row in rows], axis=0
            )
            pieces = pack_tile(tile)
            out_ref[block * GROUPS + group] = jnp.concatenate(pieces, axis=0).astype(BF)


def spectra_kernel(
    x_ref, g_ref, fwd_ref, inv_ref, out_ref,
    x_rows, g_rows, fwd_table, inv_table, padded_ref, acc_ref, send_ref, sems, out_sems,
):
    copies = [pltpu.make_async_copy(x_ref.at[0, 0], x_rows.at[0], sems.at[0])]
    copies += [pltpu.make_async_copy(fwd_ref, fwd_table, sems.at[1])]
    copies += [
        pltpu.make_async_copy(x_ref.at[0, r], x_rows.at[r], sems.at[1 + r])
        for r in range(1, ROWS)
    ]
    copies += [pltpu.make_async_copy(inv_ref, inv_table, sems.at[1 + ROWS])]
    copies += [
        pltpu.make_async_copy(g_ref.at[0, r], g_rows.at[r], sems.at[2 + ROWS + r])
        for r in range(ROWS)
    ]
    for copy in copies:
        copy.start()
    padded_ref[W - 20 :] = jnp.zeros((WPAD - W + 20, C), BF)
    for r in range(ROWS):
        copies[0 if r == 0 else 1 + r].wait()
        for start, size in ROW_CHUNKS:
            values = x_rows[r, start : start + size].astype(F32)
            padded_ref[start : start + size] = normalize(values)[0].astype(BF)
        if r == 0:
            copies[1].wait()
        acc_ref[r] = jnp.dot(fwd_table[...], padded_ref[...], preferred_element_type=F32)
    send_packed(acc_ref, send_ref.at[0])
    fields_out = pltpu.make_async_copy(
        send_ref.at[0], out_ref.at[:, pl.ds(0, PACK), :], out_sems.at[0]
    )
    fields_out.start()
    copies[1 + ROWS].wait()
    for r in range(ROWS):
        copies[2 + ROWS + r].wait()
        padded_ref[0:W] = g_rows[r]
        acc_ref[r] = jnp.dot(inv_table[...], padded_ref[...], preferred_element_type=F32)
    send_packed(acc_ref, send_ref.at[1])
    back_out = pltpu.make_async_copy(
        send_ref.at[1], out_ref.at[:, pl.ds(PACK, PACK), :], out_sems.at[1]
    )
    back_out.start()
    fields_out.wait()
    back_out.wait()


def to_spectra(fields, cotangent, forward, inverse):
    held = pl.BlockSpec(memory_space=pltpu.HBM)
    return pl.pallas_call(
        spectra_kernel,
        name="to_spectra",
        in_specs=[held, held, held, held],
        out_specs=held,
        out_shape=pltpu.HBM((BANDS, 2 * PACK, 128), BF),
        scratch_shapes=[
            pltpu.VMEM((ROWS, W, C), BF),
            pltpu.VMEM((ROWS, W, C), BF),
            pltpu.VMEM((2 * KX, WPAD), BF),
            pltpu.VMEM((2 * KX, WPAD), BF),
            pltpu.VMEM((WPAD, C), BF),
            pltpu.VMEM((ROWS, 2 * KX, C), F32),
            pltpu.VMEM((2, BANDS, PACK, 128), BF),
            pltpu.SemaphoreType.DMA((2 + 2 * ROWS,)),
            pltpu.SemaphoreType.DMA((2,)),
        ],
        compiler_params=pltpu.CompilerParams(vmem_limit_bytes=VMEM_LIMIT),
        cost_estimate=pl.CostEstimate(
            flops=4 * ROWS * W * 2 * KX * C, bytes_accessed=3000000, transcendentals=0
        ),
    )(*[pltpu.with_memory_space_constraint(a, pltpu.HBM) for a in (fields, cotangent, forward, inverse)])


PITCH = 20
BAND_PITCH = 2 * ROWS * PITCH


def eight_rows(base, row):
    return pl.ds(base + PITCH * (row // MODES) + row % MODES, 8)


def unpack_bands(recv_ref, first, rows_ref):
    def one(s, carry):
        pieces = [
            recv_ref[s, first + 24 * i : first + 24 * i + 24, :].astype(F32)
            for i in range(3)
        ]
        base = pl.multiple_of(s * BAND_PITCH, 8)
        for i, piece in enumerate(pieces + [unpack_tail(pieces)]):
            for u in range(0, 24, 8):
                rows_ref[eight_rows(base, 24 * i + u), :] = piece[u : u + 8]
        return carry

    lax.fori_loop(0, BANDS, one, 0, unroll=4)


def pack_bands(rows_ref, back_rows_ref, early_ref, late_ref, first):
    def one(s, carry):
        base = pl.multiple_of(s * BAND_PITCH, 8)

        def tile(ref):
            return jnp.concatenate(
                [ref[eight_rows(base, row), :] for row in range(0, 96, 8)], axis=0
            )

        pieces = pack_tile(tile(rows_ref))
        early_ref[s, 0:48] = jnp.concatenate(pieces[:2], axis=0).astype(BF)
        back = pack_tile(tile(back_rows_ref))
        late_ref[s] = jnp.concatenate(pieces[2:] + back, axis=0).astype(BF)
        return carry

    lax.fori_loop(first, first + BANDS // 4, one, 0, unroll=4)


def mode_rows(rows_ref, lat, pair):
    columns = jnp.concatenate(
        [
            rows_ref[pl.ds(2 * pair + j, 2 * H, stride=PITCH), :].astype(BF)
            for j in range(2)
        ],
        axis=1,
    )
    done = jnp.dot(lat, columns, preferred_element_type=F32).astype(BF)
    return jnp.concatenate(
        [
            jnp.concatenate(
                [done[0:H, 128 * j : 128 * j + 128], done[H : 2 * H, 128 * j : 128 * j + 128]],
                axis=1,
            )
            for j in range(2)
        ],
        axis=0,
    )


def spread(columns_ref, pair, modes):
    for j in range(2):
        lane = 128 * (2 * pair + j)
        for part in range(2):
            columns_ref[H * part : H * part + H, lane : lane + 128] = modes[
                H * j : H * j + H, 128 * part : 128 * part + 128
            ]


def store_rows(rows_ref, lat_t, columns_ref, pair):
    done = jnp.dot(
        lat_t, columns_ref[:, 256 * pair : 256 * pair + 256], preferred_element_type=F32
    )
    for j in range(2):
        rows_ref[pl.ds(2 * pair + j, 2 * H, stride=PITCH), :] = done[:, 128 * j : 128 * j + 128]


def fill_weight(weight_ref, form_ref):
    form_ref[...] = jnp.zeros_like(form_ref)
    real = weight_ref[0, 0]
    imag = weight_ref[1, 0]
    form_ref[0:BS, 0:BS] = real
    form_ref[0:BS, 128 : 128 + BS] = imag
    form_ref[128 : 128 + BS, 0:BS] = -imag
    form_ref[128 : 128 + BS, 128 : 128 + BS] = real


def choose_bias(block, bias_ref):
    bias = bias_ref[...]
    chosen = block_lanes(bias, 0)
    for other in range(1, NB):
        chosen = jnp.where(block == other, block_lanes(bias, other), chosen)
    chosen = jnp.where(lanes(chosen.shape) < BS, chosen, 0.0)
    return jnp.concatenate([chosen[0:1], chosen[1:2]], axis=1)


NT = (((1,), (1,)), ((), ()))
TN = (((0,), (0,)), ((), ()))


def with_one(value):
    return jnp.where(lanes(value.shape) == BS, jnp.ones_like(value), value)


def half_copy(source_ref, target_ref, sems, half):
    rows = pl.ds(HALF_PAIRS * PAIR_ROWS * half, HALF_PAIRS * PAIR_ROWS)
    return pltpu.make_async_copy(
        source_ref.at[:, rows, :], target_ref.at[:, rows, :], sems.at[half]
    )


def gradient_kernel(
    block_ref, recv_ref, lat_ref, first_ref, bias_ref, second_ref,
    saved_ref, grad_ref,
    w1_ref, w2_ref, rows_ref, back_rows_ref, modes_ref, filtered_ref, sums_ref, kept_ref, sems,
):
    fill_weight(first_ref, w1_ref)
    fill_weight(second_ref, w2_ref)
    bias = choose_bias(block_ref[0], bias_ref)
    unpack_bands(recv_ref, 0, rows_ref)
    unpack_bands(recv_ref, PACK, back_rows_ref)
    lat = lat_ref[...]
    w1 = w1_ref[...]
    w2 = w2_ref[...]
    saves = []
    for pair in range(PAIRS):
        span = slice(PAIR_ROWS * pair, PAIR_ROWS * pair + PAIR_ROWS)
        modes = mode_rows(rows_ref, lat, pair)
        modes = jnp.concatenate([with_one(modes[:, 0:128]), modes[:, 128:256]], axis=1)
        modes_ref[span] = modes
        pre = jnp.dot(modes, w1, preferred_element_type=F32) + bias
        cdf = 0.5 + 0.5 * lax.erf(pre * math.sqrt(0.5))
        hidden = (pre * cdf).astype(BF)
        hidden = jnp.concatenate([with_one(hidden[:, 0:128]), hidden[:, 128:256]], axis=1)
        kept_ref[0, span] = hidden
        slope = cdf + pre * (jnp.exp(-0.5 * pre * pre) * (1.0 / math.sqrt(2.0 * math.pi)))
        back_filtered = mode_rows(back_rows_ref, lat, pair)
        filtered_ref[span] = back_filtered
        back_hidden = lax.dot_general(back_filtered, w2, NT, preferred_element_type=F32)
        kept_ref[1, span] = (back_hidden * slope).astype(BF)
        if (pair + 1) % HALF_PAIRS == 0:
            save = half_copy(kept_ref, saved_ref, sems, pair // HALF_PAIRS)
            save.start()
            saves.append(save)
    row = 0
    bias_rows = []
    for left_ref, right_ref in ((modes_ref, kept_ref.at[1]), (kept_ref.at[0], filtered_ref)):
        right = right_ref[...]
        gathered = lax.dot_general(left_ref[...], right, TN, preferred_element_type=F32)
        real = gathered[0:BS, 0:128] + gathered[128 : 128 + BS, 128:256]
        imag = gathered[0:BS, 128:256] - gathered[128 : 128 + BS, 0:128]
        for part in (real, imag):
            for piece in pack_tile(part):
                sums_ref[row : row + 24] = piece
                row += 24
        bias_rows += [gathered[BS : BS + 8, 0:128], gathered[BS : BS + 8, 128:256]]
    for value in bias_rows:
        sums_ref[row : row + 8] = value
        row += 8
    sums_ref[row:] = jnp.zeros((CHUNKS * CHUNK_ROWS - row, 128), F32)
    for chunk in range(CHUNKS):
        grad_ref[chunk] = sums_ref[CHUNK_ROWS * chunk : CHUNK_ROWS * chunk + CHUNK_ROWS].astype(
            BF
        )
    for save in saves:
        save.wait()


def return_kernel(
    block_ref, saved_ref, lat_ref, first_ref, second_ref, bias_ref,
    early_ref, sent_ref,
    w1_ref, w2_ref, rows_ref, back_rows_ref, columns_ref, back_columns_ref,
    kept_ref, late_ref, sems, out_sems,
):
    fetches = [half_copy(saved_ref, kept_ref, sems, half) for half in range(2)]
    for fetch in fetches:
        fetch.start()
    fill_weight(first_ref, w1_ref)
    fill_weight(second_ref, w2_ref)
    bias = choose_bias(block_ref[0], bias_ref)
    lat_t = lat_ref[...]
    w1 = w1_ref[...]
    w2 = w2_ref[...]
    for pair in range(PAIRS):
        span = slice(PAIR_ROWS * pair, PAIR_ROWS * pair + PAIR_ROWS)
        if pair % HALF_PAIRS == 0:
            fetches[pair // HALF_PAIRS].wait()
        filtered = jnp.dot(kept_ref[0, span], w2, preferred_element_type=F32) + bias
        spread(columns_ref, pair, filtered.astype(BF))
        back_modes = lax.dot_general(kept_ref[1, span], w1, NT, preferred_element_type=F32)
        spread(back_columns_ref, pair, back_modes.astype(BF))
    for pair in range(PAIRS):
        store_rows(rows_ref, lat_t, columns_ref, pair)
        store_rows(back_rows_ref, lat_t, back_columns_ref, pair)
    leaving = []
    for part in range(4):
        pack_bands(rows_ref, back_rows_ref, early_ref, late_ref, part * (BANDS // 4))
        bands = pl.ds(part * (BANDS // 4), BANDS // 4)
        copy = pltpu.make_async_copy(
            late_ref.at[bands], sent_ref.at[bands], out_sems.at[part]
        )
        copy.start()
        leaving.append(copy)
    for copy in leaving:
        copy.wait()


PAIR_ROWS = 2 * H
PAIRS = MODES // 2
HALF_PAIRS = PAIRS // 2
WIDE = (MODES * H, 256)
FORM = pltpu.VMEM((256, 256), BF)
COLUMNS = pltpu.VMEM((2 * H, MODES * 128), BF)
BAND_ROWS = pltpu.VMEM((2 * H * PITCH, 128), F32)


def block_call(kernel, name, block, operands, specs, outs, places, scratch):
    return pl.pallas_call(
        kernel,
        name=name,
        grid_spec=pltpu.PrefetchScalarGridSpec(
            num_scalar_prefetch=1,
            grid=(1,),
            in_specs=[
                pl.BlockSpec((2, 1, BS, BS), lambda i, n: (0, n[0], 0, 0))
                if spec == "weight"
                else pl.BlockSpec(memory_space=pltpu.HBM)
                if spec == "far"
                else pl.BlockSpec(memory_space=pltpu.VMEM)
                for operand, spec in zip(operands, specs)
            ],
            out_specs=[
                pl.BlockSpec(memory_space=pltpu.HBM if place == "far" else pltpu.VMEM)
                for place in places
            ],
            scratch_shapes=scratch,
        ),
        out_shape=[
            pltpu.HBM(out.shape, out.dtype) if place == "far" else out
            for out, place in zip(outs, places)
        ],
        compiler_params=pltpu.CompilerParams(vmem_limit_bytes=14 * 1024 * 1024),
        cost_estimate=pl.CostEstimate(
            flops=1000000000, bytes_accessed=6000000, transcendentals=800000
        ),
    )(block, *operands)


def receive(parts, rows_ref):
    for group in range(GROUPS):
        for quad in range(2):
            tiles = []
            for block in range(4):
                band = (4 * quad + block) * GROUPS + group
                pieces = [ref[band, at : at + 24, :].astype(F32) for ref, at in parts]
                tiles.append(
                    jnp.concatenate(pieces + [unpack_tail(pieces)], axis=0).astype(BF)
                )
            for t, joined in enumerate(join_lanes(tiles)):
                for r in range(ROWS):
                    rows_ref[
                        r,
                        32 * group : 32 * group + 32,
                        384 * quad + 128 * t : 384 * quad + 128 * t + 128,
                    ] = joined[32 * r : 32 * r + 32]


def output_kernel(
    early_ref, late_ref, x_ref, g_ref, fwd_ref, inv_ref,
    out_ref, grad_ref,
    rows_ref, back_rows_ref, mixed_ref, back_ref,
):
    r = pl.program_id(0)

    @pl.when(r == 0)
    def _():
        receive(((early_ref, 0), (early_ref, 24), (late_ref, 0)), rows_ref)
        receive(((late_ref, 24), (late_ref, 48), (late_ref, 72)), back_rows_ref)

    mixed_ref[...] = jnp.dot(inv_ref[...], rows_ref[r], preferred_element_type=F32)
    back_ref[...] = jnp.dot(fwd_ref[...], back_rows_ref[r], preferred_element_type=F32)
    for start, size in ROW_CHUNKS:
        span = slice(start, start + size)
        values = x_ref[0, r, span].astype(F32)
        normed, scale = normalize(values)
        out_ref[0, 0, span] = (values + normed + mixed_ref[span]).astype(BF)
        upstream = g_ref[0, r, span].astype(F32)
        back = upstream + back_ref[span]
        mean = jnp.sum(back, axis=-1, keepdims=True) * (1.0 / C)
        along = jnp.sum(back * normed, axis=-1, keepdims=True) * (1.0 / C)
        grad_ref[0, 0, span] = (upstream + scale * (back - mean - normed * along)).astype(BF)


def from_spectra(early, late, fields, cotangent, forward, inverse):
    token_spec = pl.BlockSpec((1, 1, W, C), lambda r: (0, r, 0, 0))
    near = pl.BlockSpec(memory_space=pltpu.VMEM)
    token = jax.ShapeDtypeStruct((1, ROWS, W, C), BF)
    return pl.pallas_call(
        output_kernel,
        name="from_spectra",
        grid=(ROWS,),
        in_specs=[near] * 6,
        out_specs=[token_spec, token_spec],
        out_shape=[token, token],
        scratch_shapes=[
            pltpu.VMEM((ROWS, 2 * KX, C), BF),
            pltpu.VMEM((ROWS, 2 * KX, C), BF),
            pltpu.VMEM((WPAD, C), F32),
            pltpu.VMEM((WPAD, C), F32),
        ],
        compiler_params=pltpu.CompilerParams(vmem_limit_bytes=VMEM_LIMIT),
        cost_estimate=pl.CostEstimate(
            flops=4 * ROWS * W * 2 * KX * C, bytes_accessed=5000000, transcendentals=0
        ),
    )(early, late, fields, cotangent, forward, inverse)


def whole(shape):
    return pl.BlockSpec(shape, lambda: (0,) * len(shape))


def spectral_call(kernel, name, operands, outs, scratch):
    return pl.pallas_call(
        kernel,
        name=name,
        in_specs=[whole(operand.shape) for operand in operands],
        out_specs=[whole(out.shape) for out in outs],
        out_shape=outs,
        scratch_shapes=scratch,
        compiler_params=pltpu.CompilerParams(vmem_limit_bytes=VMEM_LIMIT),
        cost_estimate=pl.CostEstimate(
            flops=1000000, bytes_accessed=1000000, transcendentals=0
        ),
    )(*operands)


def share_kernel(recv_ref, held_ref, out_ref):
    total = recv_ref[0].astype(F32)
    for i in range(1, recv_ref.shape[0]):
        total = total + recv_ref[i].astype(F32)
    share = total.astype(BF)
    for band in range(BANDS):
        out_ref[band] = share


def add_share(shares, held):
    return pl.pallas_call(
        share_kernel,
        name="grad_share",
        grid=(1,),
        in_specs=[
            pl.BlockSpec(shares.shape, lambda i: (0, 0, 0)),
            pl.BlockSpec(memory_space=pl.ANY),
        ],
        out_specs=pl.BlockSpec((BANDS, CHUNK_ROWS, 128), lambda i: (0, 2, 0)),
        out_shape=jax.ShapeDtypeStruct(held.shape, BF),
        input_output_aliases={1: 0},
        compiler_params=pltpu.CompilerParams(vmem_limit_bytes=VMEM_LIMIT),
    )(shares, held)


def group_sum_kernel(recv_ref, out_ref):
    for block in range(NB):
        total = recv_ref[block * GROUPS].astype(F32)
        for group in range(1, GROUPS):
            total = total + recv_ref[block * GROUPS + group].astype(F32)
        out_ref[block] = total.astype(BF)


def group_sums(message):
    return pl.pallas_call(
        group_sum_kernel,
        name="grad_groups",
        grid=(1,),
        in_specs=[pl.BlockSpec((BANDS, CHUNK_ROWS, 128), lambda i: (0, 2, 0))],
        out_specs=pl.BlockSpec((NB, CHUNK_ROWS, 128), lambda i: (0, 0, 0)),
        out_shape=jax.ShapeDtypeStruct((NB, CHUNK_ROWS, 128), BF),
        compiler_params=pltpu.CompilerParams(vmem_limit_bytes=VMEM_LIMIT),
    )(message)


GRAD_SCALE = 1.0 / (SAMPLES * H)


def grads_kernel(recv_ref, w1_ref, b1_ref, w2_ref, b2_ref):
    for block in range(NB):
        chunk = 0
        for out_ref in (w1_ref, w2_ref):
            for part in range(2):
                pieces = [
                    recv_ref[chunk + i, block].astype(F32) * GRAD_SCALE for i in range(3)
                ]
                chunk += 3
                for i in range(3):
                    out_ref[part, block, 24 * i : 24 * i + 24, :] = pieces[i][:, :BS]
                out_ref[part, block, 72:96, :] = unpack_tail(pieces)[:, :BS]
    rows = [
        jnp.concatenate([recv_ref[12, block], recv_ref[13, block]], axis=0).astype(F32)
        * GRAD_SCALE
        for block in range(NB)
    ]
    for out_ref, first in ((b1_ref, 0), (b2_ref, 16)):
        for part in range(2):
            at = first + 8 * part
            for quad in range(2):
                parts = [rows[4 * quad + j][at : at + 8] for j in range(4)]
                for t, joined in enumerate(join_lanes(parts)):
                    lane = 384 * quad + 128 * t
                    out_ref[part : part + 1, lane : lane + 128] = joined[0:1]


def exchange(value):
    return lax.all_to_all(value, "lat", split_axis=0, concat_axis=0, tiled=True)


def on_device(fields, cotangent, w_first, b_first, w_second, b_second):
    block = (lax.axis_index("lat") // GROUPS).astype(jnp.int32).reshape(1)
    lon_fwd = jnp.asarray(LON_FWD, BF)
    lon_inv = jnp.asarray(LON_INV, BF)
    lon_fwd_t = jnp.asarray(LON_FWD.T, BF)
    lon_inv_t = jnp.asarray(LON_INV.T, BF)
    lat = jnp.asarray(LAT, BF)
    lat_t = jnp.asarray(LAT.T, BF)

    spectra = to_spectra(fields, cotangent, lon_fwd_t, lon_inv_t)
    spectra = exchange(spectra)
    kept, grads = block_call(
        gradient_kernel,
        "spectral_grads",
        block,
        (spectra, lat, w_first, b_first, w_second),
        ("", "", "weight", "", "weight"),
        [jax.ShapeDtypeStruct((2,) + WIDE, BF), jax.ShapeDtypeStruct((CHUNKS, CHUNK_ROWS, 128), BF)],
        ("far", "near"),
        [FORM, FORM, BAND_ROWS, BAND_ROWS, pltpu.VMEM(WIDE, BF), pltpu.VMEM(WIDE, BF)]
        + [pltpu.VMEM((CHUNKS * CHUNK_ROWS, 128), F32), pltpu.VMEM((2,) + WIDE, BF)]
        + [pltpu.SemaphoreType.DMA((2,))],
    )
    kept = pltpu.with_memory_space_constraint(kept, pltpu.HBM)
    dp_size = lax.axis_size("dp")
    if dp_size == CHUNKS:
        shares = lax.all_to_all(grads, "dp", 0, 0, tiled=True)
    else:
        shares = grads
    early, late = block_call(
        return_kernel,
        "spectral_return",
        block,
        (kept, lat_t, w_first, w_second, b_second),
        ("far", "", "weight", "weight", ""),
        [
            jax.ShapeDtypeStruct((BANDS, PACK, 128), BF),
            jax.ShapeDtypeStruct((BANDS, 96, 128), BF),
        ],
        ("near", "far"),
        [FORM, FORM, BAND_ROWS, BAND_ROWS, COLUMNS, COLUMNS, pltpu.VMEM((2,) + WIDE, BF)]
        + [pltpu.VMEM((BANDS, 96, 128), BF)]
        + [pltpu.SemaphoreType.DMA((2,)), pltpu.SemaphoreType.DMA((4,))],
    )
    early = exchange(add_share(shares, early))
    late, early = lax.optimization_barrier((late, early))
    late = exchange(late)
    blocks = group_sums(early)
    every = lax.all_gather(blocks, "dp", axis=0, tiled=False)
    if dp_size != CHUNKS:
        every = jnp.broadcast_to(every, (CHUNKS, NB, CHUNK_ROWS, 128))
    grad_w = jax.ShapeDtypeStruct((2, NB, BS, BS), F32)
    grad_b = jax.ShapeDtypeStruct((2, C), F32)
    g_w1, g_b1, g_w2, g_b2 = spectral_call(
        grads_kernel, "grad_out", (every,), [grad_w, grad_b, grad_w, grad_b], []
    )
    result, back_fields = from_spectra(early, late, fields, cotangent, lon_fwd, lon_inv)
    return (result, back_fields, g_w1, g_b1, g_w2, g_b2)


def solution(mesh):
    placed = (P("dp", "lat", None, None), P("dp", "lat", None, None), P(), P(), P(), P())
    return jax.shard_map(
        on_device,
        mesh=mesh,
        in_specs=placed,
        out_specs=(P("dp", "lat", None, None), P("dp", "lat", None, None), P(), P(), P(), P()),
        check_vma=False,
    )
```

```python
import math

import jax
import jax.numpy as jnp
import numpy as np
from jax import lax
from jax.experimental import pallas as pl
from jax.experimental.pallas import tpu as pltpu
from jax.sharding import PartitionSpec as P

C = 768
NB = 8
BS = 96
H = 96
W = 180
KX = 64
SAMPLES = 16
EPSILON = 1e-06

BANDS = 32
GROUPS = 4
MODES = KX // GROUPS
ROWS = H // BANDS
WPAD = 192
PACK = 72
CHUNKS = 16
CHUNK_ROWS = 24
BF = jnp.bfloat16
F32 = jnp.float32
VMEM_LIMIT = 10 * 1024 * 1024


def tables():
    w_index = np.arange(W)[:, None]
    k_index = np.arange(KX)[None, :]
    lon = (2.0 * math.pi / W * (w_index * k_index % W)).astype(np.float64)
    fwd = np.stack([np.cos(lon), -np.sin(lon)], axis=1) / math.sqrt(W)
    weight = np.where(k_index == 0, 1.0, 2.0)[:, None, :]
    inv = fwd * weight
    def order(table):
        grouped = table.reshape(W, 2, GROUPS, MODES).transpose(0, 2, 1, 3).reshape(W, 2 * KX)
        padded = np.zeros((WPAD, 2 * KX))
        padded[:W] = grouped
        return padded

    h_index = np.arange(H)
    lat = 2.0 * math.pi / H * (h_index[:, None] * h_index[None, :] % H)
    cosine = np.cos(lat) / math.sqrt(H)
    sine = np.sin(lat) / math.sqrt(H)
    full = np.stack(
        [np.stack([cosine, sine], axis=2), np.stack([-sine, cosine], axis=2)], axis=0
    ).reshape(2 * H, 2 * H)
    return order(fwd), order(inv), full


LON_FWD, LON_INV, LAT = tables()


def lanes(shape):
    return lax.broadcasted_iota(jnp.int32, shape, 1)


def roll(value, shift):
    return pltpu.roll(value, shift % 128, 1)


def pack_tile(tile):
    lane = lanes((24, 128))
    tail = tile[72:96]
    return [
        jnp.where(lane < 96, tile[24 * i : 24 * i + 24], roll(tail, 96 - 32 * i))
        for i in range(3)
    ]


def unpack_tail(pieces):
    lane = lanes((24, 128))
    return jnp.where(
        lane < 32,
        roll(pieces[0], 32),
        jnp.where(lane < 64, roll(pieces[1], 64), roll(pieces[2], 96)),
    )


def block_lanes(value, block):
    start = BS * block
    first, shift = start // 128, start % 128
    head = value[:, 128 * first : 128 * first + 128]
    if shift == 0:
        return head
    head = roll(head, 128 - shift)
    if shift + BS <= 128:
        return head
    after = roll(value[:, 128 * first + 128 : 128 * first + 256], 128 - shift)
    return jnp.where(lanes(head.shape) < 128 - shift, head, after)


def join_lanes(parts):
    lane = lanes(parts[0].shape)
    return [
        jnp.where(lane < 96, parts[0], roll(parts[1], 96)),
        jnp.where(lane < 64, roll(parts[1], 96), roll(parts[2], 64)),
        jnp.where(lane < 32, roll(parts[2], 64), roll(parts[3], 32)),
    ]


ROW_CHUNKS = [(start, min(32, W - start)) for start in range(0, W, 32)]


def normalize(values):
    mean = jnp.sum(values, axis=-1, keepdims=True) * (1.0 / C)
    centered = values - mean
    spread = jnp.sum(centered * centered, axis=-1, keepdims=True) * (1.0 / C)
    scale = 1.0 / jnp.sqrt(spread + EPSILON)
    return centered * scale, scale


def send_packed(acc_ref, out_ref, first):
    for block in range(NB):
        rows = [block_lanes(acc_ref[r], block) for r in range(ROWS)]
        for group in range(GROUPS):
            tile = jnp.concatenate(
                [row[32 * group : 32 * group + 32] for row in rows], axis=0
            )
            pieces = pack_tile(tile)
            out_ref[block * GROUPS + group, first : first + PACK] = jnp.concatenate(
                pieces, axis=0
            ).astype(BF)


def spectra_kernel(
    x_ref, g_ref, fwd_ref, inv_ref, out_ref,
    x_rows, g_rows, fwd_table, inv_table, padded_ref, acc_ref, sems,
):
    copies = [pltpu.make_async_copy(x_ref.at[0, 0], x_rows.at[0], sems.at[0])]
    copies += [pltpu.make_async_copy(fwd_ref, fwd_table, sems.at[1])]
    copies += [
        pltpu.make_async_copy(x_ref.at[0, r], x_rows.at[r], sems.at[1 + r])
        for r in range(1, ROWS)
    ]
    copies += [pltpu.make_async_copy(inv_ref, inv_table, sems.at[1 + ROWS])]
    copies += [
        pltpu.make_async_copy(g_ref.at[0, r], g_rows.at[r], sems.at[2 + ROWS + r])
        for r in range(ROWS)
    ]
    for copy in copies:
        copy.start()
    padded_ref[W - 20 :] = jnp.zeros((WPAD - W + 20, C), BF)
    for r in range(ROWS):
        copies[0 if r == 0 else 1 + r].wait()
        for start, size in ROW_CHUNKS:
            values = x_rows[r, start : start + size].astype(F32)
            padded_ref[start : start + size] = normalize(values)[0].astype(BF)
        if r == 0:
            copies[1].wait()
        acc_ref[r] = jnp.dot(fwd_table[...], padded_ref[...], preferred_element_type=F32)
    for copy in copies[1 + ROWS :]:
        copy.wait()
    send_packed(acc_ref, out_ref, 0)
    for r in range(ROWS):
        padded_ref[0:W] = g_rows[r]
        acc_ref[r] = jnp.dot(inv_table[...], padded_ref[...], preferred_element_type=F32)
    send_packed(acc_ref, out_ref, PACK)


def to_spectra(fields, cotangent, forward, inverse):
    held = pl.BlockSpec(memory_space=pltpu.HBM)
    return pl.pallas_call(
        spectra_kernel,
        name="to_spectra",
        in_specs=[held, held, held, held],
        out_specs=pl.BlockSpec(memory_space=pltpu.VMEM),
        out_shape=jax.ShapeDtypeStruct((BANDS, 2 * PACK, 128), BF),
        scratch_shapes=[
            pltpu.VMEM((ROWS, W, C), BF),
            pltpu.VMEM((ROWS, W, C), BF),
            pltpu.VMEM((2 * KX, WPAD), BF),
            pltpu.VMEM((2 * KX, WPAD), BF),
            pltpu.VMEM((WPAD, C), BF),
            pltpu.VMEM((ROWS, 2 * KX, C), F32),
            pltpu.SemaphoreType.DMA((2 + 2 * ROWS,)),
        ],
        compiler_params=pltpu.CompilerParams(vmem_limit_bytes=VMEM_LIMIT),
        cost_estimate=pl.CostEstimate(
            flops=4 * ROWS * W * 2 * KX * C, bytes_accessed=3000000, transcendentals=0
        ),
    )(*[pltpu.with_memory_space_constraint(a, pltpu.HBM) for a in (fields, cotangent, forward, inverse)])


PITCH = 20
BAND_PITCH = 2 * ROWS * PITCH


def eight_rows(base, row):
    return pl.ds(base + PITCH * (row // MODES) + row % MODES, 8)


def unpack_bands(recv_ref, rows_ref, back_rows_ref):
    def one(s, carry):
        base = pl.multiple_of(s * BAND_PITCH, 8)
        for first, target_ref in ((0, rows_ref), (PACK, back_rows_ref)):
            pieces = [
                recv_ref[s, first + 24 * i : first + 24 * i + 24, :].astype(F32)
                for i in range(3)
            ]
            for i, piece in enumerate(pieces + [unpack_tail(pieces)]):
                for u in range(0, 24, 8):
                    target_ref[eight_rows(base, 24 * i + u), :] = piece[u : u + 8]
        return carry

    lax.fori_loop(0, BANDS, one, 0, unroll=4)


def pack_bands(rows_ref, back_rows_ref, early_ref, late_ref, first):
    def one(s, carry):
        base = pl.multiple_of(s * BAND_PITCH, 8)

        def tile(ref):
            return jnp.concatenate(
                [ref[eight_rows(base, row), :] for row in range(0, 96, 8)], axis=0
            )

        pieces = pack_tile(tile(rows_ref))
        early_ref[s, 0:48] = jnp.concatenate(pieces[:2], axis=0).astype(BF)
        back = pack_tile(tile(back_rows_ref))
        late_ref[s] = jnp.concatenate(pieces[2:] + back, axis=0).astype(BF)
        return carry

    lax.fori_loop(first, first + BANDS // 4, one, 0, unroll=4)


def mode_rows(rows_ref, lat, pair):
    columns = jnp.concatenate(
        [
            rows_ref[pl.ds(2 * pair + j, 2 * H, stride=PITCH), :].astype(BF)
            for j in range(2)
        ],
        axis=1,
    )
    done = jnp.dot(lat, columns, preferred_element_type=F32).astype(BF)
    return jnp.concatenate(
        [
            jnp.concatenate(
                [done[0:H, 128 * j : 128 * j + 128], done[H : 2 * H, 128 * j : 128 * j + 128]],
                axis=1,
            )
            for j in range(2)
        ],
        axis=0,
    )


def spread(columns_ref, pair, modes):
    for j in range(2):
        lane = 128 * (2 * pair + j)
        for part in range(2):
            columns_ref[H * part : H * part + H, lane : lane + 128] = modes[
                H * j : H * j + H, 128 * part : 128 * part + 128
            ]


def store_rows(rows_ref, lat_t, columns_ref, pair):
    done = jnp.dot(
        lat_t, columns_ref[:, 256 * pair : 256 * pair + 256], preferred_element_type=F32
    )
    for j in range(2):
        rows_ref[pl.ds(2 * pair + j, 2 * H, stride=PITCH), :] = done[:, 128 * j : 128 * j + 128]


def fill_weight(weight_ref, block, form_ref):
    form_ref[...] = jnp.zeros_like(form_ref)
    real = weight_ref[0, block]
    imag = weight_ref[1, block]
    form_ref[0:BS, 0:BS] = real
    form_ref[0:BS, 128 : 128 + BS] = imag
    form_ref[128 : 128 + BS, 0:BS] = -imag
    form_ref[128 : 128 + BS, 128 : 128 + BS] = real


def choose_bias(block, bias_ref):
    bias = bias_ref[...]
    chosen = block_lanes(bias, 0)
    for other in range(1, NB):
        chosen = jnp.where(block == other, block_lanes(bias, other), chosen)
    chosen = jnp.where(lanes(chosen.shape) < BS, chosen, 0.0)
    return jnp.concatenate([chosen[0:1], chosen[1:2]], axis=1)


NT = (((1,), (1,)), ((), ()))
TN = (((0,), (0,)), ((), ()))


def with_one(value):
    return jnp.where(lanes(value.shape) == BS, jnp.ones_like(value), value)


def half_copy(source_ref, target_ref, sems, half):
    rows = pl.ds(HALF_PAIRS * PAIR_ROWS * half, HALF_PAIRS * PAIR_ROWS)
    return pltpu.make_async_copy(
        source_ref.at[:, rows, :], target_ref.at[:, rows, :], sems.at[half]
    )


def gradient_kernel(
    block_ref, recv_ref, lat_ref, first_ref, bias_ref, second_ref,
    saved_ref, grad_ref,
    w1_ref, w2_ref, rows_ref, back_rows_ref, modes_ref, filtered_ref, sums_ref, kept_ref, sems,
):
    block = block_ref[0]
    fill_weight(first_ref, block, w1_ref)
    fill_weight(second_ref, block, w2_ref)
    bias = choose_bias(block, bias_ref)
    unpack_bands(recv_ref, rows_ref, back_rows_ref)
    lat = lat_ref[...]
    w1 = w1_ref[...]
    w2 = w2_ref[...]
    saves = []
    for pair in range(PAIRS):
        span = slice(PAIR_ROWS * pair, PAIR_ROWS * pair + PAIR_ROWS)
        modes = mode_rows(rows_ref, lat, pair)
        modes = jnp.concatenate([with_one(modes[:, 0:128]), modes[:, 128:256]], axis=1)
        modes_ref[span] = modes
        pre = jnp.dot(modes, w1, preferred_element_type=F32) + bias
        cdf = 0.5 + 0.5 * lax.erf(pre * math.sqrt(0.5))
        hidden = (pre * cdf).astype(BF)
        hidden = jnp.concatenate([with_one(hidden[:, 0:128]), hidden[:, 128:256]], axis=1)
        kept_ref[0, span] = hidden
        slope = cdf + pre * (jnp.exp(-0.5 * pre * pre) * (1.0 / math.sqrt(2.0 * math.pi)))
        back_filtered = mode_rows(back_rows_ref, lat, pair)
        filtered_ref[span] = back_filtered
        back_hidden = lax.dot_general(back_filtered, w2, NT, preferred_element_type=F32)
        kept_ref[1, span] = (back_hidden * slope).astype(BF)
        if (pair + 1) % HALF_PAIRS == 0:
            save = half_copy(kept_ref, saved_ref, sems, pair // HALF_PAIRS)
            save.start()
            saves.append(save)
    row = 0
    bias_rows = []
    for left_ref, right_ref in ((modes_ref, kept_ref.at[1]), (kept_ref.at[0], filtered_ref)):
        right = right_ref[...]
        gathered = lax.dot_general(left_ref[...], right, TN, preferred_element_type=F32)
        real = gathered[0:BS, 0:128] + gathered[128 : 128 + BS, 128:256]
        imag = gathered[0:BS, 128:256] - gathered[128 : 128 + BS, 0:128]
        for part in (real, imag):
            for piece in pack_tile(part):
                sums_ref[row : row + 24] = piece
                row += 24
        bias_rows += [gathered[BS : BS + 8, 0:128], gathered[BS : BS + 8, 128:256]]
    for value in bias_rows:
        sums_ref[row : row + 8] = value
        row += 8
    sums_ref[row:] = jnp.zeros((CHUNKS * CHUNK_ROWS - row, 128), F32)
    for chunk in range(CHUNKS):
        grad_ref[chunk] = sums_ref[CHUNK_ROWS * chunk : CHUNK_ROWS * chunk + CHUNK_ROWS].astype(
            BF
        )
    for save in saves:
        save.wait()


def return_kernel(
    block_ref, saved_ref, lat_ref, first_ref, second_ref, bias_ref,
    early_ref, sent_ref,
    w1_ref, w2_ref, rows_ref, back_rows_ref, columns_ref, back_columns_ref,
    kept_ref, late_ref, sems, out_sems,
):
    fetches = [half_copy(saved_ref, kept_ref, sems, half) for half in range(2)]
    for fetch in fetches:
        fetch.start()
    block = block_ref[0]
    fill_weight(first_ref, block, w1_ref)
    fill_weight(second_ref, block, w2_ref)
    bias = choose_bias(block, bias_ref)
    lat_t = lat_ref[...]
    w1 = w1_ref[...]
    w2 = w2_ref[...]
    for pair in range(PAIRS):
        span = slice(PAIR_ROWS * pair, PAIR_ROWS * pair + PAIR_ROWS)
        if pair % HALF_PAIRS == 0:
            fetches[pair // HALF_PAIRS].wait()
        filtered = jnp.dot(kept_ref[0, span], w2, preferred_element_type=F32) + bias
        spread(columns_ref, pair, filtered.astype(BF))
        back_modes = lax.dot_general(kept_ref[1, span], w1, NT, preferred_element_type=F32)
        spread(back_columns_ref, pair, back_modes.astype(BF))
    for pair in range(PAIRS):
        store_rows(rows_ref, lat_t, columns_ref, pair)
        store_rows(back_rows_ref, lat_t, back_columns_ref, pair)
    leaving = []
    for part in range(4):
        pack_bands(rows_ref, back_rows_ref, early_ref, late_ref, part * (BANDS // 4))
        bands = pl.ds(part * (BANDS // 4), BANDS // 4)
        copy = pltpu.make_async_copy(
            late_ref.at[bands], sent_ref.at[bands], out_sems.at[part]
        )
        copy.start()
        leaving.append(copy)
    for copy in leaving:
        copy.wait()


PAIR_ROWS = 2 * H
PAIRS = MODES // 2
HALF_PAIRS = PAIRS // 2
WIDE = (MODES * H, 256)
FORM = pltpu.VMEM((256, 256), BF)
COLUMNS = pltpu.VMEM((2 * H, MODES * 128), BF)
BAND_ROWS = pltpu.VMEM((2 * H * PITCH, 128), F32)


def block_call(kernel, name, block, operands, operand_places, outs, places, scratch):
    return pl.pallas_call(
        kernel,
        name=name,
        grid_spec=pltpu.PrefetchScalarGridSpec(
            num_scalar_prefetch=1,
            grid=(1,),
            in_specs=[
                pl.BlockSpec(memory_space=pltpu.HBM if place == "far" else pltpu.VMEM)
                for place in operand_places
            ],
            out_specs=[
                pl.BlockSpec(memory_space=pltpu.HBM if place == "far" else pltpu.VMEM)
                for place in places
            ],
            scratch_shapes=scratch,
        ),
        out_shape=[
            pltpu.HBM(out.shape, out.dtype) if place == "far" else out
            for out, place in zip(outs, places)
        ],
        compiler_params=pltpu.CompilerParams(vmem_limit_bytes=14 * 1024 * 1024),
        cost_estimate=pl.CostEstimate(
            flops=1000000000, bytes_accessed=6000000, transcendentals=800000
        ),
    )(block, *operands)


def receive(parts, rows_ref):
    for group in range(GROUPS):
        for quad in range(2):
            tiles = []
            for block in range(4):
                band = (4 * quad + block) * GROUPS + group
                pieces = [ref[band, at : at + 24, :].astype(F32) for ref, at in parts]
                tiles.append(
                    jnp.concatenate(pieces + [unpack_tail(pieces)], axis=0).astype(BF)
                )
            for t, joined in enumerate(join_lanes(tiles)):
                for r in range(ROWS):
                    rows_ref[
                        r,
                        32 * group : 32 * group + 32,
                        384 * quad + 128 * t : 384 * quad + 128 * t + 128,
                    ] = joined[32 * r : 32 * r + 32]


def output_kernel(
    early_ref, late_ref, x_ref, g_ref, fwd_ref, inv_ref,
    out_ref, grad_ref,
    rows_ref, back_rows_ref, mixed_ref, back_ref,
):
    r = pl.program_id(0)

    @pl.when(r == 0)
    def _():
        receive(((early_ref, 0), (early_ref, 24), (late_ref, 0)), rows_ref)
        receive(((late_ref, 24), (late_ref, 48), (late_ref, 72)), back_rows_ref)

    mixed_ref[...] = jnp.dot(inv_ref[...], rows_ref[r], preferred_element_type=F32)
    back_ref[...] = jnp.dot(fwd_ref[...], back_rows_ref[r], preferred_element_type=F32)
    for start, size in ROW_CHUNKS:
        span = slice(start, start + size)
        values = x_ref[0, r, span].astype(F32)
        normed, scale = normalize(values)
        out_ref[0, 0, span] = (values + normed + mixed_ref[span]).astype(BF)
        upstream = g_ref[0, r, span].astype(F32)
        back = upstream + back_ref[span]
        mean = jnp.sum(back, axis=-1, keepdims=True) * (1.0 / C)
        along = jnp.sum(back * normed, axis=-1, keepdims=True) * (1.0 / C)
        grad_ref[0, 0, span] = (upstream + scale * (back - mean - normed * along)).astype(BF)


def from_spectra(early, late, fields, cotangent, forward, inverse):
    token_spec = pl.BlockSpec((1, 1, W, C), lambda r: (0, r, 0, 0))
    near = pl.BlockSpec(memory_space=pltpu.VMEM)
    token = jax.ShapeDtypeStruct((1, ROWS, W, C), BF)
    return pl.pallas_call(
        output_kernel,
        name="from_spectra",
        grid=(ROWS,),
        in_specs=[near] * 6,
        out_specs=[token_spec, token_spec],
        out_shape=[token, token],
        scratch_shapes=[
            pltpu.VMEM((ROWS, 2 * KX, C), BF),
            pltpu.VMEM((ROWS, 2 * KX, C), BF),
            pltpu.VMEM((WPAD, C), F32),
            pltpu.VMEM((WPAD, C), F32),
        ],
        compiler_params=pltpu.CompilerParams(vmem_limit_bytes=VMEM_LIMIT),
        cost_estimate=pl.CostEstimate(
            flops=4 * ROWS * W * 2 * KX * C, bytes_accessed=5000000, transcendentals=0
        ),
    )(early, late, fields, cotangent, forward, inverse)


def whole(shape):
    return pl.BlockSpec(shape, lambda: (0,) * len(shape))


def spectral_call(kernel, name, operands, outs, scratch):
    return pl.pallas_call(
        kernel,
        name=name,
        in_specs=[whole(operand.shape) for operand in operands],
        out_specs=[whole(out.shape) for out in outs],
        out_shape=outs,
        scratch_shapes=scratch,
        compiler_params=pltpu.CompilerParams(vmem_limit_bytes=VMEM_LIMIT),
        cost_estimate=pl.CostEstimate(
            flops=1000000, bytes_accessed=1000000, transcendentals=0
        ),
    )(*operands)


def share_kernel(recv_ref, held_ref, out_ref):
    total = recv_ref[0].astype(F32)
    for i in range(1, recv_ref.shape[0]):
        total = total + recv_ref[i].astype(F32)
    share = total.astype(BF)
    for band in range(BANDS):
        out_ref[band] = share


def add_share(shares, held):
    return pl.pallas_call(
        share_kernel,
        name="grad_share",
        grid=(1,),
        in_specs=[
            pl.BlockSpec(shares.shape, lambda i: (0, 0, 0)),
            pl.BlockSpec(memory_space=pl.ANY),
        ],
        out_specs=pl.BlockSpec((BANDS, CHUNK_ROWS, 128), lambda i: (0, 2, 0)),
        out_shape=jax.ShapeDtypeStruct(held.shape, BF),
        input_output_aliases={1: 0},
        compiler_params=pltpu.CompilerParams(vmem_limit_bytes=VMEM_LIMIT),
    )(shares, held)


def group_sum_kernel(recv_ref, out_ref):
    for block in range(NB):
        total = recv_ref[block * GROUPS].astype(F32)
        for group in range(1, GROUPS):
            total = total + recv_ref[block * GROUPS + group].astype(F32)
        out_ref[block] = total.astype(BF)


def group_sums(message):
    return pl.pallas_call(
        group_sum_kernel,
        name="grad_groups",
        grid=(1,),
        in_specs=[pl.BlockSpec((BANDS, CHUNK_ROWS, 128), lambda i: (0, 2, 0))],
        out_specs=pl.BlockSpec((NB, CHUNK_ROWS, 128), lambda i: (0, 0, 0)),
        out_shape=jax.ShapeDtypeStruct((NB, CHUNK_ROWS, 128), BF),
        compiler_params=pltpu.CompilerParams(vmem_limit_bytes=VMEM_LIMIT),
    )(message)


GRAD_SCALE = 1.0 / (SAMPLES * H)


def grads_kernel(recv_ref, w1_ref, b1_ref, w2_ref, b2_ref):
    for block in range(NB):
        chunk = 0
        for out_ref in (w1_ref, w2_ref):
            for part in range(2):
                pieces = [
                    recv_ref[chunk + i, block].astype(F32) * GRAD_SCALE for i in range(3)
                ]
                chunk += 3
                for i in range(3):
                    out_ref[part, block, 24 * i : 24 * i + 24, :] = pieces[i][:, :BS]
                out_ref[part, block, 72:96, :] = unpack_tail(pieces)[:, :BS]
    rows = [
        jnp.concatenate([recv_ref[12, block], recv_ref[13, block]], axis=0).astype(F32)
        * GRAD_SCALE
        for block in range(NB)
    ]
    for out_ref, first in ((b1_ref, 0), (b2_ref, 16)):
        for part in range(2):
            at = first + 8 * part
            for quad in range(2):
                parts = [rows[4 * quad + j][at : at + 8] for j in range(4)]
                for t, joined in enumerate(join_lanes(parts)):
                    lane = 384 * quad + 128 * t
                    out_ref[part : part + 1, lane : lane + 128] = joined[0:1]


def exchange(value):
    return lax.all_to_all(value, "lat", split_axis=0, concat_axis=0, tiled=True)


def on_device(fields, cotangent, w_first, b_first, w_second, b_second):
    block = (lax.axis_index("lat") // GROUPS).astype(jnp.int32).reshape(1)
    lon_fwd = jnp.asarray(LON_FWD, BF)
    lon_inv = jnp.asarray(LON_INV, BF)
    lon_fwd_t = jnp.asarray(LON_FWD.T, BF)
    lon_inv_t = jnp.asarray(LON_INV.T, BF)
    lat = jnp.asarray(LAT, BF)
    lat_t = jnp.asarray(LAT.T, BF)

    spectra = to_spectra(fields, cotangent, lon_fwd_t, lon_inv_t)
    spectra, block = lax.optimization_barrier((spectra, block))
    spectra = exchange(spectra)
    kept, grads = block_call(
        gradient_kernel,
        "spectral_grads",
        block,
        (spectra, lat, w_first, b_first, w_second),
        ("near",) * 5,
        [jax.ShapeDtypeStruct((2,) + WIDE, BF), jax.ShapeDtypeStruct((CHUNKS, CHUNK_ROWS, 128), BF)],
        ("far", "near"),
        [FORM, FORM, BAND_ROWS, BAND_ROWS, pltpu.VMEM(WIDE, BF), pltpu.VMEM(WIDE, BF)]
        + [pltpu.VMEM((CHUNKS * CHUNK_ROWS, 128), F32), pltpu.VMEM((2,) + WIDE, BF)]
        + [pltpu.SemaphoreType.DMA((2,))],
    )
    kept = pltpu.with_memory_space_constraint(kept, pltpu.HBM)
    dp_size = lax.axis_size("dp")
    if dp_size == CHUNKS:
        shares = lax.all_to_all(grads, "dp", 0, 0, tiled=True)
    else:
        shares = grads
    early, late = block_call(
        return_kernel,
        "spectral_return",
        block,
        (kept, lat_t, w_first, w_second, b_second),
        ("far",) + ("near",) * 4,
        [
            jax.ShapeDtypeStruct((BANDS, PACK, 128), BF),
            jax.ShapeDtypeStruct((BANDS, 96, 128), BF),
        ],
        ("near", "far"),
        [FORM, FORM, BAND_ROWS, BAND_ROWS, COLUMNS, COLUMNS, pltpu.VMEM((2,) + WIDE, BF)]
        + [pltpu.VMEM((BANDS, 96, 128), BF)]
        + [pltpu.SemaphoreType.DMA((2,)), pltpu.SemaphoreType.DMA((4,))],
    )
    early = exchange(add_share(shares, early))
    late, early = lax.optimization_barrier((late, early))
    late = exchange(late)
    blocks = group_sums(early)
    every = lax.all_gather(blocks, "dp", axis=0, tiled=False)
    if dp_size != CHUNKS:
        every = jnp.broadcast_to(every, (CHUNKS, NB, CHUNK_ROWS, 128))
    grad_w = jax.ShapeDtypeStruct((2, NB, BS, BS), F32)
    grad_b = jax.ShapeDtypeStruct((2, C), F32)
    g_w1, g_b1, g_w2, g_b2 = spectral_call(
        grads_kernel, "grad_out", (every,), [grad_w, grad_b, grad_w, grad_b], []
    )
    result, back_fields = from_spectra(early, late, fields, cotangent, lon_fwd, lon_inv)
    return (result, back_fields, g_w1, g_b1, g_w2, g_b2)


def solution(mesh):
    placed = (P("dp", "lat", None, None), P("dp", "lat", None, None), P(), P(), P(), P())
    return jax.shard_map(
        on_device,
        mesh=mesh,
        in_specs=placed,
        out_specs=(P("dp", "lat", None, None), P("dp", "lat", None, None), P(), P(), P(), P()),
        check_vma=False,
    )
```

```python
import math

import jax
import jax.numpy as jnp
import numpy as np
from jax import lax
from jax.experimental import pallas as pl
from jax.experimental.pallas import tpu as pltpu
from jax.sharding import PartitionSpec as P

C = 768
NB = 8
BS = 96
H = 96
W = 180
KX = 64
SAMPLES = 16
EPSILON = 1e-06

BANDS = 32
GROUPS = 4
MODES = KX // GROUPS
ROWS = H // BANDS
WPAD = 192
PACK = 72
CHUNKS = 16
CHUNK_ROWS = 24
BF = jnp.bfloat16
F32 = jnp.float32
VMEM_LIMIT = 10 * 1024 * 1024


def tables():
    w_index = np.arange(W)[:, None]
    k_index = np.arange(KX)[None, :]
    lon = (2.0 * math.pi / W * (w_index * k_index % W)).astype(np.float64)
    fwd = np.stack([np.cos(lon), -np.sin(lon)], axis=1) / math.sqrt(W)
    weight = np.where(k_index == 0, 1.0, 2.0)[:, None, :]
    inv = fwd * weight
    def order(table):
        grouped = table.reshape(W, 2, GROUPS, MODES).transpose(0, 2, 1, 3).reshape(W, 2 * KX)
        padded = np.zeros((WPAD, 2 * KX))
        padded[:W] = grouped
        return padded

    h_index = np.arange(H)
    lat = 2.0 * math.pi / H * (h_index[:, None] * h_index[None, :] % H)
    cosine = np.cos(lat) / math.sqrt(H)
    sine = np.sin(lat) / math.sqrt(H)
    full = np.stack(
        [np.stack([cosine, sine], axis=2), np.stack([-sine, cosine], axis=2)], axis=0
    ).reshape(2 * H, 2 * H)
    return order(fwd), order(inv), full


LON_FWD, LON_INV, LAT = tables()


def lanes(shape):
    return lax.broadcasted_iota(jnp.int32, shape, 1)


def roll(value, shift):
    return pltpu.roll(value, shift % 128, 1)


def pack_tile(tile):
    lane = lanes((24, 128))
    tail = tile[72:96]
    return [
        jnp.where(lane < 96, tile[24 * i : 24 * i + 24], roll(tail, 96 - 32 * i))
        for i in range(3)
    ]


def unpack_tail(pieces):
    lane = lanes((24, 128))
    return jnp.where(
        lane < 32,
        roll(pieces[0], 32),
        jnp.where(lane < 64, roll(pieces[1], 64), roll(pieces[2], 96)),
    )


def block_lanes(value, block):
    start = BS * block
    first, shift = start // 128, start % 128
    head = value[:, 128 * first : 128 * first + 128]
    if shift == 0:
        return head
    head = roll(head, 128 - shift)
    if shift + BS <= 128:
        return head
    after = roll(value[:, 128 * first + 128 : 128 * first + 256], 128 - shift)
    return jnp.where(lanes(head.shape) < 128 - shift, head, after)


def join_lanes(parts):
    lane = lanes(parts[0].shape)
    return [
        jnp.where(lane < 96, parts[0], roll(parts[1], 96)),
        jnp.where(lane < 64, roll(parts[1], 96), roll(parts[2], 64)),
        jnp.where(lane < 32, roll(parts[2], 64), roll(parts[3], 32)),
    ]


ROW_CHUNKS = [(start, min(32, W - start)) for start in range(0, W, 32)]


def normalize(values):
    mean = jnp.sum(values, axis=-1, keepdims=True) * (1.0 / C)
    centered = values - mean
    spread = jnp.sum(centered * centered, axis=-1, keepdims=True) * (1.0 / C)
    scale = 1.0 / jnp.sqrt(spread + EPSILON)
    return centered * scale, scale


def send_packed(acc_ref, out_ref):
    for block in range(NB):
        rows = [block_lanes(acc_ref[r], block) for r in range(ROWS)]
        for group in range(GROUPS):
            tile = jnp.concatenate(
                [row[32 * group : 32 * group + 32] for row in rows], axis=0
            )
            pieces = pack_tile(tile)
            out_ref[block * GROUPS + group] = jnp.concatenate(pieces, axis=0).astype(BF)


def spectra_kernel(
    x_ref, g_ref, fwd_ref, inv_ref, out_ref,
    x_rows, g_rows, fwd_table, inv_table, padded_ref, acc_ref, send_ref, sems, out_sems,
):
    copies = [pltpu.make_async_copy(x_ref.at[0, 0], x_rows.at[0], sems.at[0])]
    copies += [pltpu.make_async_copy(fwd_ref, fwd_table, sems.at[1])]
    copies += [
        pltpu.make_async_copy(x_ref.at[0, r], x_rows.at[r], sems.at[1 + r])
        for r in range(1, ROWS)
    ]
    copies += [pltpu.make_async_copy(inv_ref, inv_table, sems.at[1 + ROWS])]
    copies += [
        pltpu.make_async_copy(g_ref.at[0, r], g_rows.at[r], sems.at[2 + ROWS + r])
        for r in range(ROWS)
    ]
    for copy in copies:
        copy.start()
    padded_ref[W - 20 :] = jnp.zeros((WPAD - W + 20, C), BF)
    for r in range(ROWS):
        copies[0 if r == 0 else 1 + r].wait()
        for start, size in ROW_CHUNKS:
            values = x_rows[r, start : start + size].astype(F32)
            padded_ref[start : start + size] = normalize(values)[0].astype(BF)
        if r == 0:
            copies[1].wait()
        acc_ref[r] = jnp.dot(fwd_table[...], padded_ref[...], preferred_element_type=F32)
    for copy in copies[1 + ROWS :]:
        copy.wait()
    send_packed(acc_ref, send_ref.at[0])
    fields_out = pltpu.make_async_copy(
        send_ref.at[0], out_ref.at[:, pl.ds(0, PACK), :], out_sems.at[0]
    )
    fields_out.start()
    for r in range(ROWS):
        padded_ref[0:W] = g_rows[r]
        acc_ref[r] = jnp.dot(inv_table[...], padded_ref[...], preferred_element_type=F32)
    send_packed(acc_ref, send_ref.at[1])
    back_out = pltpu.make_async_copy(
        send_ref.at[1], out_ref.at[:, pl.ds(PACK, PACK), :], out_sems.at[1]
    )
    back_out.start()
    fields_out.wait()
    back_out.wait()


def to_spectra(fields, cotangent, forward, inverse):
    held = pl.BlockSpec(memory_space=pltpu.HBM)
    return pl.pallas_call(
        spectra_kernel,
        name="to_spectra",
        in_specs=[held, held, held, held],
        out_specs=held,
        out_shape=pltpu.HBM((BANDS, 2 * PACK, 128), BF),
        scratch_shapes=[
            pltpu.VMEM((ROWS, W, C), BF),
            pltpu.VMEM((ROWS, W, C), BF),
            pltpu.VMEM((2 * KX, WPAD), BF),
            pltpu.VMEM((2 * KX, WPAD), BF),
            pltpu.VMEM((WPAD, C), BF),
            pltpu.VMEM((ROWS, 2 * KX, C), F32),
            pltpu.VMEM((2, BANDS, PACK, 128), BF),
            pltpu.SemaphoreType.DMA((2 + 2 * ROWS,)),
            pltpu.SemaphoreType.DMA((2,)),
        ],
        compiler_params=pltpu.CompilerParams(vmem_limit_bytes=VMEM_LIMIT),
        cost_estimate=pl.CostEstimate(
            flops=4 * ROWS * W * 2 * KX * C, bytes_accessed=3000000, transcendentals=0
        ),
    )(*[pltpu.with_memory_space_constraint(a, pltpu.HBM) for a in (fields, cotangent, forward, inverse)])


PITCH = 20
BAND_PITCH = 2 * ROWS * PITCH


def eight_rows(base, row):
    return pl.ds(base + PITCH * (row // MODES) + row % MODES, 8)


def unpack_bands(recv_ref, rows_ref, back_rows_ref):
    def one(s, carry):
        base = pl.multiple_of(s * BAND_PITCH, 8)
        for first, target_ref in ((0, rows_ref), (PACK, back_rows_ref)):
            pieces = [
                recv_ref[s, first + 24 * i : first + 24 * i + 24, :].astype(F32)
                for i in range(3)
            ]
            for i, piece in enumerate(pieces + [unpack_tail(pieces)]):
                for u in range(0, 24, 8):
                    target_ref[eight_rows(base, 24 * i + u), :] = piece[u : u + 8]
        return carry

    lax.fori_loop(0, BANDS, one, 0, unroll=4)


def pack_bands(rows_ref, back_rows_ref, early_ref, late_ref, first):
    def one(s, carry):
        base = pl.multiple_of(s * BAND_PITCH, 8)

        def tile(ref):
            return jnp.concatenate(
                [ref[eight_rows(base, row), :] for row in range(0, 96, 8)], axis=0
            )

        pieces = pack_tile(tile(rows_ref))
        early_ref[s, 0:48] = jnp.concatenate(pieces[:2], axis=0).astype(BF)
        back = pack_tile(tile(back_rows_ref))
        late_ref[s] = jnp.concatenate(pieces[2:] + back, axis=0).astype(BF)
        return carry

    lax.fori_loop(first, first + BANDS // 4, one, 0, unroll=4)


def mode_rows(rows_ref, lat, pair):
    columns = jnp.concatenate(
        [
            rows_ref[pl.ds(2 * pair + j, 2 * H, stride=PITCH), :].astype(BF)
            for j in range(2)
        ],
        axis=1,
    )
    done = jnp.dot(lat, columns, preferred_element_type=F32).astype(BF)
    return jnp.concatenate(
        [
            jnp.concatenate(
                [done[0:H, 128 * j : 128 * j + 128], done[H : 2 * H, 128 * j : 128 * j + 128]],
                axis=1,
            )
            for j in range(2)
        ],
        axis=0,
    )


def spread(columns_ref, pair, modes):
    for j in range(2):
        lane = 128 * (2 * pair + j)
        for part in range(2):
            columns_ref[H * part : H * part + H, lane : lane + 128] = modes[
                H * j : H * j + H, 128 * part : 128 * part + 128
            ]


def store_rows(rows_ref, lat_t, columns_ref, pair):
    done = jnp.dot(
        lat_t, columns_ref[:, 256 * pair : 256 * pair + 256], preferred_element_type=F32
    )
    for j in range(2):
        rows_ref[pl.ds(2 * pair + j, 2 * H, stride=PITCH), :] = done[:, 128 * j : 128 * j + 128]


def fill_weight(weight_ref, block, form_ref):
    form_ref[...] = jnp.zeros_like(form_ref)
    real = weight_ref[0, block]
    imag = weight_ref[1, block]
    form_ref[0:BS, 0:BS] = real
    form_ref[0:BS, 128 : 128 + BS] = imag
    form_ref[128 : 128 + BS, 0:BS] = -imag
    form_ref[128 : 128 + BS, 128 : 128 + BS] = real


def choose_bias(block, bias_ref):
    bias = bias_ref[...]
    chosen = block_lanes(bias, 0)
    for other in range(1, NB):
        chosen = jnp.where(block == other, block_lanes(bias, other), chosen)
    chosen = jnp.where(lanes(chosen.shape) < BS, chosen, 0.0)
    return jnp.concatenate([chosen[0:1], chosen[1:2]], axis=1)


NT = (((1,), (1,)), ((), ()))
TN = (((0,), (0,)), ((), ()))


def with_one(value):
    return jnp.where(lanes(value.shape) == BS, jnp.ones_like(value), value)


def half_copy(source_ref, target_ref, sems, half):
    rows = pl.ds(HALF_PAIRS * PAIR_ROWS * half, HALF_PAIRS * PAIR_ROWS)
    return pltpu.make_async_copy(
        source_ref.at[:, rows, :], target_ref.at[:, rows, :], sems.at[half]
    )


def gradient_kernel(
    block_ref, recv_ref, lat_ref, first_ref, bias_ref, second_ref,
    saved_ref, grad_ref,
    w1_ref, w2_ref, rows_ref, back_rows_ref, modes_ref, filtered_ref, sums_ref, kept_ref, sems,
):
    block = block_ref[0]
    fill_weight(first_ref, block, w1_ref)
    fill_weight(second_ref, block, w2_ref)
    bias = choose_bias(block, bias_ref)
    unpack_bands(recv_ref, rows_ref, back_rows_ref)
    lat = lat_ref[...]
    w1 = w1_ref[...]
    w2 = w2_ref[...]
    saves = []
    for pair in range(PAIRS):
        span = slice(PAIR_ROWS * pair, PAIR_ROWS * pair + PAIR_ROWS)
        modes = mode_rows(rows_ref, lat, pair)
        modes = jnp.concatenate([with_one(modes[:, 0:128]), modes[:, 128:256]], axis=1)
        modes_ref[span] = modes
        pre = jnp.dot(modes, w1, preferred_element_type=F32) + bias
        cdf = 0.5 + 0.5 * lax.erf(pre * math.sqrt(0.5))
        hidden = (pre * cdf).astype(BF)
        hidden = jnp.concatenate([with_one(hidden[:, 0:128]), hidden[:, 128:256]], axis=1)
        kept_ref[0, span] = hidden
        slope = cdf + pre * (jnp.exp(-0.5 * pre * pre) * (1.0 / math.sqrt(2.0 * math.pi)))
        back_filtered = mode_rows(back_rows_ref, lat, pair)
        filtered_ref[span] = back_filtered
        back_hidden = lax.dot_general(back_filtered, w2, NT, preferred_element_type=F32)
        kept_ref[1, span] = (back_hidden * slope).astype(BF)
        if (pair + 1) % HALF_PAIRS == 0:
            save = half_copy(kept_ref, saved_ref, sems, pair // HALF_PAIRS)
            save.start()
            saves.append(save)
    row = 0
    bias_rows = []
    for left_ref, right_ref in ((modes_ref, kept_ref.at[1]), (kept_ref.at[0], filtered_ref)):
        right = right_ref[...]
        gathered = lax.dot_general(left_ref[...], right, TN, preferred_element_type=F32)
        real = gathered[0:BS, 0:128] + gathered[128 : 128 + BS, 128:256]
        imag = gathered[0:BS, 128:256] - gathered[128 : 128 + BS, 0:128]
        for part in (real, imag):
            for piece in pack_tile(part):
                sums_ref[row : row + 24] = piece
                row += 24
        bias_rows += [gathered[BS : BS + 8, 0:128], gathered[BS : BS + 8, 128:256]]
    for value in bias_rows:
        sums_ref[row : row + 8] = value
        row += 8
    sums_ref[row:] = jnp.zeros((CHUNKS * CHUNK_ROWS - row, 128), F32)
    for chunk in range(CHUNKS):
        grad_ref[chunk] = sums_ref[CHUNK_ROWS * chunk : CHUNK_ROWS * chunk + CHUNK_ROWS].astype(
            BF
        )
    for save in saves:
        save.wait()


def return_kernel(
    block_ref, saved_ref, lat_ref, first_ref, second_ref, bias_ref,
    early_ref, sent_ref,
    w1_ref, w2_ref, rows_ref, back_rows_ref, columns_ref, back_columns_ref,
    kept_ref, late_ref, sems, out_sems,
):
    fetches = [half_copy(saved_ref, kept_ref, sems, half) for half in range(2)]
    for fetch in fetches:
        fetch.start()
    block = block_ref[0]
    fill_weight(first_ref, block, w1_ref)
    fill_weight(second_ref, block, w2_ref)
    bias = choose_bias(block, bias_ref)
    lat_t = lat_ref[...]
    w1 = w1_ref[...]
    w2 = w2_ref[...]
    for pair in range(PAIRS):
        span = slice(PAIR_ROWS * pair, PAIR_ROWS * pair + PAIR_ROWS)
        if pair % HALF_PAIRS == 0:
            fetches[pair // HALF_PAIRS].wait()
        filtered = jnp.dot(kept_ref[0, span], w2, preferred_element_type=F32) + bias
        spread(columns_ref, pair, filtered.astype(BF))
        back_modes = lax.dot_general(kept_ref[1, span], w1, NT, preferred_element_type=F32)
        spread(back_columns_ref, pair, back_modes.astype(BF))
    for pair in range(PAIRS):
        store_rows(rows_ref, lat_t, columns_ref, pair)
        store_rows(back_rows_ref, lat_t, back_columns_ref, pair)
    leaving = []
    for part in range(4):
        pack_bands(rows_ref, back_rows_ref, early_ref, late_ref, part * (BANDS // 4))
        bands = pl.ds(part * (BANDS // 4), BANDS // 4)
        copy = pltpu.make_async_copy(
            late_ref.at[bands], sent_ref.at[bands], out_sems.at[part]
        )
        copy.start()
        leaving.append(copy)
    for copy in leaving:
        copy.wait()


PAIR_ROWS = 2 * H
PAIRS = MODES // 2
HALF_PAIRS = PAIRS // 2
WIDE = (MODES * H, 256)
FORM = pltpu.VMEM((256, 256), BF)
COLUMNS = pltpu.VMEM((2 * H, MODES * 128), BF)
BAND_ROWS = pltpu.VMEM((2 * H * PITCH, 128), F32)


def block_call(kernel, name, block, operands, operand_places, outs, places, scratch):
    return pl.pallas_call(
        kernel,
        name=name,
        grid_spec=pltpu.PrefetchScalarGridSpec(
            num_scalar_prefetch=1,
            grid=(1,),
            in_specs=[
                pl.BlockSpec(memory_space=pltpu.HBM if place == "far" else pltpu.VMEM)
                for place in operand_places
            ],
            out_specs=[
                pl.BlockSpec(memory_space=pltpu.HBM if place == "far" else pltpu.VMEM)
                for place in places
            ],
            scratch_shapes=scratch,
        ),
        out_shape=[
            pltpu.HBM(out.shape, out.dtype) if place == "far" else out
            for out, place in zip(outs, places)
        ],
        compiler_params=pltpu.CompilerParams(vmem_limit_bytes=14 * 1024 * 1024),
        cost_estimate=pl.CostEstimate(
            flops=1000000000, bytes_accessed=6000000, transcendentals=800000
        ),
    )(block, *operands)


def receive(parts, rows_ref):
    for group in range(GROUPS):
        for quad in range(2):
            tiles = []
            for block in range(4):
                band = (4 * quad + block) * GROUPS + group
                pieces = [ref[band, at : at + 24, :].astype(F32) for ref, at in parts]
                tiles.append(
                    jnp.concatenate(pieces + [unpack_tail(pieces)], axis=0).astype(BF)
                )
            for t, joined in enumerate(join_lanes(tiles)):
                for r in range(ROWS):
                    rows_ref[
                        r,
                        32 * group : 32 * group + 32,
                        384 * quad + 128 * t : 384 * quad + 128 * t + 128,
                    ] = joined[32 * r : 32 * r + 32]


def output_kernel(
    early_ref, late_ref, x_ref, g_ref, fwd_ref, inv_ref,
    out_ref, grad_ref,
    rows_ref, back_rows_ref, mixed_ref, back_ref,
):
    r = pl.program_id(0)

    @pl.when(r == 0)
    def _():
        receive(((early_ref, 0), (early_ref, 24), (late_ref, 0)), rows_ref)
        receive(((late_ref, 24), (late_ref, 48), (late_ref, 72)), back_rows_ref)

    mixed_ref[...] = jnp.dot(inv_ref[...], rows_ref[r], preferred_element_type=F32)
    back_ref[...] = jnp.dot(fwd_ref[...], back_rows_ref[r], preferred_element_type=F32)
    for start, size in ROW_CHUNKS:
        span = slice(start, start + size)
        values = x_ref[0, r, span].astype(F32)
        normed, scale = normalize(values)
        out_ref[0, 0, span] = (values + normed + mixed_ref[span]).astype(BF)
        upstream = g_ref[0, r, span].astype(F32)
        back = upstream + back_ref[span]
        mean = jnp.sum(back, axis=-1, keepdims=True) * (1.0 / C)
        along = jnp.sum(back * normed, axis=-1, keepdims=True) * (1.0 / C)
        grad_ref[0, 0, span] = (upstream + scale * (back - mean - normed * along)).astype(BF)


def from_spectra(early, late, fields, cotangent, forward, inverse):
    token_spec = pl.BlockSpec((1, 1, W, C), lambda r: (0, r, 0, 0))
    near = pl.BlockSpec(memory_space=pltpu.VMEM)
    token = jax.ShapeDtypeStruct((1, ROWS, W, C), BF)
    return pl.pallas_call(
        output_kernel,
        name="from_spectra",
        grid=(ROWS,),
        in_specs=[near] * 6,
        out_specs=[token_spec, token_spec],
        out_shape=[token, token],
        scratch_shapes=[
            pltpu.VMEM((ROWS, 2 * KX, C), BF),
            pltpu.VMEM((ROWS, 2 * KX, C), BF),
            pltpu.VMEM((WPAD, C), F32),
            pltpu.VMEM((WPAD, C), F32),
        ],
        compiler_params=pltpu.CompilerParams(
            vmem_limit_bytes=VMEM_LIMIT,
        ),
        cost_estimate=pl.CostEstimate(
            flops=4 * ROWS * W * 2 * KX * C, bytes_accessed=5000000, transcendentals=0
        ),
    )(early, late, fields, cotangent, forward, inverse)


def whole(shape):
    return pl.BlockSpec(shape, lambda: (0,) * len(shape))


def spectral_call(kernel, name, operands, outs, scratch):
    return pl.pallas_call(
        kernel,
        name=name,
        in_specs=[whole(operand.shape) for operand in operands],
        out_specs=[whole(out.shape) for out in outs],
        out_shape=outs,
        scratch_shapes=scratch,
        compiler_params=pltpu.CompilerParams(vmem_limit_bytes=VMEM_LIMIT),
        cost_estimate=pl.CostEstimate(
            flops=1000000, bytes_accessed=1000000, transcendentals=0
        ),
    )(*operands)


def share_kernel(recv_ref, held_ref, out_ref):
    total = recv_ref[0].astype(F32)
    for i in range(1, recv_ref.shape[0]):
        total = total + recv_ref[i].astype(F32)
    share = total.astype(BF)
    for band in range(BANDS):
        out_ref[band] = share


def add_share(shares, held):
    return pl.pallas_call(
        share_kernel,
        name="grad_share",
        grid=(1,),
        in_specs=[
            pl.BlockSpec(shares.shape, lambda i: (0, 0, 0)),
            pl.BlockSpec(memory_space=pl.ANY),
        ],
        out_specs=pl.BlockSpec((BANDS, CHUNK_ROWS, 128), lambda i: (0, 2, 0)),
        out_shape=jax.ShapeDtypeStruct(held.shape, BF),
        input_output_aliases={1: 0},
        compiler_params=pltpu.CompilerParams(vmem_limit_bytes=VMEM_LIMIT),
    )(shares, held)


def group_sum_kernel(recv_ref, out_ref):
    for block in range(NB):
        total = recv_ref[block * GROUPS].astype(F32)
        for group in range(1, GROUPS):
            total = total + recv_ref[block * GROUPS + group].astype(F32)
        out_ref[block] = total.astype(BF)


def group_sums(message):
    return pl.pallas_call(
        group_sum_kernel,
        name="grad_groups",
        grid=(1,),
        in_specs=[pl.BlockSpec((BANDS, CHUNK_ROWS, 128), lambda i: (0, 2, 0))],
        out_specs=pl.BlockSpec((NB, CHUNK_ROWS, 128), lambda i: (0, 0, 0)),
        out_shape=jax.ShapeDtypeStruct((NB, CHUNK_ROWS, 128), BF),
        compiler_params=pltpu.CompilerParams(vmem_limit_bytes=VMEM_LIMIT),
    )(message)


GRAD_SCALE = 1.0 / (SAMPLES * H)


def grads_kernel(recv_ref, w1_ref, b1_ref, w2_ref, b2_ref):
    for block in range(NB):
        chunk = 0
        for out_ref in (w1_ref, w2_ref):
            for part in range(2):
                pieces = [
                    recv_ref[chunk + i, block].astype(F32) * GRAD_SCALE for i in range(3)
                ]
                chunk += 3
                for i in range(3):
                    out_ref[part, block, 24 * i : 24 * i + 24, :] = pieces[i][:, :BS]
                out_ref[part, block, 72:96, :] = unpack_tail(pieces)[:, :BS]
    rows = [
        jnp.concatenate([recv_ref[12, block], recv_ref[13, block]], axis=0).astype(F32)
        * GRAD_SCALE
        for block in range(NB)
    ]
    for out_ref, first in ((b1_ref, 0), (b2_ref, 16)):
        for part in range(2):
            at = first + 8 * part
            for quad in range(2):
                parts = [rows[4 * quad + j][at : at + 8] for j in range(4)]
                for t, joined in enumerate(join_lanes(parts)):
                    lane = 384 * quad + 128 * t
                    out_ref[part : part + 1, lane : lane + 128] = joined[0:1]


def exchange(value):
    return lax.all_to_all(value, "lat", split_axis=0, concat_axis=0, tiled=True)


def on_device(fields, cotangent, w_first, b_first, w_second, b_second):
    block = (lax.axis_index("lat") // GROUPS).astype(jnp.int32).reshape(1)
    lon_fwd = jnp.asarray(LON_FWD, BF)
    lon_inv = jnp.asarray(LON_INV, BF)
    lon_fwd_t = jnp.asarray(LON_FWD.T, BF)
    lon_inv_t = jnp.asarray(LON_INV.T, BF)
    lat = jnp.asarray(LAT, BF)
    lat_t = jnp.asarray(LAT.T, BF)

    spectra = to_spectra(fields, cotangent, lon_fwd_t, lon_inv_t)
    spectra = exchange(spectra)
    kept, grads = block_call(
        gradient_kernel,
        "spectral_grads",
        block,
        (spectra, lat, w_first, b_first, w_second),
        ("near",) * 5,
        [jax.ShapeDtypeStruct((2,) + WIDE, BF), jax.ShapeDtypeStruct((CHUNKS, CHUNK_ROWS, 128), BF)],
        ("far", "near"),
        [FORM, FORM, BAND_ROWS, BAND_ROWS, pltpu.VMEM(WIDE, BF), pltpu.VMEM(WIDE, BF)]
        + [pltpu.VMEM((CHUNKS * CHUNK_ROWS, 128), F32), pltpu.VMEM((2,) + WIDE, BF)]
        + [pltpu.SemaphoreType.DMA((2,))],
    )
    kept = pltpu.with_memory_space_constraint(kept, pltpu.HBM)
    dp_size = lax.axis_size("dp")
    if dp_size == CHUNKS:
        shares = lax.all_to_all(grads, "dp", 0, 0, tiled=True)
    else:
        shares = grads
    early, late = block_call(
        return_kernel,
        "spectral_return",
        block,
        (kept, lat_t, w_first, w_second, b_second),
        ("far",) + ("near",) * 4,
        [
            jax.ShapeDtypeStruct((BANDS, PACK, 128), BF),
            jax.ShapeDtypeStruct((BANDS, 96, 128), BF),
        ],
        ("near", "far"),
        [FORM, FORM, BAND_ROWS, BAND_ROWS, COLUMNS, COLUMNS, pltpu.VMEM((2,) + WIDE, BF)]
        + [pltpu.VMEM((BANDS, 96, 128), BF)]
        + [pltpu.SemaphoreType.DMA((2,)), pltpu.SemaphoreType.DMA((4,))],
    )
    early = exchange(add_share(shares, early))
    late, early = lax.optimization_barrier((late, early))
    late = exchange(late)
    blocks = group_sums(early)
    every = lax.all_gather(blocks, "dp", axis=0, tiled=False)
    if dp_size != CHUNKS:
        every = jnp.broadcast_to(every, (CHUNKS, NB, CHUNK_ROWS, 128))
    grad_w = jax.ShapeDtypeStruct((2, NB, BS, BS), F32)
    grad_b = jax.ShapeDtypeStruct((2, C), F32)
    g_w1, g_b1, g_w2, g_b2 = spectral_call(
        grads_kernel, "grad_out", (every,), [grad_w, grad_b, grad_w, grad_b], []
    )
    result, back_fields = from_spectra(early, late, fields, cotangent, lon_fwd, lon_inv)
    return (result, back_fields, g_w1, g_b1, g_w2, g_b2)


def solution(mesh):
    placed = (P("dp", "lat", None, None), P("dp", "lat", None, None), P(), P(), P(), P())
    return jax.shard_map(
        on_device,
        mesh=mesh,
        in_specs=placed,
        out_specs=(P("dp", "lat", None, None), P("dp", "lat", None, None), P(), P(), P(), P()),
        check_vma=False,
    )
```

```python
import math

import jax
import jax.numpy as jnp
import numpy as np
from jax import lax
from jax.experimental import pallas as pl
from jax.experimental.pallas import tpu as pltpu
from jax.sharding import PartitionSpec as P

C = 768
NB = 8
BS = 96
H = 96
W = 180
KX = 64
SAMPLES = 16
EPSILON = 1e-06

BANDS = 32
GROUPS = 4
MODES = KX // GROUPS
ROWS = H // BANDS
WPAD = 192
PACK = 72
CHUNKS = 16
CHUNK_ROWS = 24
BF = jnp.bfloat16
F32 = jnp.float32
VMEM_LIMIT = 10 * 1024 * 1024


def tables():
    w_index = np.arange(W)[:, None]
    k_index = np.arange(KX)[None, :]
    lon = (2.0 * math.pi / W * (w_index * k_index % W)).astype(np.float64)
    fwd = np.stack([np.cos(lon), -np.sin(lon)], axis=1) / math.sqrt(W)
    weight = np.where(k_index == 0, 1.0, 2.0)[:, None, :]
    inv = fwd * weight
    def order(table):
        grouped = table.reshape(W, 2, GROUPS, MODES).transpose(0, 2, 1, 3).reshape(W, 2 * KX)
        padded = np.zeros((WPAD, 2 * KX))
        padded[:W] = grouped
        return padded

    h_index = np.arange(H)
    lat = 2.0 * math.pi / H * (h_index[:, None] * h_index[None, :] % H)
    cosine = np.cos(lat) / math.sqrt(H)
    sine = np.sin(lat) / math.sqrt(H)
    full = np.stack(
        [np.stack([cosine, sine], axis=2), np.stack([-sine, cosine], axis=2)], axis=0
    ).reshape(2 * H, 2 * H)
    return order(fwd), order(inv), full


LON_FWD, LON_INV, LAT = tables()


def lanes(shape):
    return lax.broadcasted_iota(jnp.int32, shape, 1)


def roll(value, shift):
    return pltpu.roll(value, shift % 128, 1)


def pack_tile(tile):
    lane = lanes((24, 128))
    tail = tile[72:96]
    return [
        jnp.where(lane < 96, tile[24 * i : 24 * i + 24], roll(tail, 96 - 32 * i))
        for i in range(3)
    ]


def unpack_tail(pieces):
    lane = lanes((24, 128))
    return jnp.where(
        lane < 32,
        roll(pieces[0], 32),
        jnp.where(lane < 64, roll(pieces[1], 64), roll(pieces[2], 96)),
    )


def block_lanes(value, block):
    start = BS * block
    first, shift = start // 128, start % 128
    head = value[:, 128 * first : 128 * first + 128]
    if shift == 0:
        return head
    head = roll(head, 128 - shift)
    if shift + BS <= 128:
        return head
    after = roll(value[:, 128 * first + 128 : 128 * first + 256], 128 - shift)
    return jnp.where(lanes(head.shape) < 128 - shift, head, after)


def join_lanes(parts):
    lane = lanes(parts[0].shape)
    return [
        jnp.where(lane < 96, parts[0], roll(parts[1], 96)),
        jnp.where(lane < 64, roll(parts[1], 96), roll(parts[2], 64)),
        jnp.where(lane < 32, roll(parts[2], 64), roll(parts[3], 32)),
    ]


ROW_CHUNKS = [(start, min(32, W - start)) for start in range(0, W, 32)]


def normalize(values):
    mean = jnp.sum(values, axis=-1, keepdims=True) * (1.0 / C)
    centered = values - mean
    spread = jnp.sum(centered * centered, axis=-1, keepdims=True) * (1.0 / C)
    scale = 1.0 / jnp.sqrt(spread + EPSILON)
    return centered * scale, scale


def send_packed(acc_ref, out_ref):
    for block in range(NB):
        rows = [block_lanes(acc_ref[r], block) for r in range(ROWS)]
        for group in range(GROUPS):
            tile = jnp.concatenate(
                [row[32 * group : 32 * group + 32] for row in rows], axis=0
            )
            pieces = pack_tile(tile)
            out_ref[block * GROUPS + group] = jnp.concatenate(pieces, axis=0).astype(BF)


def spectra_kernel(
    x_ref, g_ref, fwd_ref, inv_ref, out_ref,
    x_rows, g_rows, fwd_table, inv_table, padded_ref, acc_ref, send_ref, sems, out_sems,
):
    copies = [pltpu.make_async_copy(x_ref.at[0, 0], x_rows.at[0], sems.at[0])]
    copies += [pltpu.make_async_copy(fwd_ref, fwd_table, sems.at[1])]
    copies += [
        pltpu.make_async_copy(x_ref.at[0, r], x_rows.at[r], sems.at[1 + r])
        for r in range(1, ROWS)
    ]
    copies += [pltpu.make_async_copy(inv_ref, inv_table, sems.at[1 + ROWS])]
    copies += [
        pltpu.make_async_copy(g_ref.at[0, r], g_rows.at[r], sems.at[2 + ROWS + r])
        for r in range(ROWS)
    ]
    for copy in copies:
        copy.start()
    padded_ref[W - 20 :] = jnp.zeros((WPAD - W + 20, C), BF)
    for r in range(ROWS):
        copies[0 if r == 0 else 1 + r].wait()
        for start, size in ROW_CHUNKS:
            values = x_rows[r, start : start + size].astype(F32)
            padded_ref[start : start + size] = normalize(values)[0].astype(BF)
        if r == 0:
            copies[1].wait()
        acc_ref[r] = jnp.dot(fwd_table[...], padded_ref[...], preferred_element_type=F32)
    for copy in copies[1 + ROWS :]:
        copy.wait()
    send_packed(acc_ref, send_ref.at[0])
    fields_out = pltpu.make_async_copy(
        send_ref.at[0], out_ref.at[:, pl.ds(0, PACK), :], out_sems.at[0]
    )
    fields_out.start()
    for r in range(ROWS):
        padded_ref[0:W] = g_rows[r]
        acc_ref[r] = jnp.dot(inv_table[...], padded_ref[...], preferred_element_type=F32)
    send_packed(acc_ref, send_ref.at[1])
    back_out = pltpu.make_async_copy(
        send_ref.at[1], out_ref.at[:, pl.ds(PACK, PACK), :], out_sems.at[1]
    )
    back_out.start()
    fields_out.wait()
    back_out.wait()


def to_spectra(fields, cotangent, forward, inverse):
    held = pl.BlockSpec(memory_space=pltpu.HBM)
    return pl.pallas_call(
        spectra_kernel,
        name="to_spectra",
        in_specs=[held, held, held, held],
        out_specs=held,
        out_shape=pltpu.HBM((BANDS, 2 * PACK, 128), BF),
        scratch_shapes=[
            pltpu.VMEM((ROWS, W, C), BF),
            pltpu.VMEM((ROWS, W, C), BF),
            pltpu.VMEM((2 * KX, WPAD), BF),
            pltpu.VMEM((2 * KX, WPAD), BF),
            pltpu.VMEM((WPAD, C), BF),
            pltpu.VMEM((ROWS, 2 * KX, C), F32),
            pltpu.VMEM((2, BANDS, PACK, 128), BF),
            pltpu.SemaphoreType.DMA((2 + 2 * ROWS,)),
            pltpu.SemaphoreType.DMA((2,)),
        ],
        compiler_params=pltpu.CompilerParams(vmem_limit_bytes=VMEM_LIMIT),
        cost_estimate=pl.CostEstimate(
            flops=4 * ROWS * W * 2 * KX * C, bytes_accessed=3000000, transcendentals=0
        ),
    )(*[pltpu.with_memory_space_constraint(a, pltpu.HBM) for a in (fields, cotangent, forward, inverse)])


PITCH = 20
BAND_PITCH = 2 * ROWS * PITCH


def eight_rows(base, row):
    return pl.ds(base + PITCH * (row // MODES) + row % MODES, 8)


def unpack_bands(recv_ref, rows_ref, back_rows_ref):
    def one(s, carry):
        base = pl.multiple_of(s * BAND_PITCH, 8)
        for first, target_ref in ((0, rows_ref), (PACK, back_rows_ref)):
            pieces = [
                recv_ref[s, first + 24 * i : first + 24 * i + 24, :].astype(F32)
                for i in range(3)
            ]
            for i, piece in enumerate(pieces + [unpack_tail(pieces)]):
                for u in range(0, 24, 8):
                    target_ref[eight_rows(base, 24 * i + u), :] = piece[u : u + 8]
        return carry

    lax.fori_loop(0, BANDS, one, 0, unroll=4)


def pack_bands(rows_ref, back_rows_ref, early_ref, late_ref, first):
    def one(s, carry):
        base = pl.multiple_of(s * BAND_PITCH, 8)

        def tile(ref):
            return jnp.concatenate(
                [ref[eight_rows(base, row), :] for row in range(0, 96, 8)], axis=0
            )

        pieces = pack_tile(tile(rows_ref))
        early_ref[s, 0:48] = jnp.concatenate(pieces[:2], axis=0).astype(BF)
        back = pack_tile(tile(back_rows_ref))
        late_ref[s] = jnp.concatenate(pieces[2:] + back, axis=0).astype(BF)
        return carry

    lax.fori_loop(first, first + BANDS // 4, one, 0, unroll=4)


def mode_rows(rows_ref, lat, pair):
    columns = jnp.concatenate(
        [
            rows_ref[pl.ds(2 * pair + j, 2 * H, stride=PITCH), :].astype(BF)
            for j in range(2)
        ],
        axis=1,
    )
    done = jnp.dot(lat, columns, preferred_element_type=F32).astype(BF)
    return jnp.concatenate(
        [
            jnp.concatenate(
                [done[0:H, 128 * j : 128 * j + 128], done[H : 2 * H, 128 * j : 128 * j + 128]],
                axis=1,
            )
            for j in range(2)
        ],
        axis=0,
    )


def spread(columns_ref, pair, modes):
    for j in range(2):
        lane = 128 * (2 * pair + j)
        for part in range(2):
            columns_ref[H * part : H * part + H, lane : lane + 128] = modes[
                H * j : H * j + H, 128 * part : 128 * part + 128
            ]


def store_rows(rows_ref, lat_t, columns_ref, pair):
    done = jnp.dot(
        lat_t, columns_ref[:, 256 * pair : 256 * pair + 256], preferred_element_type=F32
    )
    for j in range(2):
        rows_ref[pl.ds(2 * pair + j, 2 * H, stride=PITCH), :] = done[:, 128 * j : 128 * j + 128]


def fill_weight(weight_ref, block, form_ref):
    form_ref[...] = jnp.zeros_like(form_ref)
    real = weight_ref[0, block]
    imag = weight_ref[1, block]
    form_ref[0:BS, 0:BS] = real
    form_ref[0:BS, 128 : 128 + BS] = imag
    form_ref[128 : 128 + BS, 0:BS] = -imag
    form_ref[128 : 128 + BS, 128 : 128 + BS] = real


def choose_bias(block, bias_ref):
    bias = bias_ref[...]
    chosen = block_lanes(bias, 0)
    for other in range(1, NB):
        chosen = jnp.where(block == other, block_lanes(bias, other), chosen)
    chosen = jnp.where(lanes(chosen.shape) < BS, chosen, 0.0)
    return jnp.concatenate([chosen[0:1], chosen[1:2]], axis=1)


NT = (((1,), (1,)), ((), ()))
TN = (((0,), (0,)), ((), ()))


def with_one(value):
    return jnp.where(lanes(value.shape) == BS, jnp.ones_like(value), value)


def half_copy(source_ref, target_ref, sems, half):
    rows = pl.ds(HALF_PAIRS * PAIR_ROWS * half, HALF_PAIRS * PAIR_ROWS)
    return pltpu.make_async_copy(
        source_ref.at[:, rows, :], target_ref.at[:, rows, :], sems.at[half]
    )


def gradient_kernel(
    block_ref, recv_ref, lat_ref, first_ref, bias_ref, second_ref,
    saved_ref, grad_ref,
    w1_ref, w2_ref, rows_ref, back_rows_ref, modes_ref, filtered_ref, sums_ref, kept_ref, sems,
):
    block = block_ref[0]
    fill_weight(first_ref, block, w1_ref)
    fill_weight(second_ref, block, w2_ref)
    bias = choose_bias(block, bias_ref)
    unpack_bands(recv_ref, rows_ref, back_rows_ref)
    lat = lat_ref[...]
    w1 = w1_ref[...]
    w2 = w2_ref[...]
    saves = []
    for pair in range(PAIRS):
        span = slice(PAIR_ROWS * pair, PAIR_ROWS * pair + PAIR_ROWS)
        modes = mode_rows(rows_ref, lat, pair)
        modes = jnp.concatenate([with_one(modes[:, 0:128]), modes[:, 128:256]], axis=1)
        modes_ref[span] = modes
        pre = jnp.dot(modes, w1, preferred_element_type=F32) + bias
        cdf = 0.5 + 0.5 * lax.erf(pre * math.sqrt(0.5))
        hidden = (pre * cdf).astype(BF)
        hidden = jnp.concatenate([with_one(hidden[:, 0:128]), hidden[:, 128:256]], axis=1)
        kept_ref[0, span] = hidden
        slope = cdf + pre * (jnp.exp(-0.5 * pre * pre) * (1.0 / math.sqrt(2.0 * math.pi)))
        back_filtered = mode_rows(back_rows_ref, lat, pair)
        filtered_ref[span] = back_filtered
        back_hidden = lax.dot_general(back_filtered, w2, NT, preferred_element_type=F32)
        kept_ref[1, span] = (back_hidden * slope).astype(BF)
        if (pair + 1) % HALF_PAIRS == 0:
            save = half_copy(kept_ref, saved_ref, sems, pair // HALF_PAIRS)
            save.start()
            saves.append(save)
    row = 0
    bias_rows = []
    for left_ref, right_ref in ((modes_ref, kept_ref.at[1]), (kept_ref.at[0], filtered_ref)):
        right = right_ref[...]
        gathered = lax.dot_general(left_ref[...], right, TN, preferred_element_type=F32)
        real = gathered[0:BS, 0:128] + gathered[128 : 128 + BS, 128:256]
        imag = gathered[0:BS, 128:256] - gathered[128 : 128 + BS, 0:128]
        for part in (real, imag):
            for piece in pack_tile(part):
                sums_ref[row : row + 24] = piece
                row += 24
        bias_rows += [gathered[BS : BS + 8, 0:128], gathered[BS : BS + 8, 128:256]]
    for value in bias_rows:
        sums_ref[row : row + 8] = value
        row += 8
    sums_ref[row:] = jnp.zeros((CHUNKS * CHUNK_ROWS - row, 128), F32)
    for chunk in range(CHUNKS):
        grad_ref[chunk] = sums_ref[CHUNK_ROWS * chunk : CHUNK_ROWS * chunk + CHUNK_ROWS].astype(
            BF
        )
    for save in saves:
        save.wait()


def return_kernel(
    block_ref, saved_ref, lat_ref, first_ref, second_ref, bias_ref,
    early_ref, sent_ref,
    w1_ref, w2_ref, rows_ref, back_rows_ref, columns_ref, back_columns_ref,
    kept_ref, late_ref, sems, out_sems,
):
    fetches = [half_copy(saved_ref, kept_ref, sems, half) for half in range(2)]
    for fetch in fetches:
        fetch.start()
    block = block_ref[0]
    fill_weight(first_ref, block, w1_ref)
    fill_weight(second_ref, block, w2_ref)
    bias = choose_bias(block, bias_ref)
    lat_t = lat_ref[...]
    w1 = w1_ref[...]
    w2 = w2_ref[...]
    for pair in range(PAIRS):
        span = slice(PAIR_ROWS * pair, PAIR_ROWS * pair + PAIR_ROWS)
        if pair % HALF_PAIRS == 0:
            fetches[pair // HALF_PAIRS].wait()
        filtered = jnp.dot(kept_ref[0, span], w2, preferred_element_type=F32) + bias
        spread(columns_ref, pair, filtered.astype(BF))
        back_modes = lax.dot_general(kept_ref[1, span], w1, NT, preferred_element_type=F32)
        spread(back_columns_ref, pair, back_modes.astype(BF))
    for pair in range(PAIRS):
        store_rows(rows_ref, lat_t, columns_ref, pair)
        store_rows(back_rows_ref, lat_t, back_columns_ref, pair)
    leaving = []
    for part in range(4):
        pack_bands(rows_ref, back_rows_ref, early_ref, late_ref, part * (BANDS // 4))
        bands = pl.ds(part * (BANDS // 4), BANDS // 4)
        copy = pltpu.make_async_copy(
            late_ref.at[bands], sent_ref.at[bands], out_sems.at[part]
        )
        copy.start()
        leaving.append(copy)
    for copy in leaving:
        copy.wait()


PAIR_ROWS = 2 * H
PAIRS = MODES // 2
HALF_PAIRS = PAIRS // 2
WIDE = (MODES * H, 256)
FORM = pltpu.VMEM((256, 256), BF)
COLUMNS = pltpu.VMEM((2 * H, MODES * 128), BF)
BAND_ROWS = pltpu.VMEM((2 * H * PITCH, 128), F32)


def block_call(kernel, name, block, operands, operand_places, outs, places, scratch):
    return pl.pallas_call(
        kernel,
        name=name,
        grid_spec=pltpu.PrefetchScalarGridSpec(
            num_scalar_prefetch=1,
            grid=(1,),
            in_specs=[
                pl.BlockSpec(memory_space=pltpu.HBM if place == "far" else pltpu.VMEM)
                for place in operand_places
            ],
            out_specs=[
                pl.BlockSpec(out.shape, lambda i, n, d=len(out.shape): (0,) * d)
                if place == "window"
                else pl.BlockSpec(memory_space=pltpu.HBM if place == "far" else pltpu.VMEM)
                for out, place in zip(outs, places)
            ],
            scratch_shapes=scratch,
        ),
        out_shape=[
            pltpu.HBM(out.shape, out.dtype) if place == "far" else out
            for out, place in zip(outs, places)
        ],
        compiler_params=pltpu.CompilerParams(vmem_limit_bytes=14 * 1024 * 1024),
        cost_estimate=pl.CostEstimate(
            flops=1000000000, bytes_accessed=6000000, transcendentals=800000
        ),
    )(block, *operands)


def receive(parts, rows_ref):
    for group in range(GROUPS):
        for quad in range(2):
            tiles = []
            for block in range(4):
                band = (4 * quad + block) * GROUPS + group
                pieces = [ref[band, at : at + 24, :].astype(F32) for ref, at in parts]
                tiles.append(
                    jnp.concatenate(pieces + [unpack_tail(pieces)], axis=0).astype(BF)
                )
            for t, joined in enumerate(join_lanes(tiles)):
                for r in range(ROWS):
                    rows_ref[
                        r,
                        32 * group : 32 * group + 32,
                        384 * quad + 128 * t : 384 * quad + 128 * t + 128,
                    ] = joined[32 * r : 32 * r + 32]


def output_kernel(
    early_ref, late_ref, x_ref, g_ref, fwd_ref, inv_ref,
    out_ref, grad_ref,
    rows_ref, back_rows_ref, mixed_ref, back_ref,
):
    r = pl.program_id(0)

    @pl.when(r == 0)
    def _():
        receive(((early_ref, 0), (early_ref, 24), (late_ref, 0)), rows_ref)
        receive(((late_ref, 24), (late_ref, 48), (late_ref, 72)), back_rows_ref)

    mixed_ref[...] = jnp.dot(inv_ref[...], rows_ref[r], preferred_element_type=F32)
    back_ref[...] = jnp.dot(fwd_ref[...], back_rows_ref[r], preferred_element_type=F32)
    for start, size in ROW_CHUNKS:
        span = slice(start, start + size)
        values = x_ref[0, r, span].astype(F32)
        normed, scale = normalize(values)
        out_ref[0, 0, span] = (values + normed + mixed_ref[span]).astype(BF)
        upstream = g_ref[0, r, span].astype(F32)
        back = upstream + back_ref[span]
        mean = jnp.sum(back, axis=-1, keepdims=True) * (1.0 / C)
        along = jnp.sum(back * normed, axis=-1, keepdims=True) * (1.0 / C)
        grad_ref[0, 0, span] = (upstream + scale * (back - mean - normed * along)).astype(BF)


def from_spectra(early, late, fields, cotangent, forward, inverse):
    token_spec = pl.BlockSpec((1, 1, W, C), lambda r: (0, r, 0, 0))
    near = pl.BlockSpec(memory_space=pltpu.VMEM)
    token = jax.ShapeDtypeStruct((1, ROWS, W, C), BF)
    return pl.pallas_call(
        output_kernel,
        name="from_spectra",
        grid=(ROWS,),
        in_specs=[near] * 6,
        out_specs=[token_spec, token_spec],
        out_shape=[token, token],
        scratch_shapes=[
            pltpu.VMEM((ROWS, 2 * KX, C), BF),
            pltpu.VMEM((ROWS, 2 * KX, C), BF),
            pltpu.VMEM((WPAD, C), F32),
            pltpu.VMEM((WPAD, C), F32),
        ],
        compiler_params=pltpu.CompilerParams(
            vmem_limit_bytes=VMEM_LIMIT,
        ),
        cost_estimate=pl.CostEstimate(
            flops=4 * ROWS * W * 2 * KX * C, bytes_accessed=5000000, transcendentals=0
        ),
    )(early, late, fields, cotangent, forward, inverse)


def whole(shape):
    return pl.BlockSpec(shape, lambda: (0,) * len(shape))


def spectral_call(kernel, name, operands, outs, scratch):
    return pl.pallas_call(
        kernel,
        name=name,
        in_specs=[whole(operand.shape) for operand in operands],
        out_specs=[whole(out.shape) for out in outs],
        out_shape=outs,
        scratch_shapes=scratch,
        compiler_params=pltpu.CompilerParams(vmem_limit_bytes=VMEM_LIMIT),
        cost_estimate=pl.CostEstimate(
            flops=1000000, bytes_accessed=1000000, transcendentals=0
        ),
    )(*operands)


def share_kernel(recv_ref, held_ref, out_ref):
    total = recv_ref[0].astype(F32)
    for i in range(1, recv_ref.shape[0]):
        total = total + recv_ref[i].astype(F32)
    share = total.astype(BF)
    for band in range(BANDS):
        out_ref[band] = share


def add_share(shares, held):
    return pl.pallas_call(
        share_kernel,
        name="grad_share",
        grid=(1,),
        in_specs=[
            pl.BlockSpec(shares.shape, lambda i: (0, 0, 0)),
            pl.BlockSpec(memory_space=pl.ANY),
        ],
        out_specs=pl.BlockSpec((BANDS, CHUNK_ROWS, 128), lambda i: (0, 2, 0)),
        out_shape=jax.ShapeDtypeStruct(held.shape, BF),
        input_output_aliases={1: 0},
        compiler_params=pltpu.CompilerParams(vmem_limit_bytes=VMEM_LIMIT),
    )(shares, held)


def group_sum_kernel(recv_ref, token_ref, out_ref):
    for block in range(NB):
        total = recv_ref[block * GROUPS].astype(F32)
        for group in range(1, GROUPS):
            total = total + recv_ref[block * GROUPS + group].astype(F32)
        out_ref[block] = total.astype(BF)


def group_sums(message, token):
    return pl.pallas_call(
        group_sum_kernel,
        name="grad_groups",
        grid=(1,),
        in_specs=[
            pl.BlockSpec((BANDS, CHUNK_ROWS, 128), lambda i: (0, 2, 0)),
            pl.BlockSpec(memory_space=pl.ANY),
        ],
        out_specs=pl.BlockSpec((NB, CHUNK_ROWS, 128), lambda i: (0, 0, 0)),
        out_shape=jax.ShapeDtypeStruct((NB, CHUNK_ROWS, 128), BF),
        compiler_params=pltpu.CompilerParams(vmem_limit_bytes=VMEM_LIMIT),
    )(message, token)


GRAD_SCALE = 1.0 / (SAMPLES * H)


def grads_kernel(recv_ref, w1_ref, b1_ref, w2_ref, b2_ref):
    for block in range(NB):
        chunk = 0
        for out_ref in (w1_ref, w2_ref):
            for part in range(2):
                pieces = [
                    recv_ref[chunk + i, block].astype(F32) * GRAD_SCALE for i in range(3)
                ]
                chunk += 3
                for i in range(3):
                    out_ref[part, block, 24 * i : 24 * i + 24, :] = pieces[i][:, :BS]
                out_ref[part, block, 72:96, :] = unpack_tail(pieces)[:, :BS]
    rows = [
        jnp.concatenate([recv_ref[12, block], recv_ref[13, block]], axis=0).astype(F32)
        * GRAD_SCALE
        for block in range(NB)
    ]
    for out_ref, first in ((b1_ref, 0), (b2_ref, 16)):
        for part in range(2):
            at = first + 8 * part
            for quad in range(2):
                parts = [rows[4 * quad + j][at : at + 8] for j in range(4)]
                for t, joined in enumerate(join_lanes(parts)):
                    lane = 384 * quad + 128 * t
                    out_ref[part : part + 1, lane : lane + 128] = joined[0:1]


def exchange(value):
    return lax.all_to_all(value, "lat", split_axis=0, concat_axis=0, tiled=True)


def on_device(fields, cotangent, w_first, b_first, w_second, b_second):
    block = (lax.axis_index("lat") // GROUPS).astype(jnp.int32).reshape(1)
    lon_fwd = jnp.asarray(LON_FWD, BF)
    lon_inv = jnp.asarray(LON_INV, BF)
    lon_fwd_t = jnp.asarray(LON_FWD.T, BF)
    lon_inv_t = jnp.asarray(LON_INV.T, BF)
    lat = jnp.asarray(LAT, BF)
    lat_t = jnp.asarray(LAT.T, BF)

    spectra = to_spectra(fields, cotangent, lon_fwd_t, lon_inv_t)
    spectra = exchange(spectra)
    kept, grads = block_call(
        gradient_kernel,
        "spectral_grads",
        block,
        (spectra, lat, w_first, b_first, w_second),
        ("near",) * 5,
        [jax.ShapeDtypeStruct((2,) + WIDE, BF), jax.ShapeDtypeStruct((CHUNKS, CHUNK_ROWS, 128), BF)],
        ("far", "near"),
        [FORM, FORM, BAND_ROWS, BAND_ROWS, pltpu.VMEM(WIDE, BF), pltpu.VMEM(WIDE, BF)]
        + [pltpu.VMEM((CHUNKS * CHUNK_ROWS, 128), F32), pltpu.VMEM((2,) + WIDE, BF)]
        + [pltpu.SemaphoreType.DMA((2,))],
    )
    kept = pltpu.with_memory_space_constraint(kept, pltpu.HBM)
    dp_size = lax.axis_size("dp")
    if dp_size == CHUNKS:
        shares = lax.all_to_all(grads, "dp", 0, 0, tiled=True)
    else:
        shares = grads
    early, late = block_call(
        return_kernel,
        "spectral_return",
        block,
        (kept, lat_t, w_first, w_second, b_second),
        ("far",) + ("near",) * 4,
        [
            jax.ShapeDtypeStruct((BANDS, PACK, 128), BF),
            jax.ShapeDtypeStruct((BANDS, 96, 128), BF),
        ],
        ("window", "far"),
        [FORM, FORM, BAND_ROWS, BAND_ROWS, COLUMNS, COLUMNS, pltpu.VMEM((2,) + WIDE, BF)]
        + [pltpu.VMEM((BANDS, 96, 128), BF)]
        + [pltpu.SemaphoreType.DMA((2,)), pltpu.SemaphoreType.DMA((4,))],
    )
    early = exchange(add_share(shares, early))
    token = shares[0, 0:8].astype(F32) + 1.0
    late, early, token = lax.optimization_barrier((late, early, token))
    late = exchange(late)
    blocks = group_sums(early, token)
    every = lax.all_gather(blocks, "dp", axis=0, tiled=False)
    if dp_size != CHUNKS:
        every = jnp.broadcast_to(every, (CHUNKS, NB, CHUNK_ROWS, 128))
    grad_w = jax.ShapeDtypeStruct((2, NB, BS, BS), F32)
    grad_b = jax.ShapeDtypeStruct((2, C), F32)
    g_w1, g_b1, g_w2, g_b2 = spectral_call(
        grads_kernel, "grad_out", (every,), [grad_w, grad_b, grad_w, grad_b], []
    )
    result, back_fields = from_spectra(early, late, fields, cotangent, lon_fwd, lon_inv)
    return (result, back_fields, g_w1, g_b1, g_w2, g_b2)


def solution(mesh):
    placed = (P("dp", "lat", None, None), P("dp", "lat", None, None), P(), P(), P(), P())
    return jax.shard_map(
        on_device,
        mesh=mesh,
        in_specs=placed,
        out_specs=(P("dp", "lat", None, None), P("dp", "lat", None, None), P(), P(), P(), P()),
        check_vma=False,
    )
```
